32 devices in a mesh: groups: 2 (over x), tile: 16 (over z, y, core).
Axes of the slice: x: 2, y: 2, z: 4, core: 2. Of those that a mesh axis runs over, the one named last changes fastest.
Arguments:
- probes: float32 [8, 262144], P(None, ('groups', 'tile')), parts along dimension 1, may hold values from -6 to 6
- level_set: float32 [262144], P(('groups', 'tile')), parts along dimension 0, may hold values from -6 to 6
- unit_label: int32 [262144], P(('groups', 'tile')), parts along dimension 0, may hold values from 0 to 3
- contrast: float32 [8], P('groups'), parts along dimension 0, may hold values from 0.2 to 1.5
- station_weight: float32 [65536], P('groups'), parts along dimension 0, may hold values from 0.2 to 2
- u_factor: bfloat16 [4096, 32, 512], P(('groups', 'tile')), parts along dimension 0, may hold values from -1 to 1
- v_factor: bfloat16 [4096, 32, 512], P(('groups', 'tile')), parts along dimension 0, may hold values from -0.25 to 0.25
- col_owner: int32 [4096, 1], P('groups'), parts along dimension 0, may hold values from 0 to 15; in each aligned block of 128 rows (0 to 127, 128 to 255, ...) at most 16 rows name the same one
- col_local: int32 [4096], P('groups'), parts along dimension 0, may hold values from 0 to 15
- row_owner: int32 [4096, 1], P('groups'), parts along dimension 0, may hold values from 0 to 15; in each aligned block of 128 rows (0 to 127, 128 to 255, ...) at most 16 rows name the same one
- row_local: int32 [4096], P('groups'), parts along dimension 0, may hold values from 0 to 3
- tile_rank: int32 [4096], P('groups'), parts along dimension 0, may hold values from 8 to 32
Outputs:
- hessian_probes: float32 [8, 262144], P(None, ('groups', 'tile')), parts along dimension 1
The draws below stay inside these ranges and needn't reach their ends.
There are 2 independent parts, one for each index of `groups`. The reference program is written for one: setup_inputs(seed, part) draws one part's arguments, and reference() takes and returns one part's arrays. A program takes and returns all parts, laid end to end along the dimension named above; each array names one. Nothing has to cross between parts.
Inputs may be any that keep to these rules, and one draw needn't show every extreme that they name: `col_owner`: among the 128 tiles of one device (aligned blocks of 128 entries) no owner is named more than 16 times, a bound that some block reaches. `row_owner`: among the 128 tiles of one device (aligned blocks of 128 entries) no owner is named more than 16 times, a bound that some block reaches.
All inputs are finite; a program needn't handle non-finite values.
Results may differ from the reference program's by a relative error of at most 0.005.
Values may be sent and summed in bfloat16 or wider, within the bound.
No kernel may reach another device: no remote copies, remote signals or barrier semaphores. Data moves between devices by JAX's collectives and lax.ppermute only.
A program may use at most 64 MiB of HBM per device.

```python
import math
import jax
import jax.numpy as jnp
import numpy as np
from jax import lax

PROBES = 8
RANK = 32
CELL_BLOCK = 512
STATION_BLOCK = 512
UNITS = 4
CB_DEV = 16
SB_DEV = 4
TILE_DEV = 128
CAP = 16
NCB = 256
NSB = 64
CELLS = 131072
STATIONS = 32768
TILES = 2048
N_TILE = 16


def place_ends(drawn, rng, smallest, top_value):
    longest = drawn.shape.index(max(drawn.shape))
    spots = []
    for shift in (0, 1):
        where = [jax.random.randint(jax.random.fold_in(rng, axis), (), 0, length) for axis, length in enumerate(drawn.shape)]
        where[longest] = (where[longest] + shift) % drawn.shape[longest]
        spots.append(tuple(where))
    return drawn.at[spots[0]].set(smallest).at[spots[1]].set(top_value)


def steps_of(rng, dims, split, least, high):
    gain, own = 1.0, jax.random.fold_in(rng, 6)
    for position, blocks in split:
        steps = jnp.exp(jax.random.uniform(jax.random.fold_in(own, position), (blocks,), jnp.float32, least / len(split), high / len(split)))
        gain = gain * jnp.repeat(steps, dims[position] // blocks).reshape([-1 if axis == position else 1 for axis in range(len(dims))])
    return gain


def routed_block(rng, own, number, rows, amount, top, most, skew):
    ranking = jax.random.permutation(rng, amount)
    heavy_load, ordinary = shares(amount, rows * top, most, skew, True), shares(amount, rows * top, most, skew, False)
    places = jnp.arange(amount)

    def named(tallies, offset_by):
        used = int((tallies > 0).sum())
        fixed = max(1, used // 4)
        passed = fixed + (places - fixed + offset_by * (used - fixed)) % max(1, amount - fixed)
        return jnp.zeros((amount,), jnp.int32).at[ranking[jnp.where(places < fixed, places, passed)]].set(jnp.asarray(tallies, jnp.int32))

    tallies = jnp.where(number % 4 == 0, named(heavy_load, number // 4), named(ordinary, number - number // 4 - 1))
    mixed = jax.random.permutation(jax.random.fold_in(own, 3), amount)
    source_of, sink = mixed[0:amount // 2 * 2:2], mixed[1:amount // 2 * 2:2]
    margin = jnp.minimum(tallies[source_of] - 1, most - tallies[sink]) // 2
    margin = jnp.where((source_of == ranking[0]) | (sink == ranking[0]) | (tallies[sink] == 0), 0, jnp.maximum(margin, 0))
    passed = jax.random.randint(jax.random.fold_in(own, 4), (amount // 2,), 0, 1 << 20) % (margin + 1)
    tallies = tallies.at[source_of].add(-passed).at[sink].add(passed)
    members = jnp.searchsorted(jnp.cumsum(tallies), jnp.arange(rows * top), side="right").astype(jnp.int32)
    table = members.reshape(top, rows).T
    table = table[jax.random.permutation(jax.random.fold_in(own, 1), rows)]
    offset_by = jax.random.randint(jax.random.fold_in(own, 2), (rows, 1), 0, top)
    return jnp.take_along_axis(table, (jnp.arange(top)[None, :] + offset_by) % top, axis=1)


def shares(number_of, total, reach, lean, full):
    weights = [(1 << 20) // math.isqrt(standing ** lean) + 1 for standing in range(1, number_of + 1)]
    largest = reach if full else min(reach, max(-(-total // number_of), total * weights[0] // sum(weights)))
    least = 1 if total - largest >= number_of - 1 else 0
    holding, surplus = [largest] + [least] * (number_of - 1), total - largest - least * (number_of - 1)
    while surplus > 0:
        movable = [i for i in range(1, number_of) if holding[i] < largest] or [i for i in range(1, number_of) if holding[i] < reach]
        pool, left = sum([weights[i] for i in movable]), surplus
        for i in movable:
            addition = min(reach - holding[i], max(1, left * weights[i] // pool), surplus)
            holding[i] = holding[i] + addition
            surplus = surplus - addition
    return np.array(holding)


def noise(stream_key, shape, width, reach, split=(), kind=jnp.bfloat16):
    values = width * jax.random.normal(stream_key, shape, jnp.float32)
    if split:
        values = values * steps_of(stream_key, shape, split, -0.22, 0.18)
    return jnp.clip(values, -reach, reach).astype(kind)


def setup_inputs(seed: int = 0, part: int = 0) -> dict:
    streams_of = jax.random.split(jax.random.key(seed), 13)
    part_splits = jax.random.split(jax.random.fold_in(streams_of[12], part), 13)
    probes = noise(part_splits[0], (PROBES, CELLS), 1.0, 6.0, ((1, 16),), jnp.float32)
    level_set = noise(part_splits[1], (CELLS,), 1.0, 6.0, ((0, 16),), jnp.float32)
    unit_label = place_ends(jax.random.randint(part_splits[2], (CELLS,), 0, UNITS), jax.random.fold_in(part_splits[2], 1), 0, UNITS - 1).astype(jnp.int32)
    contrast = jnp.clip(jnp.exp(jax.random.uniform(part_splits[3], (UNITS,), jnp.float32, math.log(0.2), math.log(1.5))), 0.2, 1.5)
    station_weight = jnp.clip(jnp.exp(jax.random.uniform(part_splits[4], (STATIONS,), jnp.float32, math.log(0.2), math.log(2.0))), 0.2, 2.0)
    u_factor = noise(part_splits[5], (TILES, RANK, STATION_BLOCK), RANK ** -0.5, 1.0, ((0, 16),))
    v_factor = noise(part_splits[6], (TILES, RANK, CELL_BLOCK), CELL_BLOCK ** -0.5, 0.25, ((0, 16),))
    col_owner_keys = jax.random.split(jax.random.fold_in(part_splits[7], 1), TILES // TILE_DEV)
    col_owner_turns = jax.random.permutation(jax.random.fold_in(part_splits[7], 3), TILES // TILE_DEV)
    col_owner = jax.vmap(lambda own, number: routed_block(jax.random.fold_in(part_splits[7], 2), own, number, TILE_DEV, N_TILE, 1, CAP, 2))(col_owner_keys, col_owner_turns).reshape((TILES, 1))
    col_local = place_ends(jax.random.randint(part_splits[8], (TILES,), 0, CB_DEV), jax.random.fold_in(part_splits[8], 1), 0, CB_DEV - 1).astype(jnp.int32)
    row_owner_keys = jax.random.split(jax.random.fold_in(part_splits[9], 1), TILES // TILE_DEV)
    row_owner_turns = jax.random.permutation(jax.random.fold_in(part_splits[9], 3), TILES // TILE_DEV)
    row_owner = jax.vmap(lambda own, number: routed_block(jax.random.fold_in(part_splits[9], 2), own, number, TILE_DEV, N_TILE, 1, CAP, 2))(row_owner_keys, row_owner_turns).reshape((TILES, 1))
    row_local = place_ends(jax.random.randint(part_splits[10], (TILES,), 0, SB_DEV), jax.random.fold_in(part_splits[10], 1), 0, SB_DEV - 1).astype(jnp.int32)
    tile_rank = place_ends(jax.random.randint(part_splits[11], (TILES,), RANK // 4, RANK + 1), jax.random.fold_in(part_splits[11], 1), RANK // 4, RANK).astype(jnp.int32)
    return {"probes": probes, "level_set": level_set, "unit_label": unit_label, "contrast": contrast, "station_weight": station_weight, "u_factor": u_factor, "v_factor": v_factor, "col_owner": col_owner, "col_local": col_local, "row_owner": row_owner, "row_local": row_local, "tile_rank": tile_rank}


def forward_tiles(operands):
    cells, v_part, u_part, keep_part = operands
    coeff = jnp.einsum('tkc,trc->tkr', cells.astype(jnp.float32), v_part.astype(jnp.float32))
    coeff = (coeff * keep_part).astype(jnp.bfloat16)
    return jnp.einsum('tkr,trs->tks', coeff.astype(jnp.float32), u_part.astype(jnp.float32))


def adjoint_tiles(operands):
    data, v_part, u_part, keep_part = operands
    back = jnp.einsum('tks,trs->tkr', data.astype(jnp.float32), u_part.astype(jnp.float32))
    back = (back * keep_part).astype(jnp.bfloat16)
    return jnp.einsum('tkr,trc->tkc', back.astype(jnp.float32), v_part.astype(jnp.float32))


def grouped(array):
    return array.reshape((N_TILE, TILE_DEV) + array.shape[1:])


def reference(probes, level_set, unit_label, contrast, station_weight, u_factor, v_factor, col_owner, col_local, row_owner, row_local, tile_rank):
    scaling = contrast[unit_label] / (1.0 + level_set * level_set)
    scaled = (probes * scaling[None, :]).astype(jnp.bfloat16)
    cell_rows = scaled.reshape(PROBES, NCB, CELL_BLOCK).transpose(1, 0, 2)
    col_global = (col_owner[:, 0] * CB_DEV + col_local).astype(jnp.int32)
    row_global = (row_owner[:, 0] * SB_DEV + row_local).astype(jnp.int32)
    keep = (jnp.arange(RANK, dtype=jnp.int32)[None, :] < tile_rank[:, None]).astype(jnp.float32)[:, None, :]
    tile_cells = cell_rows[col_global]
    partial_value = lax.map(forward_tiles, (grouped(tile_cells), grouped(v_factor), grouped(u_factor), grouped(keep)))
    predicted = jax.ops.segment_sum(partial_value.reshape(TILES, PROBES, STATION_BLOCK), row_global, num_segments=NSB)
    weighted = (predicted * station_weight.reshape(NSB, 1, STATION_BLOCK)).astype(jnp.bfloat16)
    tile_data = weighted[row_global]
    spread = lax.map(adjoint_tiles, (grouped(tile_data), grouped(v_factor), grouped(u_factor), grouped(keep)))
    summed = jax.ops.segment_sum(spread.reshape(TILES, PROBES, CELL_BLOCK), col_global, num_segments=NCB)
    gradient = summed.transpose(1, 0, 2).reshape(PROBES, CELLS)
    return scaling[None, :] * gradient
```

```python
import jax
import jax.numpy as jnp
from jax import lax
from jax.experimental import pallas as pl
from jax.experimental.pallas import tpu as pltpu
from jax.sharding import PartitionSpec as P

BF16 = jnp.bfloat16
F32 = jnp.float32
GROUP = 8
VMEM_LIMIT = 56 * 1024 * 1024


def whole(space=pltpu.VMEM):
    return pl.BlockSpec(memory_space=space)


def swap(array, bit):
    count = lax.axis_size("tile")
    return lax.ppermute(array, "tile", [(i, i ^ bit) for i in range(count)])


def local(body, outs, *ins, name, scratch=(), specs=None, flops=0):
    nbytes = sum(a.size * a.dtype.itemsize for a in ins) + sum(a.size * a.dtype.itemsize for a in outs)
    return pl.pallas_call(
        body,
        out_shape=list(outs),
        in_specs=specs or [whole()] * len(ins),
        out_specs=[whole()] * len(outs),
        scratch_shapes=list(scratch),
        compiler_params=pltpu.CompilerParams(vmem_limit_bytes=VMEM_LIMIT),
        cost_estimate=pl.CostEstimate(flops=flops, bytes_accessed=nbytes, transcendentals=0),
        name=name,
    )(*ins)


def shape(dims, dtype):
    return jax.ShapeDtypeStruct(tuple(dims), dtype)


def scale_body(contrast, level, label, probes, first, second, scaling):
    value = level[...]
    unit = label[...]
    factor = jnp.zeros_like(value)
    for k in range(contrast.shape[0]):
        factor = jnp.where(unit == k, contrast[k], factor)
    scaling[...] = factor / (1.0 + value * value)
    blocks, _, width = first.shape
    rows = width // 128
    for half, out in enumerate((first, second)):
        for b in range(blocks):
            for c in range(rows):
                j = (half * blocks + b) * rows + c
                piece = probes[:, j * 128 : (j + 1) * 128] * scaling[j : j + 1, :]
                out[b, :, c * 128 : (c + 1) * 128] = piece.astype(BF16)


def final_body(keep_p, recv_p, keep_q, recv_q, scaling, out):
    blocks, _, width = keep_p.shape
    rows = width // 128
    for half, (keep, recv) in enumerate(((keep_p, recv_p), (keep_q, recv_q))):
        for b in range(blocks):
            for c in range(rows):
                j = (half * blocks + b) * rows + c
                lanes = slice(c * 128, (c + 1) * 128)
                total = keep[b, :, lanes] + recv[b, :, lanes].astype(F32)
                out[:, j * 128 : (j + 1) * 128] = total * scaling[j : j + 1, :]


def join_body(*refs):
    count = len(refs) // 3
    for i in range(count):
        a, b, out = refs[2 * i], refs[2 * i + 1], refs[2 * count + i]
        out[: a.shape[0]] = a[...]
        out[a.shape[0] :] = b[...]


def join(*pairs):
    outs = [shape((2 * a.shape[0],) + a.shape[1:], a.dtype) for a, _ in pairs]
    return local(join_body, outs, *[x for pair in pairs for x in pair], name="join")


def fold_body(*refs):
    count = len(refs) // 4
    for i in range(count):
        keep, recv = refs[2 * i], refs[2 * i + 1]
        mine, send = refs[2 * count + 2 * i], refs[2 * count + 2 * i + 1]
        half = mine.shape[0]
        mine[...] = keep[:half] + recv[:half].astype(F32)
        send[...] = (keep[half:] + recv[half:].astype(F32)).astype(BF16)


def fold(*pairs):
    outs = []
    for keep, _ in pairs:
        dims = (keep.shape[0] // 2,) + keep.shape[1:]
        outs += [shape(dims, F32), shape(dims, BF16)]
    flat = local(fold_body, outs, *[x for pair in pairs for x in pair], name="fold")
    return [(flat[2 * i], flat[2 * i + 1]) for i in range(len(pairs))]


def tiles_body(piece_count, src_at, dst_at, keep, *refs):
    pieces = refs[:piece_count]
    first_hbm, second_hbm, mine, send, table, first, second, acc, sems = refs[piece_count:]
    groups = keep.shape[0]
    rank = first.shape[1]
    width = table.shape[2]
    copies = []
    for g in range(groups):
        rows = pl.ds(g * GROUP, GROUP)
        pair = (
            pltpu.make_async_copy(first_hbm.at[rows], first.at[rows], sems.at[0, g]),
            pltpu.make_async_copy(second_hbm.at[rows], second.at[rows], sems.at[1, g]),
        )
        for copy in pair:
            copy.start()
        copies.append(pair)
    acc[...] = jnp.zeros_like(acc)
    per = pieces[0].shape[0]
    for i, piece in enumerate(pieces):
        table[i * per : (i + 1) * per] = piece[...]
    probes = table.shape[1]
    span = GROUP * rank
    row_tile = lax.broadcasted_iota(jnp.int32, (GROUP * probes, span), 0) // probes
    col_tile = lax.broadcasted_iota(jnp.int32, (GROUP * probes, span), 1) // rank
    own = row_tile == col_tile
    for g in range(groups):
        for copy in copies[g]:
            copy.wait()
        taken = jnp.concatenate(
            [table[src_at[g * GROUP + i]].astype(F32) for i in range(GROUP)], axis=0
        ).astype(BF16)
        left = first[g * GROUP : (g + 1) * GROUP].reshape(span, width)
        right = second[g * GROUP : (g + 1) * GROUP].reshape(span, width)
        inner = lax.dot_general(taken, left, (((1,), (1,)), ((), ())), preferred_element_type=F32)
        kept = jnp.where(own & (keep[g : g + 1, :] > 0), inner, 0.0).astype(BF16)
        outer = jnp.dot(kept, right, preferred_element_type=F32)
        for i in range(GROUP):
            at = dst_at[g * GROUP + i]
            acc[at] = acc[at] + outer[i * probes : (i + 1) * probes]
    half = mine.shape[0]
    mine[...] = acc[:half].astype(mine.dtype)
    send[...] = acc[half:].astype(send.dtype)


def tiles(pieces, src_at, dst_at, keep, first, second, blocks, send_dtype, name):
    count, rank, width = first.shape
    probes = pieces[0].shape[1]
    groups = keep.shape[0]
    rows = len(pieces) * pieces[0].shape[0]
    half = (blocks // 2, probes, width)

    def body(*refs):
        tiles_body(len(pieces), *refs)

    smem = whole(pltpu.SMEM)
    specs = [smem, smem, whole()] + [whole()] * len(pieces) + [whole(pl.ANY)] * 2
    return local(
        body,
        [shape(half, F32), shape(half, send_dtype)],
        src_at,
        dst_at,
        keep,
        *pieces,
        first,
        second,
        name=name,
        specs=specs,
        flops=4 * count * rank * width * probes * GROUP,
        scratch=[
            pltpu.VMEM((rows, probes, width), BF16),
            pltpu.VMEM((count, rank, width), BF16),
            pltpu.VMEM((count, rank, width), BF16),
            pltpu.VMEM((blocks, probes, width), F32),
            pltpu.SemaphoreType.DMA((2, groups)),
        ],
    )


def place(relative, order):
    at = jnp.zeros_like(relative)
    for k, bit in enumerate(order):
        at = at + jnp.where((relative & bit) != 0, 1 << k, 0)
    return at


def shards(
    probes,
    level_set,
    unit_label,
    contrast,
    station_weight,
    u_factor,
    v_factor,
    col_owner,
    col_local,
    row_owner,
    row_local,
    tile_rank,
):
    peers = lax.axis_size("tile")
    me = lax.axis_index("tile")
    tile_count, rank_max, station_width = u_factor.shape
    cell_width = v_factor.shape[2]
    probe_count, cell_total = probes.shape
    cell_blocks = cell_total // cell_width
    station_blocks = station_weight.shape[0] // (peers * station_width)
    half_blocks = cell_blocks // 2
    far = [1 << k for k in range(2, peers.bit_length() - 1)][::-1]
    order_p = [2] + far
    order_q = far + [2]
    split_bits = [1 << k for k in range(peers.bit_length() - 3)]
    join_bits = [peers // 4, peers // 2]

    start = me * tile_count

    def mine_of(table):
        return lax.dynamic_slice_in_dim(table.reshape(-1), start, tile_count)

    col_relative = mine_of(col_owner) ^ me
    col_here = mine_of(col_local)
    row_holder = mine_of(row_owner)
    row_here = mine_of(row_local)
    rank_mine = mine_of(tile_rank)
    is_q = col_here >= half_blocks
    span = peers // 2
    cell_at = (
        (col_relative & 1) * (span * cell_blocks)
        + jnp.where(is_q, place(col_relative, order_q), place(col_relative, order_p)) * half_blocks
        + jnp.where(is_q, span * half_blocks - half_blocks, 0)
        + col_here
    )
    row_at = place(row_holder ^ me, split_bits[::-1]) * (4 * station_blocks)
    row_at = row_at + (row_holder // (peers // 4)) * station_blocks + row_here
    keep = (jnp.arange(rank_max, dtype=jnp.int32)[None, :] < rank_mine[:, None]).astype(F32)
    keep = keep.reshape(tile_count // GROUP, GROUP * rank_max)
    weight = lax.dynamic_slice_in_dim(
        station_weight.reshape(4, peers // 4, station_blocks, station_width), me % (peers // 4), 1, 1
    ).reshape(4 * station_blocks, 1, station_width)

    half_dims = (half_blocks, probe_count, cell_width)
    lanes = (cell_total // 128, 128)
    part_p, part_q, scaling = local(
        scale_body,
        [shape(half_dims, BF16), shape(half_dims, BF16), shape(lanes, F32)],
        contrast,
        level_set.reshape(lanes),
        unit_label.reshape(lanes),
        probes,
        name="scale",
        specs=[whole(pltpu.SMEM)] + [whole()] * 3,
    )
    for step in range(len(order_p)):
        got_p = swap(part_p, order_p[step])
        got_q = swap(part_q, order_q[step])
        if step < len(order_p) - 1:
            part_p, part_q = join((part_p, got_p), (part_q, got_q))
    pieces = [part_p, got_p, part_q, got_q]
    pieces = pieces + [swap(piece, 1) for piece in pieces]

    total, send = tiles(
        pieces, cell_at, row_at, keep, v_factor, u_factor, peers * station_blocks, F32, "forward"
    )
    total = total + swap(send, split_bits[0])
    for bit in split_bits[1:]:
        half = total.shape[0] // 2
        got = swap(total[half:].astype(BF16), bit)
        total = total[:half] + got.astype(F32)
    for bit in join_bits:
        total = total + swap(total.astype(BF16), bit).astype(F32)
    weighted = (total * weight).astype(BF16)
    pieces = [weighted]
    for bit in split_bits[::-1]:
        pieces = pieces + [swap(piece, bit) for piece in pieces]

    keep_all, send_all = tiles(
        pieces, row_at, cell_at, keep, u_factor, v_factor, peers * cell_blocks, BF16, "adjoint"
    )
    got_all = swap(send_all, 1)
    half = keep_all.shape[0] // 2
    pair_p = (keep_all[:half], got_all[:half])
    pair_q = (keep_all[half:], got_all[half:])
    for bit_p, bit_q in zip(order_p[::-1], order_q[::-1]):
        (keep_p, send_p), (keep_q, send_q) = fold(pair_p, pair_q)
        pair_p = (keep_p, swap(send_p, bit_p))
        pair_q = (keep_q, swap(send_q, bit_q))
    return local(
        final_body,
        [shape((probe_count, cell_total), F32)],
        *pair_p,
        *pair_q,
        scaling,
        name="final",
    )[0]


def solution(mesh):
    placed = (
        P(None, ("groups", "tile")),
        P(("groups", "tile")),
        P(("groups", "tile")),
        P("groups"),
        P("groups"),
        P(("groups", "tile"), None, None),
        P(("groups", "tile"), None, None),
        P("groups", None),
        P("groups"),
        P("groups", None),
        P("groups"),
        P("groups"),
    )
    return jax.shard_map(
        shards, mesh=mesh, in_specs=placed, out_specs=P(None, ("groups", "tile")), check_vma=False
    )
```

```python
import math

import jax
import jax.numpy as jnp
from jax import lax
from jax.experimental import pallas as pl
from jax.experimental.pallas import tpu as pltpu
from jax.sharding import PartitionSpec as P

BF16 = jnp.bfloat16
F32 = jnp.float32
GROUP = 8
MIB = 1024 * 1024


def whole(space=pltpu.VMEM):
    return pl.BlockSpec(memory_space=space)


def swap(array, bit):
    count = lax.axis_size("tile")
    return lax.ppermute(array, "tile", [(i, i ^ bit) for i in range(count)])


def size_of(array):
    return math.prod(array.shape) * jnp.dtype(array.dtype).itemsize


def near(array):
    return pltpu.with_memory_space_constraint(array, pltpu.VMEM)


def local(body, outs, *ins, name, scratch=0, scratches=(), specs=None, flops=0, far_out=False):
    nbytes = sum(size_of(a) for a in (*ins, *outs))
    specs = specs or [whole()] * len(ins)
    ins = [near(a) if s.memory_space == pltpu.VMEM else a for a, s in zip(ins, specs)]
    return pl.pallas_call(
        body,
        out_shape=[a if far_out else pltpu.VMEM(a.shape, a.dtype) for a in outs],
        in_specs=specs,
        out_specs=[whole()] * len(outs),
        scratch_shapes=list(scratches),
        compiler_params=pltpu.CompilerParams(vmem_limit_bytes=scratch + 8 * MIB),
        cost_estimate=pl.CostEstimate(flops=flops, bytes_accessed=nbytes, transcendentals=0),
        name=name,
    )(*ins)


def shape(dims, dtype):
    return jax.ShapeDtypeStruct(tuple(dims), dtype)


def scale_body(contrast, level, label, probes, first, second, scaling):
    value = level[...]
    unit = label[...]
    factor = jnp.zeros_like(value)
    for k in range(contrast.shape[0]):
        factor = jnp.where(unit == k, contrast[k], factor)
    scaling[...] = factor / (1.0 + value * value)
    blocks, _, width = first.shape
    rows = width // 128
    for half, out in enumerate((first, second)):
        for b in range(blocks):
            for c in range(rows):
                j = (half * blocks + b) * rows + c
                piece = probes[:, j * 128 : (j + 1) * 128] * scaling[j : j + 1, :]
                out[b, :, c * 128 : (c + 1) * 128] = piece.astype(BF16)


def final_body(keep_p, recv_p, keep_q, recv_q, scaling, out):
    blocks, _, width = keep_p.shape
    rows = width // 128
    for half, (keep, recv) in enumerate(((keep_p, recv_p), (keep_q, recv_q))):
        for b in range(blocks):
            for c in range(rows):
                j = (half * blocks + b) * rows + c
                lanes = slice(c * 128, (c + 1) * 128)
                total = keep[b, :, lanes] + recv[b, :, lanes].astype(F32)
                out[:, j * 128 : (j + 1) * 128] = total * scaling[j : j + 1, :]


def join_body(*refs):
    count = len(refs) // 3
    for i in range(count):
        a, b, out = refs[2 * i], refs[2 * i + 1], refs[2 * count + i]
        out[: a.shape[0]] = a[...]
        out[a.shape[0] :] = b[...]


def join(*pairs):
    outs = [shape((2 * a.shape[0],) + a.shape[1:], a.dtype) for a, _ in pairs]
    return local(join_body, outs, *[x for pair in pairs for x in pair], name="join")


def fold(*pairs):
    per = 4 // len(pairs)
    outs = []
    for keep, _ in pairs:
        dims = (keep.shape[0] // per,) + keep.shape[1:]
        outs += [shape(dims, F32), shape(dims, BF16)] * (per // 2)

    def body(*refs):
        done = refs[2 * len(pairs) :]
        for i in range(4):
            keep, recv = refs[2 * (i // per)], refs[2 * (i // per) + 1]
            n = done[i].shape[0]
            at = slice((i % per) * n, (i % per + 1) * n)
            done[i][...] = (keep[at] + recv[at].astype(F32)).astype(done[i].dtype)

    return local(body, outs, *[x for pair in pairs for x in pair], name="fold")


def tiles_body(piece_count, src_at, dst_at, keep, *refs):
    pieces = refs[:piece_count]
    first, second, mine, send, table, acc = refs[piece_count:]
    groups = keep.shape[0]
    rank = first.shape[1]
    width = table.shape[2]
    acc[...] = jnp.zeros_like(acc)
    per = pieces[0].shape[0]
    for i, piece in enumerate(pieces):
        table[i * per : (i + 1) * per] = piece[...]
    probes = table.shape[1]
    span = GROUP * rank
    row_tile = lax.broadcasted_iota(jnp.int32, (GROUP * probes, span), 0) // probes
    col_tile = lax.broadcasted_iota(jnp.int32, (GROUP * probes, span), 1) // rank
    own = row_tile == col_tile
    for g in range(groups):
        taken = jnp.concatenate(
            [table[src_at[g * GROUP + i]].astype(F32) for i in range(GROUP)], axis=0
        ).astype(BF16)
        left = first[g * GROUP : (g + 1) * GROUP].reshape(span, width)
        right = second[g * GROUP : (g + 1) * GROUP].reshape(span, width)
        inner = lax.dot_general(taken, left, (((1,), (1,)), ((), ())), preferred_element_type=F32)
        kept = jnp.where(own & (keep[g : g + 1, :] > 0), inner, 0.0).astype(BF16)
        outer = jnp.dot(kept, right, preferred_element_type=F32)
        for i in range(GROUP):
            at = dst_at[g * GROUP + i]
            acc[at] = acc[at] + outer[i * probes : (i + 1) * probes]
    half = mine.shape[0]
    mine[...] = acc[:half].astype(mine.dtype)
    send[...] = acc[half:].astype(send.dtype)


def tiles(pieces, src_at, dst_at, keep, first, second, blocks, send_dtype, name):
    count, rank, width = first.shape
    probes = pieces[0].shape[1]
    rows = len(pieces) * pieces[0].shape[0]
    half = (blocks // 2, probes, width)

    def body(*refs):
        tiles_body(len(pieces), *refs)

    smem = whole(pltpu.SMEM)
    specs = [smem, smem] + [whole()] * (len(pieces) + 3)
    return local(
        body,
        [shape(half, F32), shape(half, send_dtype)],
        src_at,
        dst_at,
        keep,
        *pieces,
        first,
        second,
        name=name,
        specs=specs,
        flops=4 * count * rank * width * probes * GROUP,
        scratch=(2 * rows + 4 * blocks) * probes * width,
        scratches=[
            pltpu.VMEM((rows, probes, width), BF16),
            pltpu.VMEM((blocks, probes, width), F32),
        ],
    )


def place(relative, order):
    at = jnp.zeros_like(relative)
    for k, bit in enumerate(order):
        at = at + jnp.where((relative & bit) != 0, 1 << k, 0)
    return at


def shards(
    probes,
    level_set,
    unit_label,
    contrast,
    station_weight,
    u_factor,
    v_factor,
    col_owner,
    col_local,
    row_owner,
    row_local,
    tile_rank,
):
    peers = lax.axis_size("tile")
    me = lax.axis_index("tile")
    tile_count, rank_max, station_width = u_factor.shape
    cell_width = v_factor.shape[2]
    probe_count, cell_total = probes.shape
    cell_blocks = cell_total // cell_width
    station_blocks = station_weight.shape[0] // (peers * station_width)
    half_blocks = cell_blocks // 2
    far = [1 << k for k in range(2, peers.bit_length() - 1)][::-1]
    order_p = [2] + far
    order_q = far + [2]
    split_bits = [1 << k for k in range(peers.bit_length() - 3)]
    join_bits = [peers // 4, peers // 2]

    start = me * tile_count

    def mine_of(table):
        return lax.dynamic_slice_in_dim(table.reshape(-1), start, tile_count)

    col_relative = mine_of(col_owner) ^ me
    col_here = mine_of(col_local)
    row_holder = mine_of(row_owner)
    row_here = mine_of(row_local)
    rank_mine = mine_of(tile_rank)
    is_q = col_here >= half_blocks
    span = peers // 2
    cell_at = (
        (col_relative & 1) * (span * cell_blocks)
        + jnp.where(is_q, place(col_relative, order_q), place(col_relative, order_p)) * half_blocks
        + jnp.where(is_q, span * half_blocks - half_blocks, 0)
        + col_here
    )
    row_at = place(row_holder ^ me, split_bits[::-1]) * (4 * station_blocks)
    row_at = row_at + (row_holder // (peers // 4)) * station_blocks + row_here
    keep = (jnp.arange(rank_max, dtype=jnp.int32)[None, :] < rank_mine[:, None]).astype(F32)
    keep = keep.reshape(tile_count // GROUP, GROUP * rank_max)
    weight = lax.dynamic_slice_in_dim(
        station_weight.reshape(4, peers // 4, station_blocks, station_width), me % (peers // 4), 1, 1
    ).reshape(4 * station_blocks, 1, station_width)

    half_dims = (half_blocks, probe_count, cell_width)
    lanes = (cell_total // 128, 128)
    part_p, part_q, scaling = local(
        scale_body,
        [shape(half_dims, BF16), shape(half_dims, BF16), shape(lanes, F32)],
        contrast,
        level_set.reshape(lanes),
        unit_label.reshape(lanes),
        probes,
        name="scale",
        specs=[whole(pltpu.SMEM)] + [whole()] * 3,
    )
    for step in range(len(order_p)):
        got_p = swap(part_p, order_p[step])
        got_q = swap(part_q, order_q[step])
        if step < len(order_p) - 1:
            part_p, part_q = join((part_p, got_p), (part_q, got_q))
    pieces = [part_p, got_p, part_q, got_q]
    pieces = pieces + [swap(piece, 1) for piece in pieces]

    total, send = tiles(
        pieces, cell_at, row_at, keep, v_factor, u_factor, peers * station_blocks, F32, "forward"
    )
    total = total + swap(send, split_bits[0])
    for bit in split_bits[1:]:
        half = total.shape[0] // 2
        got = swap(total[half:].astype(BF16), bit)
        total = total[:half] + got.astype(F32)
    for bit in join_bits:
        total = total + swap(total.astype(BF16), bit).astype(F32)
    weighted = (total * weight).astype(BF16)
    pieces = [weighted]
    for bit in split_bits[::-1]:
        pieces = pieces + [swap(piece, bit) for piece in pieces]

    keep_all, send_all = tiles(
        pieces, row_at, cell_at, keep, u_factor, v_factor, peers * cell_blocks, BF16, "adjoint"
    )
    got_all = swap(send_all, 1)
    pairs = [(keep_all, got_all)]
    for bit_p, bit_q in zip(order_p[::-1], order_q[::-1]):
        keep_p, send_p, keep_q, send_q = fold(*pairs)
        pairs = [(keep_p, swap(send_p, bit_p)), (keep_q, swap(send_q, bit_q))]
    return local(
        final_body,
        [shape((probe_count, cell_total), F32)],
        *pairs[0],
        *pairs[1],
        scaling,
        name="final",
        far_out=True,
    )[0]


def solution(mesh):
    placed = (
        P(None, ("groups", "tile")),
        P(("groups", "tile")),
        P(("groups", "tile")),
        P("groups"),
        P("groups"),
        P(("groups", "tile"), None, None),
        P(("groups", "tile"), None, None),
        P("groups", None),
        P("groups"),
        P("groups", None),
        P("groups"),
        P("groups"),
    )
    return jax.shard_map(
        shards, mesh=mesh, in_specs=placed, out_specs=P(None, ("groups", "tile")), check_vma=False
    )
```

```python
import math

import jax
import jax.numpy as jnp
from jax import lax
from jax.experimental import pallas as pl
from jax.experimental.pallas import tpu as pltpu
from jax.sharding import PartitionSpec as P

BF16 = jnp.bfloat16
F32 = jnp.float32
GROUP = 8
MIB = 1024 * 1024


def whole(space=pltpu.VMEM):
    return pl.BlockSpec(memory_space=space)


def swap(array, bit):
    count = lax.axis_size("tile")
    return lax.ppermute(array, "tile", [(i, i ^ bit) for i in range(count)])


def size_of(array):
    return math.prod(array.shape) * jnp.dtype(array.dtype).itemsize


def near(array, space):
    return pltpu.with_memory_space_constraint(array, space)


def local(body, outs, *ins, name, scratch=0, scratches=(), specs=None, flops=0, far_out=False, after=()):
    nbytes = sum(size_of(a) for a in (*ins, *outs))
    specs = list(specs or [whole()] * len(ins)) + [whole()] * len(after)
    own = len(ins)
    ins = [a if s.memory_space == pltpu.SMEM else near(a, s.memory_space) for a, s in zip((*ins, *after), specs)]

    def run(*refs):
        body(*refs[:own], *refs[len(ins) :])

    return pl.pallas_call(
        run,
        out_shape=[a if far_out else pltpu.VMEM(a.shape, a.dtype) for a in outs],
        in_specs=specs,
        out_specs=[whole()] * len(outs),
        scratch_shapes=list(scratches),
        compiler_params=pltpu.CompilerParams(vmem_limit_bytes=scratch + 8 * MIB),
        cost_estimate=pl.CostEstimate(flops=flops, bytes_accessed=nbytes, transcendentals=0),
        name=name,
    )(*ins)


def shape(dims, dtype):
    return jax.ShapeDtypeStruct(tuple(dims), dtype)


def load_body(source, out, sems):
    copies = []
    for i in range(sems.shape[0]):
        n = source.shape[0] // sems.shape[0]
        rows = pl.ds(i * n, n)
        copies.append(pltpu.make_async_copy(source.at[rows], out.at[rows], sems.at[i]))
    for copy in copies:
        copy.start()
    for copy in copies:
        copy.wait()


def load(array, after, name):
    return local(
        load_body,
        [shape(array.shape, array.dtype)],
        array,
        name=name,
        specs=[whole(pltpu.HBM)],
        scratches=[pltpu.SemaphoreType.DMA((8,))],
        after=after,
    )[0]


def scale_body(contrast, *refs):
    far, (first, second, scaling), near_refs, sems = refs[:3], refs[3:6], refs[6:9], refs[9]
    copies = [pltpu.make_async_copy(a, b, sems.at[i]) for i, (a, b) in enumerate(zip(far, near_refs))]
    for copy in copies:
        copy.start()
    for copy in copies:
        copy.wait()
    level, label, probes = near_refs
    value = level[...]
    unit = label[...]
    factor = jnp.zeros_like(value)
    for k in range(contrast.shape[0]):
        factor = jnp.where(unit == k, contrast[k], factor)
    scaling[...] = factor / (1.0 + value * value)
    blocks, _, width = first.shape
    rows = width // 128
    for half, out in enumerate((first, second)):
        for b in range(blocks):
            for c in range(rows):
                j = (half * blocks + b) * rows + c
                piece = probes[:, j * 128 : (j + 1) * 128] * scaling[j : j + 1, :]
                out[b, :, c * 128 : (c + 1) * 128] = piece.astype(BF16)


def final_body(keep_p, recv_p, keep_q, recv_q, scaling, out):
    blocks, _, width = keep_p.shape
    rows = width // 128
    for half, (keep, recv) in enumerate(((keep_p, recv_p), (keep_q, recv_q))):
        for b in range(blocks):
            for c in range(rows):
                j = (half * blocks + b) * rows + c
                lanes = slice(c * 128, (c + 1) * 128)
                total = keep[b, :, lanes] + recv[b, :, lanes].astype(F32)
                out[:, j * 128 : (j + 1) * 128] = total * scaling[j : j + 1, :]


def join_body(*refs):
    count = len(refs) // 3
    for i in range(count):
        a, b, out = refs[2 * i], refs[2 * i + 1], refs[2 * count + i]
        out[: a.shape[0]] = a[...]
        out[a.shape[0] :] = b[...]


def join(*pairs, after=()):
    outs = [shape((2 * a.shape[0],) + a.shape[1:], a.dtype) for a, _ in pairs]
    return local(join_body, outs, *[x for pair in pairs for x in pair], name="join", after=after)


def plus(total, got, weight=None):
    outs = [shape(total.shape, BF16)] if weight is not None else [shape(total.shape, F32), shape(total.shape, BF16)]
    ins = (total, got) if weight is None else (total, got, weight)

    def body(*refs):
        done = refs[0][...] + refs[1][...].astype(F32)
        if weight is not None:
            done = done * refs[2][...]
        for out in refs[len(ins) :]:
            out[...] = done.astype(out.dtype)

    return local(body, outs, *ins, name="plus")


def fold(*pairs, parts=4):
    per = parts // len(pairs)
    outs = []
    for keep, _ in pairs:
        dims = (keep.shape[0] // per,) + keep.shape[1:]
        outs += [shape(dims, F32), shape(dims, BF16)] * (per // 2)

    def body(*refs):
        done = refs[2 * len(pairs) :]
        for i in range(parts):
            keep, recv = refs[2 * (i // per)], refs[2 * (i // per) + 1]
            n = done[i].shape[0]
            at = slice((i % per) * n, (i % per + 1) * n)
            done[i][...] = (keep[at] + recv[at].astype(F32)).astype(done[i].dtype)

    return local(body, outs, *[x for pair in pairs for x in pair], name="fold")


def tiles_body(piece_count, src_at, dst_at, keep, *refs):
    pieces = refs[:piece_count]
    first, second, mine, send, table, acc = refs[piece_count:]
    groups = keep.shape[0]
    rank = first.shape[1]
    width = table.shape[2]
    acc[...] = jnp.zeros_like(acc)
    per = pieces[0].shape[0]
    for i, piece in enumerate(pieces):
        table[i * per : (i + 1) * per] = piece[...]
    probes = table.shape[1]
    span = GROUP * rank
    row_tile = lax.broadcasted_iota(jnp.int32, (GROUP * probes, span), 0) // probes
    col_tile = lax.broadcasted_iota(jnp.int32, (GROUP * probes, span), 1) // rank
    own = row_tile == col_tile
    for g in range(groups):
        taken = jnp.concatenate(
            [table[src_at[g * GROUP + i]].astype(F32) for i in range(GROUP)], axis=0
        ).astype(BF16)
        left = first[g * GROUP : (g + 1) * GROUP].reshape(span, width)
        right = second[g * GROUP : (g + 1) * GROUP].reshape(span, width)
        inner = lax.dot_general(taken, left, (((1,), (1,)), ((), ())), preferred_element_type=F32)
        kept = jnp.where(own & (keep[g : g + 1, :] > 0), inner, 0.0).astype(BF16)
        outer = jnp.dot(kept, right, preferred_element_type=F32)
        for i in range(GROUP):
            at = dst_at[g * GROUP + i]
            acc[at] = acc[at] + outer[i * probes : (i + 1) * probes]
    half = mine.shape[0]
    mine[...] = acc[:half].astype(mine.dtype)
    send[...] = acc[half:].astype(send.dtype)


def tiles(pieces, src_at, dst_at, keep, first, second, blocks, send_dtype, name):
    count, rank, width = first.shape
    probes = pieces[0].shape[1]
    rows = len(pieces) * pieces[0].shape[0]
    half = (blocks // 2, probes, width)

    def body(*refs):
        tiles_body(len(pieces), *refs)

    smem = whole(pltpu.SMEM)
    specs = [smem, smem] + [whole()] * (len(pieces) + 3)
    return local(
        body,
        [shape(half, F32), shape(half, send_dtype)],
        src_at,
        dst_at,
        keep,
        *pieces,
        first,
        second,
        name=name,
        specs=specs,
        flops=4 * count * rank * width * probes * GROUP,
        scratch=(2 * rows + 4 * blocks) * probes * width,
        scratches=[
            pltpu.VMEM((rows, probes, width), BF16),
            pltpu.VMEM((blocks, probes, width), F32),
        ],
    )


def place(relative, order):
    at = jnp.zeros_like(relative)
    for k, bit in enumerate(order):
        at = at + jnp.where((relative & bit) != 0, 1 << k, 0)
    return at


def shards(
    probes,
    level_set,
    unit_label,
    contrast,
    station_weight,
    u_factor,
    v_factor,
    col_owner,
    col_local,
    row_owner,
    row_local,
    tile_rank,
):
    peers = lax.axis_size("tile")
    me = lax.axis_index("tile")
    tile_count, rank_max, station_width = u_factor.shape
    cell_width = v_factor.shape[2]
    probe_count, cell_total = probes.shape
    cell_blocks = cell_total // cell_width
    station_blocks = station_weight.shape[0] // (peers * station_width)
    half_blocks = cell_blocks // 2
    far = [1 << k for k in range(2, peers.bit_length() - 1)][::-1]
    order_p = [2] + far
    order_q = far + [2]
    split_bits = [1 << k for k in range(peers.bit_length() - 3)]
    join_bits = [peers // 4, peers // 2]

    half_dims = (half_blocks, probe_count, cell_width)
    lanes = (cell_total // 128, 128)
    part_p, part_q, scaling = local(
        scale_body,
        [shape(half_dims, BF16), shape(half_dims, BF16), shape(lanes, F32)],
        contrast,
        level_set.reshape(lanes),
        unit_label.reshape(lanes),
        probes,
        name="scale",
        specs=[whole(pltpu.SMEM)] + [whole(pltpu.HBM)] * 3,
        scratches=[
            pltpu.VMEM(lanes, F32),
            pltpu.VMEM(lanes, jnp.int32),
            pltpu.VMEM(probes.shape, F32),
            pltpu.SemaphoreType.DMA((3,)),
        ],
    )
    scaling, station_weight, col_owner, col_local, row_owner, row_local, tile_rank = lax.optimization_barrier(
        (scaling, station_weight, col_owner, col_local, row_owner, row_local, tile_rank)
    )

    start = me * tile_count

    def mine_of(table):
        return lax.dynamic_slice_in_dim(table.reshape(-1), start, tile_count)

    col_relative = mine_of(col_owner) ^ me
    col_here = mine_of(col_local)
    row_holder = mine_of(row_owner)
    row_here = mine_of(row_local)
    rank_mine = mine_of(tile_rank)
    is_q = col_here >= half_blocks
    span = peers // 2
    cell_at = (
        (col_relative & 1) * (span * cell_blocks)
        + jnp.where(is_q, place(col_relative, order_q), place(col_relative, order_p)) * half_blocks
        + jnp.where(is_q, span * half_blocks - half_blocks, 0)
        + col_here
    )
    row_at = place(row_holder ^ me, split_bits[::-1]) * (4 * station_blocks)
    row_at = row_at + (row_holder // (peers // 4)) * station_blocks + row_here
    keep = (jnp.arange(rank_max, dtype=jnp.int32)[None, :] < rank_mine[:, None]).astype(F32)
    keep = keep.reshape(tile_count // GROUP, GROUP * rank_max)
    weight = lax.dynamic_slice_in_dim(
        station_weight.reshape(4, peers // 4, station_blocks, station_width), me % (peers // 4), 1, 1
    ).reshape(4 * station_blocks, 1, station_width)

    for step in range(len(order_p)):
        got_p = swap(part_p, order_p[step])
        got_q = swap(part_q, order_q[step])
        if step < len(order_p) - 1:
            after = ()
            if step == 0:
                after = (cell_at, row_at, keep, weight)
            if step == 1:
                v_here = load(v_factor, (part_p, part_q), "load_v")
                u_here = load(u_factor, (part_p, part_q, v_here), "load_u")
                after = (u_here,)
            part_p, part_q = join((part_p, got_p), (part_q, got_q), after=after)
    pieces = [part_p, got_p, part_q, got_q]
    pieces = pieces + [swap(piece, 1) for piece in pieces]

    total, send = tiles(
        pieces, cell_at, row_at, keep, v_here, u_here, peers * station_blocks, F32, "forward"
    )
    got = swap(send, split_bits[0])
    for bit in split_bits[1:]:
        total, send = fold((total, got), parts=2)
        got = swap(send, bit)
    for bit in join_bits:
        total, send = plus(total, got)
        got = swap(send, bit)
    weighted = plus(total, got, weight)[0]
    pieces = [weighted]
    for bit in split_bits[::-1]:
        pieces = pieces + [swap(piece, bit) for piece in pieces]

    keep_all, send_all = tiles(
        pieces, row_at, cell_at, keep, u_here, v_here, peers * cell_blocks, BF16, "adjoint"
    )
    got_all = swap(send_all, 1)
    pairs = [(keep_all, got_all)]
    for bit_p, bit_q in zip(order_p[::-1], order_q[::-1]):
        keep_p, send_p, keep_q, send_q = fold(*pairs)
        pairs = [(keep_p, swap(send_p, bit_p)), (keep_q, swap(send_q, bit_q))]
    return local(
        final_body,
        [shape((probe_count, cell_total), F32)],
        *pairs[0],
        *pairs[1],
        scaling,
        name="final",
        far_out=True,
    )[0]


def solution(mesh):
    placed = (
        P(None, ("groups", "tile")),
        P(("groups", "tile")),
        P(("groups", "tile")),
        P("groups"),
        P("groups"),
        P(("groups", "tile"), None, None),
        P(("groups", "tile"), None, None),
        P("groups", None),
        P("groups"),
        P("groups", None),
        P("groups"),
        P("groups"),
    )
    return jax.shard_map(
        shards, mesh=mesh, in_specs=placed, out_specs=P(None, ("groups", "tile")), check_vma=False
    )
```

```python
import math

import jax
import jax.numpy as jnp
from jax import lax
from jax.experimental import pallas as pl
from jax.experimental.pallas import tpu as pltpu
from jax.sharding import PartitionSpec as P

BF16 = jnp.bfloat16
F32 = jnp.float32
I32 = jnp.int32
GROUP = 8
LANES = 128
MIB = 1024 * 1024


def whole(space=pltpu.VMEM):
    return pl.BlockSpec(memory_space=space)


def shape(dims, dtype):
    return jax.ShapeDtypeStruct(tuple(dims), dtype)


def size_of(array):
    return math.prod(array.shape) * jnp.dtype(array.dtype).itemsize


def swap(array, bits):
    count = lax.axis_size("tile")
    return lax.ppermute(array, "tile", [(i, i ^ bits[i & 1]) for i in range(count)])


def local(body, outs, *ins, name, scratch=0, scratches=(), specs=None, flops=0, far_out=False, after=()):
    nbytes = sum(size_of(a) for a in (*ins, *outs))
    specs = list(specs or [whole()] * len(ins)) + [whole()] * len(after)
    own = len(ins)
    ins = [pltpu.with_memory_space_constraint(a, s.memory_space) for a, s in zip((*ins, *after), specs)]

    def run(*refs):
        body(*refs[:own], *refs[len(ins) :])

    return pl.pallas_call(
        run,
        out_shape=[a if far_out else pltpu.VMEM(a.shape, a.dtype) for a in outs],
        in_specs=specs,
        out_specs=[whole()] * len(outs),
        scratch_shapes=list(scratches),
        compiler_params=pltpu.CompilerParams(vmem_limit_bytes=scratch + 8 * MIB),
        cost_estimate=pl.CostEstimate(flops=flops, bytes_accessed=nbytes, transcendentals=0),
        name=name,
    )(*ins)


def fetch(pairs, sems):
    copies = [pltpu.make_async_copy(a, b, sems.at[i]) for i, (a, b) in enumerate(pairs)]
    for copy in copies:
        copy.start()
    for copy in copies:
        copy.wait()


def load_body(source, out, sems):
    n = source.shape[0] // sems.shape[0]
    rows = [pl.ds(i * n, n) for i in range(sems.shape[0])]
    fetch([(source.at[r], out.at[r]) for r in rows], sems)


def load(array, after, name):
    return local(
        load_body,
        [shape(array.shape, array.dtype)],
        array,
        name=name,
        specs=[whole(pltpu.HBM)],
        scratches=[pltpu.SemaphoreType.DMA((8,))],
        after=after,
    )[0]


def scale_body(contrast, level, label, probes, part, scaling, contrast_near, level_near, label_near, probes_near, sems):
    fetch(
        [(contrast, contrast_near), (level, level_near), (label, label_near), (probes, probes_near)],
        sems,
    )
    value = level_near[...]
    unit = label_near[...]
    factor = jnp.zeros_like(value)
    for k in range(contrast.shape[0]):
        factor = jnp.where(unit == k, contrast_near[k], factor)
    scaling[...] = factor / (1.0 + value * value)
    blocks, _, width = part.shape
    rows = width // LANES
    for b in range(blocks):
        for c in range(rows):
            j = b * rows + c
            piece = probes_near[:, j * LANES : (j + 1) * LANES] * scaling[j : j + 1, :]
            part[b, :, c * LANES : (c + 1) * LANES] = piece.astype(BF16)


def final_body(keep, recv, scaling, out):
    blocks, _, width = keep.shape
    rows = width // LANES
    for b in range(blocks):
        for c in range(rows):
            j = b * rows + c
            lanes = slice(c * LANES, (c + 1) * LANES)
            total = keep[b, :, lanes] + recv[b, :, lanes].astype(F32)
            out[:, j * LANES : (j + 1) * LANES] = total * scaling[j : j + 1, :]


def join_body(first, second, out):
    n = first.shape[0]
    out[:n] = first[...]
    out[n:] = second[...]


def join(first, second, after=()):
    out = shape((2 * first.shape[0],) + first.shape[1:], first.dtype)
    return local(join_body, [out], first, second, name="join", after=after)[0]


def plus(total, got):
    def body(total, got, out, send):
        done = total[...] + got[...].astype(F32)
        out[...] = done
        send[...] = done.astype(BF16)

    return local(body, [shape(total.shape, F32), shape(total.shape, BF16)], total, got, name="plus")


def weigh(total, got, weight):
    def body(total, got, weight, out):
        blocks, _, width = out.shape
        rows = width // LANES
        for b in range(blocks):
            for c in range(rows):
                lanes = slice(c * LANES, (c + 1) * LANES)
                done = total[b, :, lanes] + got[b, :, lanes].astype(F32)
                j = b * rows + c
                out[b, :, lanes] = (done * weight[j : j + 1, :]).astype(BF16)

    return local(body, [shape(total.shape, BF16)], total, got, weight, name="weigh")[0]


def fold(keep, recv):
    half = keep.shape[0] // 2
    dims = (half,) + keep.shape[1:]

    def body(keep, recv, mine, send):
        mine[...] = keep[:half] + recv[:half].astype(F32)
        send[...] = (keep[half:] + recv[half:].astype(F32)).astype(BF16)

    return local(body, [shape(dims, F32), shape(dims, BF16)], keep, recv, name="fold")


def tiles_body(piece_count, src_row, dst_row, table_near, *refs):
    pieces = refs[:piece_count]
    first, second, mine, send, at, table, acc, sem = refs[piece_count:]
    count, rank, width = first.shape
    groups = count // GROUP
    copy = pltpu.make_async_copy(table_near, at, sem)
    copy.start()
    acc[...] = jnp.zeros_like(acc)
    per = pieces[0].shape[0]
    for i, piece in enumerate(pieces):
        table[i * per : (i + 1) * per] = piece[...]
    probes = table.shape[1]
    span = GROUP * rank
    row_tile = lax.broadcasted_iota(I32, (GROUP * probes, span), 0) // probes
    col_tile = lax.broadcasted_iota(I32, (GROUP * probes, span), 1) // rank
    component = lax.broadcasted_iota(I32, (GROUP * probes, span), 1) % rank
    own = jnp.where(row_tile == col_tile, component, rank)
    lane_tile = lax.broadcasted_iota(I32, (1, span), 1) // rank
    copy.wait()
    for g in range(groups):
        taken = jnp.concatenate(
            [table[at[src_row, g * GROUP + i]].astype(F32) for i in range(GROUP)], axis=0
        ).astype(BF16)
        left = first[g * GROUP : (g + 1) * GROUP].reshape(span, width)
        right = second[g * GROUP : (g + 1) * GROUP].reshape(span, width)
        inner = lax.dot_general(taken, left, (((1,), (1,)), ((), ())), preferred_element_type=F32)
        limit = jnp.zeros((1, span), I32)
        for i in range(GROUP):
            limit = jnp.where(lane_tile == i, at[2, g * GROUP + i], limit)
        kept = jnp.where(own < limit, inner, 0.0).astype(BF16)
        outer = jnp.dot(kept, right, preferred_element_type=F32)
        for i in range(GROUP):
            to = at[dst_row, g * GROUP + i]
            acc[to] = acc[to] + outer[i * probes : (i + 1) * probes]
    half = mine.shape[0]
    mine[...] = acc[:half].astype(mine.dtype)
    send[...] = acc[half:].astype(send.dtype)


def tiles(pieces, src_row, dst_row, table, first, second, blocks, send_dtype, name):
    count, rank, width = first.shape
    probes = pieces[0].shape[1]
    rows = len(pieces) * pieces[0].shape[0]
    half = (blocks // 2, probes, width)

    def body(*refs):
        tiles_body(len(pieces), src_row, dst_row, *refs)

    return local(
        body,
        [shape(half, F32), shape(half, send_dtype)],
        table,
        *pieces,
        first,
        second,
        name=name,
        flops=4 * count * rank * width * probes * GROUP,
        scratch=(2 * rows + 4 * blocks) * probes * width,
        scratches=[
            pltpu.SMEM(table.shape, I32),
            pltpu.VMEM((rows, probes, width), BF16),
            pltpu.VMEM((blocks, probes, width), F32),
            pltpu.SemaphoreType.DMA,
        ],
    )


def place(relative, order):
    at = jnp.zeros_like(relative)
    for k, bit in enumerate(order):
        at = at + jnp.where((relative & bit) != 0, 1 << k, 0)
    return at


def plan(owners, weight, orders, splits, joins, cell_blocks, station_blocks, after):
    peers, count = owners[0].shape
    rows = weight.shape[0] // peers

    def body(*refs):
        far, weight_far, table, weight_near, near, sems = refs[:5], refs[5], refs[6], refs[7], refs[8:13], refs[13]
        me = lax.axis_index("tile")
        odd = (me & 1) != 0
        pairs = list(zip(far, near))
        for k in range(4):
            holder = me
            for bits in (0, 1):
                bit = jnp.where(odd, joins[1][bits], joins[0][bits])
                holder = (holder | bit) if (k >> bits) & 1 else (holder & ~bit)
            start = pl.multiple_of(holder * rows, rows)
            pairs.append((weight_far.at[pl.ds(start, rows)], weight_near.at[pl.ds(k * rows, rows)]))
        fetch(pairs, sems)
        col_owner, col_local, row_owner, row_local, rank = [ref[pl.ds(me, 1), :] for ref in near]
        span = peers // 2
        away = col_owner ^ me
        spot = jnp.where((col_owner & 1) != 0, place(away, orders[1]), place(away, orders[0]))
        table[0:1, :] = ((away & 1) * span + spot) * cell_blocks + col_local
        away = row_owner ^ me
        spots = []
        for q in (0, 1):
            spot = place(away, splits[q][::-1]) * 4 + place(row_owner, joins[q])
            spots.append(spot)
        spot = jnp.where((row_owner & 1) != 0, spots[1], spots[0])
        table[1:2, :] = ((away & 1) * span + spot) * station_blocks + row_local
        table[2:3, :] = rank

    return local(
        body,
        [shape((8, count), I32), shape((4 * rows, LANES), F32)],
        *owners,
        weight,
        name="plan",
        specs=[whole(pltpu.HBM)] * 6,
        scratches=[pltpu.VMEM((peers, count), I32)] * 5 + [pltpu.SemaphoreType.DMA((9,))],
        after=after,
    )


def shards(
    probes,
    level_set,
    unit_label,
    contrast,
    station_weight,
    u_factor,
    v_factor,
    col_owner,
    col_local,
    row_owner,
    row_local,
    tile_rank,
):
    peers = lax.axis_size("tile")
    tile_count, _, station_width = u_factor.shape
    cell_width = v_factor.shape[2]
    probe_count, cell_total = probes.shape
    cell_blocks = cell_total // cell_width
    station_blocks = station_weight.shape[0] // (peers * station_width)
    bits = [1 << k for k in range(1, peers.bit_length() - 1)]
    far = bits[:0:-1]
    orders = (bits[:1] + far, far + bits[:1])
    splits = (bits[:-2], bits[1:-1])
    joins = ((bits[-1], bits[-2]), (bits[0], bits[-1]))

    lanes = (cell_total // LANES, LANES)
    part, scaling = local(
        scale_body,
        [shape((cell_blocks, probe_count, cell_width), BF16), shape(lanes, F32)],
        contrast,
        level_set.reshape(lanes),
        unit_label.reshape(lanes),
        probes,
        name="scale",
        specs=[whole(pltpu.HBM)] * 4,
        scratches=[
            pltpu.SMEM(contrast.shape, F32),
            pltpu.VMEM(lanes, F32),
            pltpu.VMEM(lanes, I32),
            pltpu.VMEM(probes.shape, F32),
            pltpu.SemaphoreType.DMA((4,)),
        ],
    )
    steps = list(zip(*orders))
    for step, pair in enumerate(steps):
        got = swap(part, pair)
        if step == 0:
            table, weight = plan(
                [a.reshape(peers, tile_count) for a in (col_owner, col_local, row_owner, row_local, tile_rank)],
                station_weight.reshape(-1, LANES),
                orders,
                splits,
                joins,
                cell_blocks,
                station_blocks,
                (scaling,),
            )
            part = join(part, got, after=(table,))
        elif step == 1:
            v_here = load(v_factor, (part,), "load_v")
            u_here = load(u_factor, (part, v_here), "load_u")
            part = join(part, got, after=(u_here,))
        elif step < len(steps) - 1:
            part = join(part, got)
    pieces = [part, got]
    pieces = pieces + [swap(piece, (1, 1)) for piece in pieces]

    total, send = tiles(pieces, 0, 1, table, v_here, u_here, peers * station_blocks, F32, "forward")
    got = swap(send, (1, 1))
    for pair in zip(*splits):
        total, send = fold(total, got)
        got = swap(send, pair)
    for pair in zip(*joins):
        total, send = plus(total, got)
        got = swap(send, pair)
    pieces = [weigh(total, got, weight)]
    for pair in list(zip(*splits))[::-1] + [(1, 1)]:
        pieces = pieces + [swap(piece, pair) for piece in pieces]

    keep, send = tiles(pieces, 1, 0, table, u_here, v_here, peers * cell_blocks, BF16, "adjoint")
    got = swap(send, (1, 1))
    for pair in steps[::-1]:
        keep, send = fold(keep, got)
        got = swap(send, pair)
    return local(
        final_body,
        [shape((probe_count, cell_total), F32)],
        keep,
        got,
        scaling,
        name="final",
        far_out=True,
    )[0]


def solution(mesh):
    placed = (
        P(None, ("groups", "tile")),
        P(("groups", "tile")),
        P(("groups", "tile")),
        P("groups"),
        P("groups"),
        P(("groups", "tile"), None, None),
        P(("groups", "tile"), None, None),
        P("groups", None),
        P("groups"),
        P("groups", None),
        P("groups"),
        P("groups"),
    )
    return jax.shard_map(
        shards, mesh=mesh, in_specs=placed, out_specs=P(None, ("groups", "tile")), check_vma=False
    )
```

```python
import math

import jax
import jax.numpy as jnp
from jax import lax
from jax.experimental import pallas as pl
from jax.experimental.pallas import tpu as pltpu
from jax.sharding import PartitionSpec as P

BF16 = jnp.bfloat16
F32 = jnp.float32
I32 = jnp.int32
GROUP = 8
SKEW = 3
SQUARE = (6, 2, 4)
LANES = 128
MIB = 1024 * 1024


def whole(space=pltpu.VMEM):
    return pl.BlockSpec(memory_space=space)


def shape(dims, dtype):
    return jax.ShapeDtypeStruct(tuple(dims), dtype)


def size_of(array):
    return math.prod(array.shape) * jnp.dtype(array.dtype).itemsize


def swap(array, bits):
    count = lax.axis_size("tile")
    return lax.ppermute(array, "tile", [(i, i ^ bits) for i in range(count)])


def local(body, outs, *ins, name, scratch=0, scratches=(), specs=None, flops=0, far_out=False, after=()):
    nbytes = sum(size_of(a) for a in (*ins, *outs))
    specs = list(specs or [whole()] * len(ins)) + [whole()] * len(after)
    own = len(ins)
    ins = [pltpu.with_memory_space_constraint(a, s.memory_space) for a, s in zip((*ins, *after), specs)]

    def run(*refs):
        body(*refs[:own], *refs[len(ins) :])

    return pl.pallas_call(
        run,
        out_shape=[a if far_out else pltpu.VMEM(a.shape, a.dtype) for a in outs],
        in_specs=specs,
        out_specs=[whole()] * len(outs),
        scratch_shapes=list(scratches),
        compiler_params=pltpu.CompilerParams(vmem_limit_bytes=scratch + 8 * MIB),
        cost_estimate=pl.CostEstimate(flops=flops, bytes_accessed=nbytes, transcendentals=0),
        name=name,
    )(*ins)


def fetch(pairs, sems):
    copies = [pltpu.make_async_copy(a, b, sems.at[i]) for i, (a, b) in enumerate(pairs)]
    for copy in copies:
        copy.start()
    for copy in copies:
        copy.wait()


def load_body(source, out, sems):
    n = source.shape[0] // sems.shape[0]
    rows = [pl.ds(i * n, n) for i in range(sems.shape[0])]
    fetch([(source.at[r], out.at[r]) for r in rows], sems)


def load(array, after, name):
    return local(
        load_body,
        [shape(array.shape, array.dtype)],
        array,
        name=name,
        specs=[whole(pltpu.HBM)],
        scratches=[pltpu.SemaphoreType.DMA((8,))],
        after=after,
    )[0]


def scale_body(
    contrast, level, label, probes, part_p, part_q, scaling, contrast_near, level_near, label_near, probes_near, sems
):
    fetch(
        [(contrast, contrast_near), (level, level_near), (label, label_near), (probes, probes_near)],
        sems,
    )
    value = level_near[...]
    unit = label_near[...]
    factor = jnp.zeros_like(value)
    for k in range(contrast.shape[0]):
        factor = jnp.where(unit == k, contrast_near[k], factor)
    scaling[...] = factor / (1.0 + value * value)
    blocks, _, width = part_p.shape
    rows = width // LANES
    for half, part in enumerate((part_p, part_q)):
        for b in range(blocks):
            for c in range(rows):
                j = (half * blocks + b) * rows + c
                piece = probes_near[:, j * LANES : (j + 1) * LANES] * scaling[j : j + 1, :]
                part[b, :, c * LANES : (c + 1) * LANES] = piece.astype(BF16)


def final_body(keep_p, recv_p, keep_q, recv_q, scaling, out):
    blocks, _, width = keep_p.shape
    rows = width // LANES
    for half, (keep, recv) in enumerate(((keep_p, recv_p), (keep_q, recv_q))):
        for b in range(blocks):
            for c in range(rows):
                j = (half * blocks + b) * rows + c
                lanes = slice(c * LANES, (c + 1) * LANES)
                total = keep[b, :, lanes] + recv[b, :, lanes].astype(F32)
                out[:, j * LANES : (j + 1) * LANES] = total * scaling[j : j + 1, :]


def join_body(*refs):
    out, at = refs[-1], 0
    for ref in refs[:-1]:
        out[at : at + ref.shape[0]] = ref[...]
        at += ref.shape[0]


def join(*pieces, after=()):
    out = shape((sum(a.shape[0] for a in pieces),) + pieces[0].shape[1:], pieces[0].dtype)
    return local(join_body, [out], *pieces, name="join", after=after)[0]


def plus(total, *gots):
    def body(total, *refs):
        done = total[...]
        for ref in refs[:-2]:
            done = done + ref[...].astype(F32)
        refs[-2][...] = done
        refs[-1][...] = done.astype(BF16)

    return local(body, [shape(total.shape, F32), shape(total.shape, BF16)], total, *gots, name="plus")


def weigh(total, got, weight):
    def body(total, got, weight, out):
        blocks, _, width = out.shape
        rows = width // LANES
        for b in range(blocks):
            for c in range(rows):
                lanes = slice(c * LANES, (c + 1) * LANES)
                done = total[b, :, lanes] + got[b, :, lanes].astype(F32)
                j = b * rows + c
                out[b, :, lanes] = (done * weight[j : j + 1, :]).astype(BF16)

    return local(body, [shape(total.shape, BF16)], total, got, weight, name="weigh")[0]


def fold(keep, recv, dtypes=(F32, BF16)):
    n = keep.shape[0] // len(dtypes)

    def body(keep, recv, *outs):
        for i, out in enumerate(outs):
            at = slice(i * n, (i + 1) * n)
            out[...] = (keep[at] + recv[at].astype(F32)).astype(out.dtype)

    return local(body, [shape((n,) + keep.shape[1:], t) for t in dtypes], keep, recv, name="fold")


def tiles_body(piece_count, src_row, dst_row, table_near, *refs):
    pieces = refs[:piece_count]
    first, second, mine, send, at, table, acc, sem = refs[piece_count:]
    count, rank, width = first.shape
    groups = count // GROUP
    copy = pltpu.make_async_copy(table_near, at, sem)
    copy.start()
    acc[...] = jnp.zeros_like(acc)
    join_body(*pieces, table)
    probes = table.shape[1]
    span = GROUP * rank
    row_tile = lax.broadcasted_iota(I32, (GROUP * probes, span), 0) // probes
    col_tile = lax.broadcasted_iota(I32, (GROUP * probes, span), 1) // rank
    component = lax.broadcasted_iota(I32, (GROUP * probes, span), 1) % rank
    own = jnp.where(row_tile == col_tile, component, rank)
    lane_tile = lax.broadcasted_iota(I32, (1, span), 1) // rank
    copy.wait()

    def inner_of(g):
        taken = jnp.concatenate(
            [table[at[src_row, g * GROUP + i]].astype(F32) for i in range(GROUP)], axis=0
        ).astype(BF16)
        left = first[g * GROUP : (g + 1) * GROUP].reshape(span, width)
        inner = lax.dot_general(taken, left, (((1,), (1,)), ((), ())), preferred_element_type=F32)
        limit = jnp.zeros((1, span), I32)
        for i in range(GROUP):
            limit = jnp.where(lane_tile == i, at[2, g * GROUP + i], limit)
        return jnp.where(own < limit, inner, 0.0).astype(BF16)

    def outer_of(g, kept):
        right = second[g * GROUP : (g + 1) * GROUP].reshape(span, width)
        return jnp.dot(kept, right, preferred_element_type=F32)

    def add(g, outer):
        for i in range(GROUP):
            to = at[dst_row, g * GROUP + i]
            acc[to] = acc[to] + outer[i * probes : (i + 1) * probes]

    kept, outer = {}, {}
    for step in range(groups + 2 * SKEW):
        if step >= 2 * SKEW:
            add(step - 2 * SKEW, outer.pop(step - 2 * SKEW))
        if 0 <= step - SKEW < groups:
            outer[step - SKEW] = outer_of(step - SKEW, kept.pop(step - SKEW))
        if step < groups:
            kept[step] = inner_of(step)
    half = mine.shape[0]
    mine[...] = acc[:half].astype(mine.dtype)
    send[...] = acc[half:].astype(send.dtype)


def tiles(pieces, src_row, dst_row, table, first, second, blocks, send_dtype, name):
    count, rank, width = first.shape
    probes = pieces[0].shape[1]
    rows = sum(piece.shape[0] for piece in pieces)
    half = (blocks // 2, probes, width)

    def body(*refs):
        tiles_body(len(pieces), src_row, dst_row, *refs)

    return local(
        body,
        [shape(half, F32), shape(half, send_dtype)],
        table,
        *pieces,
        first,
        second,
        name=name,
        flops=4 * count * rank * width * probes * GROUP,
        scratch=(2 * rows + 4 * blocks) * probes * width,
        scratches=[
            pltpu.SMEM(table.shape, I32),
            pltpu.VMEM((rows, probes, width), BF16),
            pltpu.VMEM((blocks, probes, width), F32),
            pltpu.SemaphoreType.DMA,
        ],
    )


def place(relative, order):
    at = jnp.zeros_like(relative)
    for k, bit in enumerate(order):
        at = at + jnp.where((relative & bit) != 0, 1 << k, 0)
    return at


def plan(owners, weight, orders, cell_blocks, station_blocks, after):
    peers, count = owners[0].shape
    rows = weight.shape[0] // peers
    rest = peers // 8
    half = cell_blocks // 2

    def body(*refs):
        far, weight_far, table, weight_near, near, sems = refs[:5], refs[5], refs[6], refs[7], refs[8:13], refs[13]
        me = lax.axis_index("tile")
        pairs = list(zip(far, near))
        for k in range(rest):
            start = pl.multiple_of((k * 8 + (me & 7)) * rows, rows)
            pairs.append((weight_far.at[pl.ds(start, rows)], weight_near.at[pl.ds(k * rows, rows)]))
        fetch(pairs, sems)
        col_owner, col_local, row_owner, row_local, rank = [ref[pl.ds(me, 1), :] for ref in near]
        span = peers // 2
        away = col_owner ^ me
        is_q = col_local >= half
        spot = jnp.where(is_q, place(away, orders[1]) + (span - 1), place(away, orders[0]))
        table[0:1, :] = (away & 1) * (span * cell_blocks) + spot * half + col_local
        away = row_owner ^ me
        spot = (away & 1) * 4 + ((away & 4) // 2) + ((away & 2) // 2)
        table[1:2, :] = (spot * rest + row_owner // 8) * station_blocks + row_local
        table[2:3, :] = rank

    return local(
        body,
        [shape((8, count), I32), shape((rest * rows, LANES), F32)],
        *owners,
        weight,
        name="plan",
        specs=[whole(pltpu.HBM)] * 6,
        scratches=[pltpu.VMEM((peers, count), I32)] * 5 + [pltpu.SemaphoreType.DMA((5 + rest,))],
        after=after,
    )


def shards(
    probes,
    level_set,
    unit_label,
    contrast,
    station_weight,
    u_factor,
    v_factor,
    col_owner,
    col_local,
    row_owner,
    row_local,
    tile_rank,
):
    peers = lax.axis_size("tile")
    tile_count, _, station_width = u_factor.shape
    cell_width = v_factor.shape[2]
    probe_count, cell_total = probes.shape
    cell_blocks = cell_total // cell_width
    station_blocks = station_weight.shape[0] // (peers * station_width)
    bits = [1 << k for k in range(1, peers.bit_length() - 1)]
    far = bits[:0:-1]
    orders = (bits[:1] + far, far + bits[:1])

    lanes = (cell_total // LANES, LANES)
    half_dims = (cell_blocks // 2, probe_count, cell_width)
    part_p, part_q, scaling = local(
        scale_body,
        [shape(half_dims, BF16), shape(half_dims, BF16), shape(lanes, F32)],
        contrast,
        level_set.reshape(lanes),
        unit_label.reshape(lanes),
        probes,
        name="scale",
        specs=[whole(pltpu.HBM)] * 4,
        scratches=[
            pltpu.SMEM(contrast.shape, F32),
            pltpu.VMEM(lanes, F32),
            pltpu.VMEM(lanes, I32),
            pltpu.VMEM(probes.shape, F32),
            pltpu.SemaphoreType.DMA((4,)),
        ],
    )
    table, weight = plan(
        [a.reshape(peers, tile_count) for a in (col_owner, col_local, row_owner, row_local, tile_rank)],
        station_weight.reshape(-1, LANES),
        orders,
        cell_blocks,
        station_blocks,
        (scaling,),
    )
    steps = list(zip(*orders))
    after = (table,)
    for step, (bit_p, bit_q) in enumerate(steps):
        got_p = swap(part_p, bit_p)
        got_q = swap(part_q, bit_q)
        if step == 1:
            v_here = load(v_factor, (part_p, part_q), "load_v")
            u_here = load(u_factor, (part_p, part_q, v_here), "load_u")
            after = (u_here,)
        if step < len(steps) - 1:
            part_p = join(part_p, got_p, after=after)
            part_q = join(part_q, got_q)
            after = ()
    pieces = [part_p, got_p, part_q, got_q]
    pieces = pieces + [swap(piece, 1) for piece in pieces]

    total, send = tiles(pieces, 0, 1, table, v_here, u_here, peers * station_blocks, F32, "forward")
    got = swap(send, 1)
    total, send_y, send_z, send_yz = fold(total, got, (F32, BF16, BF16, BF16))
    sends = {2: send_y, 4: send_z, 6: send_yz}
    total, send = plus(total, *[swap(sends[k], k) for k in SQUARE])
    for bit in bits[2:-1]:
        total, send = plus(total, swap(send, bit))
    weighted = weigh(total, swap(send, bits[-1]), weight)
    gots = {k: swap(weighted, k) for k in SQUARE}
    around = join(gots[2], gots[4], gots[6])
    pieces = [weighted, around, swap(weighted, 1), swap(around, 1)]

    keep, send = tiles(pieces, 1, 0, table, u_here, v_here, peers * cell_blocks, BF16, "adjoint")
    got = swap(send, 1)
    keep_p, send_p, keep_q, send_q = fold(keep, got, (F32, BF16, F32, BF16))
    for step, (bit_p, bit_q) in enumerate(steps[::-1]):
        if step > 0:
            keep_p, send_p = fold(keep_p, got_p)
            keep_q, send_q = fold(keep_q, got_q)
        got_p = swap(send_p, bit_p)
        got_q = swap(send_q, bit_q)
    return local(
        final_body,
        [shape((probe_count, cell_total), F32)],
        keep_p,
        got_p,
        keep_q,
        got_q,
        scaling,
        name="final",
        far_out=True,
    )[0]


def solution(mesh):
    placed = (
        P(None, ("groups", "tile")),
        P(("groups", "tile")),
        P(("groups", "tile")),
        P("groups"),
        P("groups"),
        P(("groups", "tile"), None, None),
        P(("groups", "tile"), None, None),
        P("groups", None),
        P("groups"),
        P("groups", None),
        P("groups"),
        P("groups"),
    )
    return jax.shard_map(
        shards, mesh=mesh, in_specs=placed, out_specs=P(None, ("groups", "tile")), check_vma=False
    )
```

```python
import math

import jax
import jax.numpy as jnp
from jax import lax
from jax.experimental import pallas as pl
from jax.experimental.pallas import tpu as pltpu
from jax.sharding import PartitionSpec as P

BF16 = jnp.bfloat16
F32 = jnp.float32
I32 = jnp.int32
GROUP = 8
SKEW = 3
SQUARE = (6, 2, 4)
LANES = 128
MIB = 1024 * 1024


def whole(space=pltpu.VMEM):
    return pl.BlockSpec(memory_space=space)


def shape(dims, dtype):
    return jax.ShapeDtypeStruct(tuple(dims), dtype)


def size_of(array):
    return math.prod(array.shape) * jnp.dtype(array.dtype).itemsize


def swap(array, bits):
    count = lax.axis_size("tile")
    return lax.ppermute(array, "tile", [(i, i ^ bits) for i in range(count)])


def local(
    body, outs, *ins, name, scratch=0, scratches=(), specs=None, out_specs=None, flops=0, after=(), aliases=None
):
    nbytes = sum(size_of(a) for a in (*ins, *outs))
    specs = list(specs or [whole()] * len(ins)) + [whole()] * len(after)
    out_specs = list(out_specs or [whole()] * len(outs))
    own = len(ins)
    ins = [pltpu.with_memory_space_constraint(a, s.memory_space) for a, s in zip((*ins, *after), specs)]

    def run(*refs):
        body(*refs[:own], *refs[len(ins) :])

    return pl.pallas_call(
        run,
        out_shape=[a if s.memory_space is None else s.memory_space(a.shape, a.dtype) for a, s in zip(outs, out_specs)],
        in_specs=specs,
        out_specs=[whole() if s.memory_space is None else s for s in out_specs],
        input_output_aliases=aliases or {},
        scratch_shapes=list(scratches),
        compiler_params=pltpu.CompilerParams(vmem_limit_bytes=scratch + 8 * MIB),
        cost_estimate=pl.CostEstimate(flops=flops, bytes_accessed=nbytes, transcendentals=0),
        name=name,
    )(*ins)


def fetch(pairs, sems):
    copies = [pltpu.make_async_copy(a, b, sems.at[i]) for i, (a, b) in enumerate(pairs)]
    for copy in copies:
        copy.start()
    for copy in copies:
        copy.wait()


def load_body(source, out, sems):
    n = source.shape[0] // sems.shape[0]
    rows = [pl.ds(i * n, n) for i in range(sems.shape[0])]
    fetch([(source.at[r], out.at[r]) for r in rows], sems)


def load(array, after, name):
    return local(
        load_body,
        [shape(array.shape, array.dtype)],
        array,
        name=name,
        specs=[whole(pltpu.HBM)],
        scratches=[pltpu.SemaphoreType.DMA((8,))],
        after=after,
    )[0]


def scale_body(
    contrast, level, label, probes, part_p, part_q, scaling, contrast_near, level_near, label_near, probes_near, sems
):
    fetch(
        [(contrast, contrast_near), (level, level_near), (label, label_near), (probes, probes_near)],
        sems,
    )
    value = level_near[...]
    unit = label_near[...]
    factor = jnp.zeros_like(value)
    for k in range(contrast.shape[0]):
        factor = jnp.where(unit == k, contrast_near[k], factor)
    scaling[...] = factor / (1.0 + value * value)
    blocks, _, width = part_p.shape
    rows = width // LANES
    for half, part in enumerate((part_p, part_q)):
        for b in range(blocks):
            for c in range(rows):
                j = (half * blocks + b) * rows + c
                piece = probes_near[:, j * LANES : (j + 1) * LANES] * scaling[j : j + 1, :]
                part[b, :, c * LANES : (c + 1) * LANES] = piece.astype(BF16)


def final_body(keep_p, recv_p, keep_q, recv_q, scaling, out):
    blocks, _, width = keep_p.shape
    rows = width // LANES
    for half, (keep, recv) in enumerate(((keep_p, recv_p), (keep_q, recv_q))):
        for b in range(blocks):
            for c in range(rows):
                j = (half * blocks + b) * rows + c
                lanes = slice(c * LANES, (c + 1) * LANES)
                total = keep[b, :, lanes] + recv[b, :, lanes].astype(F32)
                out[:, j * LANES : (j + 1) * LANES] = total * scaling[j : j + 1, :]


def join_body(*refs):
    out, at = refs[-1], 0
    for ref in refs[:-1]:
        out[at : at + ref.shape[0]] = ref[...]
        at += ref.shape[0]


def join(*pieces, after=()):
    out = shape((sum(a.shape[0] for a in pieces),) + pieces[0].shape[1:], pieces[0].dtype)
    return local(join_body, [out], *pieces, name="join", after=after)[0]


def plus(total, *gots):
    def body(total, *refs):
        done = total[...]
        for ref in refs[:-2]:
            done = done + ref[...].astype(F32)
        refs[-2][...] = done
        refs[-1][...] = done.astype(BF16)

    return local(body, [shape(total.shape, F32), shape(total.shape, BF16)], total, *gots, name="plus")


def weigh(total, got, weight):
    def body(total, got, weight, out):
        blocks, _, width = out.shape
        rows = width // LANES
        for b in range(blocks):
            for c in range(rows):
                lanes = slice(c * LANES, (c + 1) * LANES)
                done = total[b, :, lanes] + got[b, :, lanes].astype(F32)
                j = b * rows + c
                out[b, :, lanes] = (done * weight[j : j + 1, :]).astype(BF16)

    return local(body, [shape(total.shape, BF16)], total, got, weight, name="weigh")[0]


def fold(keep, recv, dtypes=(F32, BF16), base=0):
    n = recv.shape[0] // len(dtypes)

    def body(keep, recv, *outs):
        for i, out in enumerate(outs):
            mine = keep[base + i * n : base + (i + 1) * n]
            out[...] = (mine + recv[i * n : (i + 1) * n].astype(F32)).astype(out.dtype)

    return local(body, [shape((n,) + keep.shape[1:], t) for t in dtypes], keep, recv, name="fold")


def zeros(dims, after):
    def body(out):
        out[...] = jnp.zeros_like(out)

    return local(body, [shape(dims, F32)], name="zeros", after=after)[0]


def tiles_body(piece_count, src_row, dst_row, at, _, *refs):
    pieces = refs[:piece_count]
    first, second, acc, *sends, table = refs[piece_count:]
    count, rank, width = first.shape
    groups = count // GROUP
    join_body(*pieces, table)
    probes = table.shape[1]
    span = GROUP * rank
    row_tile = lax.broadcasted_iota(I32, (GROUP * probes, span), 0) // probes
    col_tile = lax.broadcasted_iota(I32, (GROUP * probes, span), 1) // rank
    component = lax.broadcasted_iota(I32, (GROUP * probes, span), 1) % rank
    own = jnp.where(row_tile == col_tile, component, rank)
    lane_tile = lax.broadcasted_iota(I32, (1, span), 1) // rank

    def inner_of(g):
        taken = jnp.concatenate(
            [table[at[src_row, g * GROUP + i]].astype(F32) for i in range(GROUP)], axis=0
        ).astype(BF16)
        left = first[g * GROUP : (g + 1) * GROUP].reshape(span, width)
        inner = lax.dot_general(taken, left, (((1,), (1,)), ((), ())), preferred_element_type=F32)
        limit = jnp.zeros((1, span), I32)
        for i in range(GROUP):
            limit = jnp.where(lane_tile == i, at[2, g * GROUP + i], limit)
        return jnp.where(own < limit, inner, 0.0).astype(BF16)

    def outer_of(g, kept):
        right = second[g * GROUP : (g + 1) * GROUP].reshape(span, width)
        return jnp.dot(kept, right, preferred_element_type=F32)

    def add(g, outer):
        for i in range(GROUP):
            to = at[dst_row, g * GROUP + i]
            acc[to] = acc[to] + outer[i * probes : (i + 1) * probes]

    kept, outer = {}, {}
    for step in range(groups + 2 * SKEW):
        if step >= 2 * SKEW:
            add(step - 2 * SKEW, outer.pop(step - 2 * SKEW))
        if 0 <= step - SKEW < groups:
            outer[step - SKEW] = outer_of(step - SKEW, kept.pop(step - SKEW))
        if step < groups:
            kept[step] = inner_of(step)
    base = acc.shape[0] // 2
    for send in sends:
        send[...] = acc[base : base + send.shape[0]].astype(send.dtype)
        base += send.shape[0]


def tiles(pieces, src_row, dst_row, table, first, second, acc, parts, send_dtype, name):
    count, rank, width = first.shape
    blocks, probes, _ = acc.shape
    rows = sum(piece.shape[0] for piece in pieces)

    def body(*refs):
        tiles_body(len(pieces), src_row, dst_row, *refs)

    return local(
        body,
        [shape(acc.shape, F32)] + [shape((blocks // 2 // parts, probes, width), send_dtype)] * parts,
        table,
        acc,
        *pieces,
        first,
        second,
        name=name,
        specs=[whole(pltpu.SMEM)] + [whole()] * (len(pieces) + 3),
        aliases={1: 0},
        flops=4 * count * rank * width * probes * GROUP,
        scratch=2 * rows * probes * width,
        scratches=[pltpu.VMEM((rows, probes, width), BF16)],
    )


def place(relative, order):
    at = jnp.zeros_like(relative)
    for k, bit in enumerate(order):
        at = at + jnp.where((relative & bit) != 0, 1 << k, 0)
    return at


def plan(owners, weight, orders, cell_blocks, station_blocks, after):
    peers, count = owners[0].shape
    rows = weight.shape[0] // peers
    rest = peers // 8
    half = cell_blocks // 2

    def body(*refs):
        far, weight_far, table_out, weight_near = refs[:5], refs[5], refs[6], refs[7]
        near, table, sems = refs[8:13], refs[13], refs[14]
        me = lax.axis_index("tile")
        pairs = list(zip(far, near))
        for k in range(rest):
            start = pl.multiple_of((k * 8 + (me & 7)) * rows, rows)
            pairs.append((weight_far.at[pl.ds(start, rows)], weight_near.at[pl.ds(k * rows, rows)]))
        fetch(pairs, sems)
        col_owner, col_local, row_owner, row_local, rank = [ref[pl.ds(me, 1), :] for ref in near]
        span = peers // 2
        away = col_owner ^ me
        is_q = col_local >= half
        spot = jnp.where(is_q, place(away, orders[1]) + (span - 1), place(away, orders[0]))
        table[0:1, :] = (away & 1) * (span * cell_blocks) + spot * half + col_local
        away = row_owner ^ me
        spot = (away & 1) * 4 + ((away & 4) // 2) + ((away & 2) // 2)
        table[1:2, :] = (spot * rest + row_owner // 8) * station_blocks + row_local
        table[2:3, :] = rank
        fetch([(table, table_out)], sems)

    return local(
        body,
        [shape((8, count), I32), shape((rest * rows, LANES), F32)],
        *owners,
        weight,
        name="plan",
        specs=[whole(pltpu.HBM)] * 6,
        out_specs=[whole(pltpu.SMEM), whole()],
        scratches=[pltpu.VMEM((peers, count), I32)] * 5
        + [pltpu.VMEM((8, count), I32), pltpu.SemaphoreType.DMA((5 + rest,))],
        after=after,
    )


def shards(
    probes,
    level_set,
    unit_label,
    contrast,
    station_weight,
    u_factor,
    v_factor,
    col_owner,
    col_local,
    row_owner,
    row_local,
    tile_rank,
):
    peers = lax.axis_size("tile")
    tile_count, _, station_width = u_factor.shape
    cell_width = v_factor.shape[2]
    probe_count, cell_total = probes.shape
    cell_blocks = cell_total // cell_width
    station_blocks = station_weight.shape[0] // (peers * station_width)
    bits = [1 << k for k in range(1, peers.bit_length() - 1)]
    far = bits[:0:-1]
    orders = (bits[:1] + far, far + bits[:1])

    lanes = (cell_total // LANES, LANES)
    half_dims = (cell_blocks // 2, probe_count, cell_width)
    part_p, part_q, scaling = local(
        scale_body,
        [shape(half_dims, BF16), shape(half_dims, BF16), shape(lanes, F32)],
        contrast,
        level_set.reshape(lanes),
        unit_label.reshape(lanes),
        probes,
        name="scale",
        specs=[whole(pltpu.HBM)] * 4,
        scratches=[
            pltpu.SMEM(contrast.shape, F32),
            pltpu.VMEM(lanes, F32),
            pltpu.VMEM(lanes, I32),
            pltpu.VMEM(probes.shape, F32),
            pltpu.SemaphoreType.DMA((4,)),
        ],
    )
    table, weight = plan(
        [a.reshape(peers, tile_count) for a in (col_owner, col_local, row_owner, row_local, tile_rank)],
        station_weight.reshape(-1, LANES),
        orders,
        cell_blocks,
        station_blocks,
        (scaling,),
    )
    steps = list(zip(*orders))
    after = (weight,)
    for step, (bit_p, bit_q) in enumerate(steps):
        got_p = swap(part_p, bit_p)
        got_q = swap(part_q, bit_q)
        if step == 1:
            v_here = load(v_factor, (part_p, part_q), "load_v")
            u_here = load(u_factor, (part_p, part_q, v_here), "load_u")
            after = (u_here,)
        if step < len(steps) - 1:
            part_p = join(part_p, got_p, after=after)
            part_q = join(part_q, got_q)
            after = ()
    pieces = [part_p, got_p, part_q, got_q]
    pieces = pieces + [swap(piece, 1) for piece in pieces]

    acc = zeros((peers * station_blocks, probe_count, station_width), (part_p, part_q))
    total, *sends = tiles(pieces, 0, 1, table, v_here, u_here, acc, 4, F32, "forward")
    quarters = [0] * 4
    for k in SQUARE + (0,):
        kept = F32 if k == 0 else BF16
        quarters[k // 2] = fold(total, swap(sends[k // 2], 1), (kept,), base=k // 2 * sends[0].shape[0])[0]
    total, send = plus(quarters[0], *[swap(quarters[k // 2], k) for k in SQUARE])
    for bit in bits[2:-1]:
        total, send = plus(total, swap(send, bit))
    weighted = weigh(total, swap(send, bits[-1]), weight)
    gots = {k: swap(weighted, k) for k in SQUARE}
    around = join(gots[2], gots[4], gots[6])
    pieces = [weighted, around, swap(weighted, 1), swap(around, 1)]

    acc = zeros((peers * cell_blocks, probe_count, cell_width), (total,))
    total, send_p, send_q = tiles(pieces, 1, 0, table, u_here, v_here, acc, 2, BF16, "adjoint")
    keep_p, send_p = fold(total, swap(send_p, 1))
    keep_q, send_q = fold(total, swap(send_q, 1), base=total.shape[0] // 4)
    for step, (bit_p, bit_q) in enumerate(steps[::-1]):
        if step > 0:
            keep_p, send_p = fold(keep_p, got_p)
            keep_q, send_q = fold(keep_q, got_q)
        got_p = swap(send_p, bit_p)
        got_q = swap(send_q, bit_q)
    return local(
        final_body,
        [shape((probe_count, cell_total), F32)],
        keep_p,
        got_p,
        keep_q,
        got_q,
        scaling,
        name="final",
        out_specs=[whole(None)],
    )[0]


def solution(mesh):
    placed = (
        P(None, ("groups", "tile")),
        P(("groups", "tile")),
        P(("groups", "tile")),
        P("groups"),
        P("groups"),
        P(("groups", "tile"), None, None),
        P(("groups", "tile"), None, None),
        P("groups", None),
        P("groups"),
        P("groups", None),
        P("groups"),
        P("groups"),
    )
    return jax.shard_map(
        shards, mesh=mesh, in_specs=placed, out_specs=P(None, ("groups", "tile")), check_vma=False
    )
```

```python
import math

import jax
import jax.numpy as jnp
from jax import lax
from jax.experimental import pallas as pl
from jax.experimental.pallas import tpu as pltpu
from jax.sharding import PartitionSpec as P

BF16 = jnp.bfloat16
F32 = jnp.float32
I32 = jnp.int32
GROUP = 8
SKEW = 3
SQUARE = (6, 2, 4)
MORE = 1
LANES = 128
MIB = 1024 * 1024


def whole(space=pltpu.VMEM):
    return pl.BlockSpec(memory_space=space)


def shape(dims, dtype):
    return jax.ShapeDtypeStruct(tuple(dims), dtype)


def size_of(array):
    return math.prod(array.shape) * jnp.dtype(array.dtype).itemsize


def swap(array, bits):
    count = lax.axis_size("tile")
    return lax.ppermute(array, "tile", [(i, i ^ bits) for i in range(count)])


def local(
    body, outs, *ins, name, scratch=0, scratches=(), specs=None, out_specs=None, flops=0, after=(), aliases=None
):
    nbytes = sum(size_of(a) for a in (*ins, *outs))
    specs = list(specs or [whole()] * len(ins)) + [whole()] * len(after)
    out_specs = list(out_specs or [whole()] * len(outs))
    own = len(ins)
    ins = [pltpu.with_memory_space_constraint(a, s.memory_space) for a, s in zip((*ins, *after), specs)]

    def run(*refs):
        body(*refs[:own], *refs[len(ins) :])

    return pl.pallas_call(
        run,
        out_shape=[a if s.memory_space is None else s.memory_space(a.shape, a.dtype) for a, s in zip(outs, out_specs)],
        in_specs=specs,
        out_specs=[whole() if s.memory_space is None else s for s in out_specs],
        input_output_aliases=aliases or {},
        scratch_shapes=list(scratches),
        compiler_params=pltpu.CompilerParams(vmem_limit_bytes=scratch + 8 * MIB),
        cost_estimate=pl.CostEstimate(flops=flops, bytes_accessed=nbytes, transcendentals=0),
        name=name,
    )(*ins)


def fetch(pairs, sems):
    copies = [pltpu.make_async_copy(a, b, sems.at[i]) for i, (a, b) in enumerate(pairs)]
    for copy in copies:
        copy.start()
    for copy in copies:
        copy.wait()


def load_body(source, out, sems):
    n = source.shape[0] // sems.shape[0]
    rows = [pl.ds(i * n, n) for i in range(sems.shape[0])]
    fetch([(source.at[r], out.at[r]) for r in rows], sems)


def load(array, after, name):
    return local(
        load_body,
        [shape(array.shape, array.dtype)],
        array,
        name=name,
        specs=[whole(pltpu.HBM)],
        scratches=[pltpu.SemaphoreType.DMA((8,))],
        after=after,
    )[0]


def scale_body(
    contrast, level, label, probes, part_p, part_q, scaling, contrast_near, level_near, label_near, probes_near, sems
):
    fetch(
        [(contrast, contrast_near), (level, level_near), (label, label_near), (probes, probes_near)],
        sems,
    )
    value = level_near[...]
    unit = label_near[...]
    factor = jnp.zeros_like(value)
    for k in range(contrast.shape[0]):
        factor = jnp.where(unit == k, contrast_near[k], factor)
    scaling[...] = factor / (1.0 + value * value)
    rows = part_p.shape[2] // LANES
    for first, part in ((0, part_p), (part_p.shape[0], part_q)):
        for b in range(part.shape[0]):
            for c in range(rows):
                j = (first + b) * rows + c
                piece = probes_near[:, j * LANES : (j + 1) * LANES] * scaling[j : j + 1, :]
                part[b, :, c * LANES : (c + 1) * LANES] = piece.astype(BF16)


def final_body(keep_p, recv_p, keep_q, recv_q, scaling, out):
    rows = keep_p.shape[2] // LANES
    for first, keep, recv in ((0, keep_p, recv_p), (keep_p.shape[0], keep_q, recv_q)):
        for b in range(keep.shape[0]):
            for c in range(rows):
                j = (first + b) * rows + c
                lanes = slice(c * LANES, (c + 1) * LANES)
                total = keep[b, :, lanes] + recv[b, :, lanes].astype(F32)
                out[:, j * LANES : (j + 1) * LANES] = total * scaling[j : j + 1, :]


def join_body(*refs):
    out, at = refs[-1], 0
    for ref in refs[:-1]:
        out[at : at + ref.shape[0]] = ref[...]
        at += ref.shape[0]


def join(*pieces, after=()):
    out = shape((sum(a.shape[0] for a in pieces),) + pieces[0].shape[1:], pieces[0].dtype)
    return local(join_body, [out], *pieces, name="join", after=after)[0]


def plus(total, *gots):
    def body(total, *refs):
        done = total[...]
        for ref in refs[:-2]:
            done = done + ref[...].astype(F32)
        refs[-2][...] = done
        refs[-1][...] = done.astype(BF16)

    return local(body, [shape(total.shape, F32), shape(total.shape, BF16)], total, *gots, name="plus")


def weigh(total, got, weight):
    def body(total, got, weight, out):
        blocks, _, width = out.shape
        rows = width // LANES
        for b in range(blocks):
            for c in range(rows):
                lanes = slice(c * LANES, (c + 1) * LANES)
                done = total[b, :, lanes] + got[b, :, lanes].astype(F32)
                j = b * rows + c
                out[b, :, lanes] = (done * weight[j : j + 1, :]).astype(BF16)

    return local(body, [shape(total.shape, BF16)], total, got, weight, name="weigh")[0]


def fold(keep, recv, dtypes=(F32, BF16), base=0):
    n = recv.shape[0] // len(dtypes)

    def body(keep, recv, *outs):
        for i, out in enumerate(outs):
            mine = keep[base + i * n : base + (i + 1) * n]
            out[...] = (mine + recv[i * n : (i + 1) * n].astype(F32)).astype(out.dtype)

    return local(body, [shape((n,) + keep.shape[1:], t) for t in dtypes], keep, recv, name="fold")


def zeros(dims, after):
    def body(out):
        out[...] = jnp.zeros_like(out)

    return local(body, [shape(dims, F32)], name="zeros", after=after)[0]


def tiles_body(piece_count, src_row, dst_row, at, _, *refs):
    pieces = refs[:piece_count]
    first, second, acc, *sends, table = refs[piece_count:]
    count, rank, width = first.shape
    groups = count // GROUP
    join_body(*pieces, table)
    probes = table.shape[1]
    span = GROUP * rank
    row_tile = lax.broadcasted_iota(I32, (GROUP * probes, span), 0) // probes
    col_tile = lax.broadcasted_iota(I32, (GROUP * probes, span), 1) // rank
    component = lax.broadcasted_iota(I32, (GROUP * probes, span), 1) % rank
    own = jnp.where(row_tile == col_tile, component, rank)
    lane_tile = lax.broadcasted_iota(I32, (1, span), 1) // rank

    def inner_of(g):
        taken = jnp.concatenate(
            [table[at[src_row, g * GROUP + i]].astype(F32) for i in range(GROUP)], axis=0
        ).astype(BF16)
        left = first[g * GROUP : (g + 1) * GROUP].reshape(span, width)
        inner = lax.dot_general(taken, left, (((1,), (1,)), ((), ())), preferred_element_type=F32)
        limit = jnp.zeros((1, span), I32)
        for i in range(GROUP):
            limit = jnp.where(lane_tile == i, at[2, g * GROUP + i], limit)
        return jnp.where(own < limit, inner, 0.0).astype(BF16)

    def outer_of(g, kept):
        right = second[g * GROUP : (g + 1) * GROUP].reshape(span, width)
        return jnp.dot(kept, right, preferred_element_type=F32)

    def add(g, outer):
        for i in range(GROUP):
            to = at[dst_row, g * GROUP + i]
            acc[to] = acc[to] + outer[i * probes : (i + 1) * probes]

    kept, outer = {}, {}
    for step in range(groups + 2 * SKEW):
        if step >= 2 * SKEW:
            add(step - 2 * SKEW, outer.pop(step - 2 * SKEW))
        if 0 <= step - SKEW < groups:
            outer[step - SKEW] = outer_of(step - SKEW, kept.pop(step - SKEW))
        if step < groups:
            kept[step] = inner_of(step)
    base = acc.shape[0] // 2
    for send in sends:
        send[...] = acc[base : base + send.shape[0]].astype(send.dtype)
        base += send.shape[0]


def tiles(pieces, src_row, dst_row, table, first, second, acc, parts, send_dtype, name):
    count, rank, width = first.shape
    probes = acc.shape[1]
    rows = sum(piece.shape[0] for piece in pieces)

    def body(*refs):
        tiles_body(len(pieces), src_row, dst_row, *refs)

    return local(
        body,
        [shape(acc.shape, F32)] + [shape((n, probes, width), send_dtype) for n in parts],
        table,
        acc,
        *pieces,
        first,
        second,
        name=name,
        specs=[whole(pltpu.SMEM)] + [whole()] * (len(pieces) + 3),
        aliases={1: 0},
        flops=4 * count * rank * width * probes * GROUP,
        scratch=2 * rows * probes * width,
        scratches=[pltpu.VMEM((rows, probes, width), BF16)],
    )


def place(relative, order):
    at = jnp.zeros_like(relative)
    for k, bit in enumerate(order):
        at = at + jnp.where((relative & bit) != 0, 1 << k, 0)
    return at


def plan(owners, weight, orders, cell_blocks, station_blocks, after):
    peers, count = owners[0].shape
    rows = weight.shape[0] // peers
    rest = peers // 8
    ahead = cell_blocks // 2 + MORE

    def body(*refs):
        far, weight_far, table_out, weight_near = refs[:5], refs[5], refs[6], refs[7]
        near, table, sems = refs[8:13], refs[13], refs[14]
        me = lax.axis_index("tile")
        pairs = list(zip(far, near))
        for k in range(rest):
            start = pl.multiple_of((k * 8 + (me & 7)) * rows, rows)
            pairs.append((weight_far.at[pl.ds(start, rows)], weight_near.at[pl.ds(k * rows, rows)]))
        fetch(pairs, sems)
        col_owner, col_local, row_owner, row_local, rank = [ref[pl.ds(me, 1), :] for ref in near]
        span = peers // 2
        away = col_owner ^ me
        in_p = place(away, orders[0]) * ahead + col_local
        in_q = place(away, orders[1]) * (cell_blocks - ahead) + (col_local + (span - 1) * ahead)
        table[0:1, :] = (away & 1) * (span * cell_blocks) + jnp.where(col_local >= ahead, in_q, in_p)
        away = row_owner ^ me
        spot = (away & 1) * 4 + ((away & 4) // 2) + ((away & 2) // 2)
        table[1:2, :] = (spot * rest + row_owner // 8) * station_blocks + row_local
        table[2:3, :] = rank
        fetch([(table, table_out)], sems)

    return local(
        body,
        [shape((8, count), I32), shape((rest * rows, LANES), F32)],
        *owners,
        weight,
        name="plan",
        specs=[whole(pltpu.HBM)] * 6,
        out_specs=[whole(pltpu.SMEM), whole()],
        scratches=[pltpu.VMEM((peers, count), I32)] * 5
        + [pltpu.VMEM((8, count), I32), pltpu.SemaphoreType.DMA((5 + rest,))],
        after=after,
    )


def shards(
    probes,
    level_set,
    unit_label,
    contrast,
    station_weight,
    u_factor,
    v_factor,
    col_owner,
    col_local,
    row_owner,
    row_local,
    tile_rank,
):
    peers = lax.axis_size("tile")
    tile_count, _, station_width = u_factor.shape
    cell_width = v_factor.shape[2]
    probe_count, cell_total = probes.shape
    cell_blocks = cell_total // cell_width
    station_blocks = station_weight.shape[0] // (peers * station_width)
    bits = [1 << k for k in range(1, peers.bit_length() - 1)]
    far = bits[:0:-1]
    orders = (bits[:1] + far, far + bits[:1])

    lanes = (cell_total // LANES, LANES)
    ahead = cell_blocks // 2 + MORE
    behind = cell_blocks - ahead
    part_p, part_q, scaling = local(
        scale_body,
        [shape((n, probe_count, cell_width), BF16) for n in (ahead, behind)] + [shape(lanes, F32)],
        contrast,
        level_set.reshape(lanes),
        unit_label.reshape(lanes),
        probes,
        name="scale",
        specs=[whole(pltpu.HBM)] * 4,
        scratches=[
            pltpu.SMEM(contrast.shape, F32),
            pltpu.VMEM(lanes, F32),
            pltpu.VMEM(lanes, I32),
            pltpu.VMEM(probes.shape, F32),
            pltpu.SemaphoreType.DMA((4,)),
        ],
    )
    table, weight = plan(
        [a.reshape(peers, tile_count) for a in (col_owner, col_local, row_owner, row_local, tile_rank)],
        station_weight.reshape(-1, LANES),
        orders,
        cell_blocks,
        station_blocks,
        (scaling,),
    )
    steps = list(zip(*orders))
    after = (weight,)
    for step, (bit_p, bit_q) in enumerate(steps):
        got_p = swap(part_p, bit_p)
        got_q = swap(part_q, bit_q)
        if step == 1:
            v_here = load(v_factor, (part_p, part_q), "load_v")
            u_here = load(u_factor, (part_p, part_q, v_here), "load_u")
            after = (u_here,)
        if step < len(steps) - 1:
            part_p = join(part_p, got_p, after=after)
            part_q = join(part_q, got_q)
            after = ()
    pieces = [part_p, got_p, part_q, got_q]
    pieces = pieces + [swap(piece, 1) for piece in pieces]

    len_quarter = peers * station_blocks // 8
    acc = zeros((peers * station_blocks, probe_count, station_width), (part_p, part_q))
    total, *sends = tiles(pieces, 0, 1, table, v_here, u_here, acc, [len_quarter] * 4, F32, "forward")
    quarters = [0] * 4
    for k in SQUARE + (0,):
        kept = F32 if k == 0 else BF16
        quarters[k // 2] = fold(total, swap(sends[k // 2], 1), (kept,), base=k // 2 * len_quarter)[0]
    total, send = plus(quarters[0], *[swap(quarters[k // 2], k) for k in SQUARE])
    for bit in bits[2:-1]:
        total, send = plus(total, swap(send, bit))
    weighted = weigh(total, swap(send, bits[-1]), weight)
    gots = {k: swap(weighted, k) for k in SQUARE}
    pieces = [weighted, gots[2], gots[4], gots[6]]
    pieces = pieces + [swap(piece, 1) for piece in pieces]

    acc = zeros((peers * cell_blocks, probe_count, cell_width), (total,))
    total, send_p, send_q = tiles(pieces, 1, 0, table, u_here, v_here, acc, [n * peers // 2 for n in (ahead, behind)], BF16, "adjoint")
    keep_p, send_p = fold(total, swap(send_p, 1))
    keep_q, send_q = fold(total, swap(send_q, 1), base=ahead * peers // 2)
    for step, (bit_p, bit_q) in enumerate(steps[::-1]):
        if step > 0:
            keep_p, send_p = fold(keep_p, got_p)
            keep_q, send_q = fold(keep_q, got_q)
        got_p = swap(send_p, bit_p)
        got_q = swap(send_q, bit_q)
    return local(
        final_body,
        [shape((probe_count, cell_total), F32)],
        keep_p,
        got_p,
        keep_q,
        got_q,
        scaling,
        name="final",
        out_specs=[whole(None)],
    )[0]


def solution(mesh):
    placed = (
        P(None, ("groups", "tile")),
        P(("groups", "tile")),
        P(("groups", "tile")),
        P("groups"),
        P("groups"),
        P(("groups", "tile"), None, None),
        P(("groups", "tile"), None, None),
        P("groups", None),
        P("groups"),
        P("groups", None),
        P("groups"),
        P("groups"),
    )
    return jax.shard_map(
        shards, mesh=mesh, in_specs=placed, out_specs=P(None, ("groups", "tile")), check_vma=False
    )
```

```python
import math

import jax
import jax.numpy as jnp
from jax import lax
from jax.experimental import pallas as pl
from jax.experimental.pallas import tpu as pltpu
from jax.sharding import PartitionSpec as P

BF16 = jnp.bfloat16
F32 = jnp.float32
I32 = jnp.int32
GROUP = 8
SKEW = 3
SQUARE = (6, 2, 4)
LANES = 128
MIB = 1024 * 1024


def whole(space=pltpu.VMEM):
    return pl.BlockSpec(memory_space=space)


def shape(dims, dtype):
    return jax.ShapeDtypeStruct(tuple(dims), dtype)


def size_of(array):
    return math.prod(array.shape) * jnp.dtype(array.dtype).itemsize


def swap(array, bits):
    count = lax.axis_size("tile")
    return lax.ppermute(array, "tile", [(i, i ^ bits) for i in range(count)])


def local(
    body, outs, *ins, name, scratch=0, scratches=(), specs=None, out_specs=None, flops=0, after=(), aliases=None
):
    nbytes = sum(size_of(a) for a in (*ins, *outs))
    specs = list(specs or [whole()] * len(ins)) + [whole()] * len(after)
    out_specs = list(out_specs or [whole()] * len(outs))
    own = len(ins)
    ins = [pltpu.with_memory_space_constraint(a, s.memory_space) for a, s in zip((*ins, *after), specs)]

    def run(*refs):
        body(*refs[:own], *refs[len(ins) :])

    return pl.pallas_call(
        run,
        out_shape=[a if s.memory_space is None else s.memory_space(a.shape, a.dtype) for a, s in zip(outs, out_specs)],
        in_specs=specs,
        out_specs=[whole() if s.memory_space is None else s for s in out_specs],
        input_output_aliases=aliases or {},
        scratch_shapes=list(scratches),
        compiler_params=pltpu.CompilerParams(vmem_limit_bytes=scratch + 8 * MIB),
        cost_estimate=pl.CostEstimate(flops=flops, bytes_accessed=nbytes, transcendentals=0),
        name=name,
    )(*ins)


def fetch(pairs, sems):
    copies = [pltpu.make_async_copy(a, b, sems.at[i]) for i, (a, b) in enumerate(pairs)]
    for copy in copies:
        copy.start()
    for copy in copies:
        copy.wait()


def load(array, after, name):
    count, rank, width = array.shape
    half = width // 2
    pieces = 4
    n = count // pieces

    def body(source, mine, other, sems):
        core = lax.axis_index("tile") & 1
        pairs = []
        for out, which in ((other, 1 - core), (mine, core)):
            lanes = pl.ds(pl.multiple_of(which * half, half), half)
            for i in range(pieces):
                rows = pl.ds(i * n, n)
                pairs.append((source.at[rows, :, lanes], out.at[rows]))
        fetch(pairs, sems)

    return local(
        body,
        [shape((count, rank, half), array.dtype)] * 2,
        array,
        name=name,
        specs=[whole(pltpu.HBM)],
        scratches=[pltpu.SemaphoreType.DMA((2 * pieces,))],
        after=after,
    )


def scale_body(contrast, level, label, probes, mine, other, scaling, contrast_near, level_near, label_near, probes_near, sems):
    fetch(
        [(contrast, contrast_near), (level, level_near), (label, label_near), (probes, probes_near)],
        sems,
    )
    odd = (lax.axis_index("tile") & 1) != 0
    value = level_near[...]
    unit = label_near[...]
    factor = jnp.zeros_like(value)
    for k in range(contrast.shape[0]):
        factor = jnp.where(unit == k, contrast_near[k], factor)
    scaling[...] = factor / (1.0 + value * value)
    blocks, _, half = mine.shape
    rows = half // LANES
    for b in range(blocks):
        for c in range(rows):
            low, high = [
                probes_near[:, j * LANES : (j + 1) * LANES] * scaling[j : j + 1, :]
                for j in (2 * b * rows + c, (2 * b + 1) * rows + c)
            ]
            lanes = slice(c * LANES, (c + 1) * LANES)
            mine[b, :, lanes] = jnp.where(odd, high, low).astype(BF16)
            other[b, :, lanes] = jnp.where(odd, low, high).astype(BF16)


def final_body(keep, recv, other, scaling, out):
    odd = (lax.axis_index("tile") & 1) != 0
    blocks, _, half = other.shape
    rows = half // LANES
    for b in range(blocks):
        for c in range(rows):
            lanes = slice(c * LANES, (c + 1) * LANES)
            own = keep[b, :, lanes] + recv[b, :, lanes].astype(F32)
            got = other[b, :, lanes]
            for j, total in (
                (2 * b * rows + c, jnp.where(odd, got, own)),
                ((2 * b + 1) * rows + c, jnp.where(odd, own, got)),
            ):
                out[:, j * LANES : (j + 1) * LANES] = total * scaling[j : j + 1, :]


def join_body(*refs):
    out, at = refs[-1], 0
    for ref in refs[:-1]:
        out[at : at + ref.shape[0]] = ref[...]
        at += ref.shape[0]


def join(*pieces, after=()):
    out = shape((sum(a.shape[0] for a in pieces),) + pieces[0].shape[1:], pieces[0].dtype)
    return local(join_body, [out], *pieces, name="join", after=after)[0]


def plus(total, *gots):
    dims = gots[0].shape

    def body(total, *refs):
        done = total[: dims[0]]
        for ref in refs[:-2]:
            done = done + ref[...].astype(F32)
        refs[-2][...] = done
        refs[-1][...] = done.astype(BF16)

    return local(body, [shape(dims, F32), shape(dims, BF16)], total, *gots, name="plus")


def weigh(total, got, weight):
    def body(total, got, weight, out):
        core = lax.axis_index("tile") & 1
        blocks, _, half = out.shape
        rows = half // LANES
        for b in range(blocks):
            for c in range(rows):
                lanes = slice(c * LANES, (c + 1) * LANES)
                done = total[b, :, lanes] + got[b, :, lanes].astype(F32)
                row = weight[pl.ds((2 * b + core) * rows + c, 1), :]
                out[b, :, lanes] = (done * row).astype(BF16)

    return local(body, [shape(total.shape, BF16)], total, got, weight, name="weigh")[0]


def fold(keep, recv, dtypes=(F32, BF16), base=0):
    n = recv.shape[0] // len(dtypes)
    outs = [shape((n,) + keep.shape[1:], t) for t in dtypes]

    def body(keep, recv, *outs):
        for i, out in enumerate(outs):
            mine = keep[base + i * n : base + (i + 1) * n]
            out[...] = (mine + recv[i * n : (i + 1) * n].astype(F32)).astype(out.dtype)

    return local(body, outs, keep, recv, name="fold")


def zeros(dims, after):
    def body(out):
        out[...] = jnp.zeros_like(out)

    return local(body, [shape(dims, F32)], name="zeros", after=after)[0]


def own_mask(rank, probes):
    dims = (GROUP * probes, GROUP * rank)
    rows = lax.broadcasted_iota(I32, dims, 0) // probes
    columns = lax.broadcasted_iota(I32, dims, 1)
    return jnp.where(rows == columns // rank, columns % rank, rank)


def skewed(groups, *stages):
    held = {}
    last = SKEW * (len(stages) - 1)
    for step in range(groups + last):
        for k in range(len(stages) - 1, -1, -1):
            g = step - k * SKEW
            if 0 <= g < groups:
                held[g] = stages[k](g, held.get(g))
                if k == len(stages) - 1:
                    del held[g]


def shrink(pieces, at_rows, table, factors, name):
    count, rank, half = factors[0].shape
    probes = pieces[0].shape[1]
    groups = count // GROUP
    span = GROUP * rank
    rows = sum(piece.shape[0] for piece in pieces)

    def body(at, *refs):
        mine, other, out, near = refs[len(pieces) :]
        join_body(*refs[: len(pieces)], near)
        own = own_mask(rank, probes)
        lane_tile = lax.broadcasted_iota(I32, (1, span), 1) // rank

        def dots(g, _):
            row, first = at_rows[g // groups], (g % groups) * GROUP
            taken = jnp.concatenate([near[at[row, first + i]].astype(F32) for i in range(GROUP)], axis=0)
            factor = (mine, other)[g // groups][first : first + GROUP].reshape(span, half)
            return lax.dot_general(
                taken.astype(BF16), factor, (((1,), (1,)), ((), ())), preferred_element_type=F32
            )

        def store(g, inner):
            row, first = 4 + g // groups, (g % groups) * GROUP
            limit = jnp.zeros((1, span), I32)
            for i in range(GROUP):
                limit = jnp.where(lane_tile == i, at[row, first + i], limit)
            inner = jnp.where(own < limit, inner, 0.0)
            out[g] = sum(inner[i * probes : (i + 1) * probes] for i in range(GROUP))

        skewed(2 * groups, dots, store)

    return local(
        body,
        [shape((2 * groups, probes, span), F32)],
        table,
        *pieces,
        *factors,
        name=name,
        specs=[whole(pltpu.SMEM)] + [whole()] * (len(pieces) + 2),
        flops=4 * count * rank * half * probes * GROUP,
        scratch=2 * rows * probes * half,
        scratches=[pltpu.VMEM((rows, probes, half), BF16)],
    )[0]


def expand(mine_sum, other_sum, at_rows, table, factors, acc, sends, name):
    count, rank, half = factors[0].shape
    probes = acc.shape[1]
    groups = count // GROUP
    span = GROUP * rank

    def body(at, _, sums, got, mine, other, out, *parts):
        own = own_mask(rank, probes) < rank

        def dots(g, _):
            total = sums[g] + got[(g + groups) % (2 * groups)]
            total = jnp.concatenate([total.astype(BF16).astype(F32)] * GROUP, axis=0)
            total = jnp.where(own, total, 0.0).astype(BF16)
            first = (g % groups) * GROUP
            factor = (mine, other)[g // groups][first : first + GROUP].reshape(span, half)
            return jnp.dot(total, factor, preferred_element_type=F32)

        def add(g, outer):
            row, first = at_rows[g // groups], (g % groups) * GROUP
            for i in range(GROUP):
                to = at[row, first + i]
                out[to] = out[to] + outer[i * probes : (i + 1) * probes]

        skewed(2 * groups, dots, add)
        for part, (start, size) in zip(parts, sends):
            part[...] = out[start : start + size].astype(BF16)

    return local(
        body,
        [shape(acc.shape, F32)] + [shape((size, probes, half), BF16) for _, size in sends],
        table,
        acc,
        mine_sum,
        other_sum,
        *factors,
        name=name,
        specs=[whole(pltpu.SMEM)] + [whole()] * 5,
        aliases={1: 0},
        flops=4 * count * rank * half * probes * GROUP,
    )


def place(relative, order):
    at = jnp.zeros_like(relative)
    for k, bit in enumerate(order):
        at = at + jnp.where((relative & bit) != 0, 1 << k, 0)
    return at


def plan(owners, weight, orders, cell_blocks, station_blocks, after):
    peers, count = owners[0].shape
    rows = 2 * (weight.shape[0] // peers)
    rest = peers // 8

    def body(*refs):
        far, weight_far, table_out, weight_near = refs[:5], refs[5], refs[6], refs[7]
        near, table, sems = refs[8:13], refs[13], refs[14]
        me = lax.axis_index("tile")
        pairs = list(zip(far, near))
        for k in range(rest):
            start = pl.multiple_of((k * 4 + (me & 6) // 2) * rows, rows)
            pairs.append((weight_far.at[pl.ds(start, rows)], weight_near.at[pl.ds(k * rows, rows)]))
        fetch(pairs, sems)
        span = peers // 2
        for k, holder in enumerate((me, me ^ 1)):
            col_owner, col_local, row_owner, row_local, rank = [ref[pl.ds(holder, 1), :] for ref in near]
            away = col_owner ^ me
            spot = jnp.where((away & 1) != 0, span + place(away, orders[1]), place(away, orders[0]))
            table[k : k + 1, :] = spot * cell_blocks + col_local
            away = row_owner ^ me
            spot = (((away & 6) // 2) * rest + row_owner // 8) * 2 + (row_owner & 1)
            table[k + 2 : k + 3, :] = spot * station_blocks + row_local
            table[k + 4 : k + 5, :] = rank
        fetch([(table, table_out)], sems)

    return local(
        body,
        [shape((8, count), I32), shape((rest * rows, LANES), F32)],
        *owners,
        weight,
        name="plan",
        specs=[whole(pltpu.HBM)] * 6,
        out_specs=[whole(pltpu.SMEM), whole()],
        scratches=[pltpu.VMEM((peers, count), I32)] * 5
        + [pltpu.VMEM((8, count), I32), pltpu.SemaphoreType.DMA((5 + rest,))],
        after=after,
    )


def shards(
    probes,
    level_set,
    unit_label,
    contrast,
    station_weight,
    u_factor,
    v_factor,
    col_owner,
    col_local,
    row_owner,
    row_local,
    tile_rank,
):
    peers = lax.axis_size("tile")
    tile_count, _, station_width = u_factor.shape
    cell_width = v_factor.shape[2]
    probe_count, cell_total = probes.shape
    cell_blocks = cell_total // cell_width
    station_blocks = station_weight.shape[0] // (peers * station_width)
    bits = [1 << k for k in range(1, peers.bit_length() - 1)]
    far = bits[:0:-1]
    orders = (far + bits[:1], bits[:1] + far)

    lanes = (cell_total // LANES, LANES)
    half_dims = (cell_blocks, probe_count, cell_width // 2)
    part_p, send, scaling = local(
        scale_body,
        [shape(half_dims, BF16), shape(half_dims, BF16), shape(lanes, F32)],
        contrast,
        level_set.reshape(lanes),
        unit_label.reshape(lanes),
        probes,
        name="scale",
        specs=[whole(pltpu.HBM)] * 4,
        scratches=[
            pltpu.SMEM(contrast.shape, F32),
            pltpu.VMEM(lanes, F32),
            pltpu.VMEM(lanes, I32),
            pltpu.VMEM(probes.shape, F32),
            pltpu.SemaphoreType.DMA((4,)),
        ],
    )
    part_q = swap(send, 1)
    table, weight = plan(
        [a.reshape(peers, tile_count) for a in (col_owner, col_local, row_owner, row_local, tile_rank)],
        station_weight.reshape(-1, LANES),
        orders,
        cell_blocks,
        station_blocks,
        (scaling,),
    )
    steps = list(zip(*orders))
    after = (weight,)
    for step, (bit_p, bit_q) in enumerate(steps):
        got_p = swap(part_p, bit_p)
        got_q = swap(part_q, bit_q)
        if step == 1:
            v_here, v_send = load(v_factor, (part_p, part_q), "load_v")
            u_here, u_send = load(u_factor, (part_p, part_q, v_here), "load_u")
            after = (u_here,)
        if step < len(steps) - 1:
            part_p = join(part_p, got_p, after=after)
            part_q = join(part_q, got_q)
            after = ()
    v_both = (v_here, swap(v_send, 1))
    u_both = (u_here, swap(u_send, 1))

    stations = peers * station_blocks
    acc = zeros((stations, probe_count, station_width // 2), (part_p, part_q))
    coeff = shrink([part_p, got_p, part_q, got_q], (0, 1), table, v_both, "coeff")
    quarter = stations // 4
    total, *sends = expand(
        coeff,
        swap(coeff, 1),
        (2, 3),
        table,
        u_both,
        acc,
        [(k // 2 * quarter, quarter) for k in SQUARE],
        "partial",
    )
    total, send = plus(total, *[swap(send, k) for k, send in zip(SQUARE, sends)])
    for bit in bits[2:-1]:
        total, send = plus(total, swap(send, bit))
    weighted = weigh(total, swap(send, bits[-1]), weight)
    gots = {k: swap(weighted, k) for k in SQUARE}

    cells = peers * cell_blocks
    acc = zeros((cells, probe_count, cell_width // 2), (total,))
    back = shrink([weighted, gots[2], gots[4], gots[6]], (2, 3), table, u_both, "back")
    total, send_p, send_q = expand(
        back,
        swap(back, 1),
        (0, 1),
        table,
        v_both,
        acc,
        [(cells // 4, cells // 4), (3 * cells // 4, cells // 4)],
        "spread",
    )
    keep_p, keep_q, base = total, total, cells // 2
    for step, (bit_p, bit_q) in enumerate(steps[::-1]):
        got_p = swap(send_p, bit_p)
        got_q = swap(send_q, bit_q)
        if step < len(steps) - 1:
            keep_p, send_p = fold(keep_p, got_p)
            keep_q, send_q = fold(keep_q, got_q, base=base)
            base = 0
    other = fold(keep_q, got_q, (F32,))[0]
    return local(
        final_body,
        [shape((probe_count, cell_total), F32)],
        keep_p,
        got_p,
        swap(other, 1),
        scaling,
        name="final",
        out_specs=[whole(None)],
    )[0]


def solution(mesh):
    placed = (
        P(None, ("groups", "tile")),
        P(("groups", "tile")),
        P(("groups", "tile")),
        P("groups"),
        P("groups"),
        P(("groups", "tile"), None, None),
        P(("groups", "tile"), None, None),
        P("groups", None),
        P("groups"),
        P("groups", None),
        P("groups"),
        P("groups"),
    )
    return jax.shard_map(
        shards, mesh=mesh, in_specs=placed, out_specs=P(None, ("groups", "tile")), check_vma=False
    )
```

```python
import math

import jax
import jax.numpy as jnp
from jax import lax
from jax.experimental import pallas as pl
from jax.experimental.pallas import tpu as pltpu
from jax.sharding import PartitionSpec as P

BF16 = jnp.bfloat16
F32 = jnp.float32
I32 = jnp.int32
GROUP = 8
SKEW = 3
SQUARE = (6, 2, 4)
LANES = 128
MIB = 1024 * 1024


def whole(space=pltpu.VMEM):
    return pl.BlockSpec(memory_space=space)


def shape(dims, dtype):
    return jax.ShapeDtypeStruct(tuple(dims), dtype)


def size_of(array):
    return math.prod(array.shape) * jnp.dtype(array.dtype).itemsize


def swap(array, bits):
    count = lax.axis_size("tile")
    return lax.ppermute(array, "tile", [(i, i ^ bits) for i in range(count)])


def local(
    body, outs, *ins, name, scratch=0, scratches=(), specs=None, out_specs=None, flops=0, after=(), aliases=None
):
    nbytes = sum(size_of(a) for a in (*ins, *outs))
    specs = list(specs or [whole()] * len(ins)) + [whole()] * len(after)
    out_specs = list(out_specs or [whole()] * len(outs))
    own = len(ins)
    ins = [pltpu.with_memory_space_constraint(a, s.memory_space) for a, s in zip((*ins, *after), specs)]

    def run(*refs):
        body(*refs[:own], *refs[len(ins) :])

    return pl.pallas_call(
        run,
        out_shape=[a if s.memory_space is None else s.memory_space(a.shape, a.dtype) for a, s in zip(outs, out_specs)],
        in_specs=specs,
        out_specs=[whole() if s.memory_space is None else s for s in out_specs],
        input_output_aliases=aliases or {},
        scratch_shapes=list(scratches),
        compiler_params=pltpu.CompilerParams(vmem_limit_bytes=scratch + 8 * MIB),
        cost_estimate=pl.CostEstimate(flops=0, bytes_accessed=0, transcendentals=0),
        name=name,
    )(*ins)


def fetch(pairs, sems):
    copies = [pltpu.make_async_copy(a, b, sems.at[i]) for i, (a, b) in enumerate(pairs)]
    for copy in copies:
        copy.start()
    for copy in copies:
        copy.wait()


def load(array, after, name):
    count, rank, width = array.shape
    half = width // 2
    pieces = 4
    n = count // pieces

    def body(source, mine, other, sems):
        core = lax.axis_index("tile") & 1
        pairs = []
        for out, which in ((other, 1 - core), (mine, core)):
            lanes = pl.ds(pl.multiple_of(which * half, half), half)
            for i in range(pieces):
                rows = pl.ds(i * n, n)
                pairs.append((source.at[rows, :, lanes], out.at[rows]))
        fetch(pairs, sems)

    return local(
        body,
        [shape((count, rank, half), array.dtype)] * 2,
        array,
        name=name,
        specs=[whole(pltpu.HBM)],
        scratches=[pltpu.SemaphoreType.DMA((2 * pieces,))],
        after=after,
    )


def scale_body(contrast, level, label, probes, mine, other, scaling, contrast_near, level_near, label_near, probes_near, sems):
    fetch(
        [(contrast, contrast_near), (level, level_near), (label, label_near), (probes, probes_near)],
        sems,
    )
    odd = (lax.axis_index("tile") & 1) != 0
    value = level_near[...]
    unit = label_near[...]
    factor = jnp.zeros_like(value)
    for k in range(contrast.shape[0]):
        factor = jnp.where(unit == k, contrast_near[k], factor)
    scaling[...] = factor / (1.0 + value * value)
    blocks, _, half = mine.shape
    rows = half // LANES
    for b in range(blocks):
        for c in range(rows):
            low, high = [
                probes_near[:, j * LANES : (j + 1) * LANES] * scaling[j : j + 1, :]
                for j in (2 * b * rows + c, (2 * b + 1) * rows + c)
            ]
            lanes = slice(c * LANES, (c + 1) * LANES)
            mine[b, :, lanes] = jnp.where(odd, high, low).astype(BF16)
            other[b, :, lanes] = jnp.where(odd, low, high).astype(BF16)


def final_body(keep, recv, other_keep, other_recv, scaling, out):
    odd = (lax.axis_index("tile") & 1) != 0
    blocks, _, half = keep.shape
    rows = half // LANES
    for b in range(blocks):
        for c in range(rows):
            lanes = slice(c * LANES, (c + 1) * LANES)
            own = keep[b, :, lanes] + recv[b, :, lanes].astype(F32)
            got = other_keep[b, :, lanes] + other_recv[b, :, lanes].astype(F32)
            for j, total in (
                (2 * b * rows + c, jnp.where(odd, got, own)),
                ((2 * b + 1) * rows + c, jnp.where(odd, own, got)),
            ):
                out[:, j * LANES : (j + 1) * LANES] = total * scaling[j : j + 1, :]


def join_body(*refs):
    out, at = refs[-1], 0
    for ref in refs[:-1]:
        out[at : at + ref.shape[0]] = ref[...]
        at += ref.shape[0]


def join(*pieces, after=()):
    out = shape((sum(a.shape[0] for a in pieces),) + pieces[0].shape[1:], pieces[0].dtype)
    return local(join_body, [out], *pieces, name="join", after=after)[0]


def plus(total, *gots):
    dims = gots[0].shape

    def body(total, *refs):
        done = total[: dims[0]]
        for ref in refs[:-2]:
            done = done + ref[...].astype(F32)
        refs[-2][...] = done
        refs[-1][...] = done.astype(BF16)

    return local(body, [shape(dims, F32), shape(dims, BF16)], total, *gots, name="plus")


def weigh(total, got, weight):
    def body(total, got, weight, out):
        core = lax.axis_index("tile") & 1
        blocks, _, half = out.shape
        rows = half // LANES
        for b in range(blocks):
            for c in range(rows):
                lanes = slice(c * LANES, (c + 1) * LANES)
                done = total[b, :, lanes] + got[b, :, lanes].astype(F32)
                row = weight[pl.ds((2 * b + core) * rows + c, 1), :]
                out[b, :, lanes] = (done * row).astype(BF16)

    return local(body, [shape(total.shape, BF16)], total, got, weight, name="weigh")[0]


def fold(keep, recv, dtypes=(F32, BF16), base=0):
    n = recv.shape[0] // len(dtypes)
    outs = [shape((n,) + keep.shape[1:], t) for t in dtypes]

    def body(keep, recv, *outs):
        for i, out in enumerate(outs):
            mine = keep[base + i * n : base + (i + 1) * n]
            out[...] = (mine + recv[i * n : (i + 1) * n].astype(F32)).astype(out.dtype)

    return local(body, outs, keep, recv, name="fold")


def gate(arrays, after):
    def body(*refs):
        pass

    outs = [shape(a.shape, a.dtype) for a in arrays]
    return local(body, outs, *arrays, name="gate", after=after, aliases={i: i for i in range(len(arrays))})


def zeros(dims, after):
    def body(out):
        out[...] = jnp.zeros_like(out)

    return local(body, [shape(dims, F32)], name="zeros", after=after)[0]


def own_mask(rank, probes):
    dims = (GROUP * probes, GROUP * rank)
    rows = lax.broadcasted_iota(I32, dims, 0) // probes
    columns = lax.broadcasted_iota(I32, dims, 1)
    return jnp.where(rows == columns // rank, columns % rank, rank)


def skewed(groups, *stages):
    held = {}
    last = SKEW * (len(stages) - 1)
    for step in range(groups + last):
        for k in range(len(stages) - 1, -1, -1):
            g = step - k * SKEW
            if 0 <= g < groups:
                held[g] = stages[k](g, held.get(g))
                if k == len(stages) - 1:
                    del held[g]


def shrink(pieces, at_rows, table, factors, name):
    count, rank, half = factors[0].shape
    probes = pieces[0].shape[1]
    groups = count // GROUP
    span = GROUP * rank
    rows = sum(piece.shape[0] for piece in pieces)

    def body(at, *refs):
        mine, other, out, near = refs[len(pieces) :]
        join_body(*refs[: len(pieces)], near)
        own = own_mask(rank, probes)
        lane_tile = lax.broadcasted_iota(I32, (1, span), 1) // rank

        def dots(g, _):
            row, first = at_rows[g // groups], (g % groups) * GROUP
            taken = jnp.concatenate([near[at[row, first + i]].astype(F32) for i in range(GROUP)], axis=0)
            factor = (mine, other)[g // groups][first : first + GROUP].reshape(span, half)
            return lax.dot_general(
                taken.astype(BF16), factor, (((1,), (1,)), ((), ())), preferred_element_type=F32
            )

        def store(g, inner):
            row, first = 4 + g // groups, (g % groups) * GROUP
            limit = jnp.zeros((1, span), I32)
            for i in range(GROUP):
                limit = jnp.where(lane_tile == i, at[row, first + i], limit)
            inner = jnp.where(own < limit, inner, 0.0)
            out[g] = sum(inner[i * probes : (i + 1) * probes] for i in range(GROUP))

        skewed(2 * groups, dots, store)

    return local(
        body,
        [shape((2 * groups, probes, span), F32)],
        table,
        *pieces,
        *factors,
        name=name,
        specs=[whole(pltpu.SMEM)] + [whole()] * (len(pieces) + 2),
        flops=4 * count * rank * half * probes * GROUP,
        scratch=2 * rows * probes * half,
        scratches=[pltpu.VMEM((rows, probes, half), BF16)],
    )[0]


def expand(mine_sum, other_sum, at_rows, table, factors, acc, sends, name):
    count, rank, half = factors[0].shape
    probes = acc.shape[1]
    groups = count // GROUP
    span = GROUP * rank

    def body(at, _, sums, got, mine, other, out, *parts):
        own = own_mask(rank, probes) < rank

        def dots(g, _):
            total = sums[g] + got[(g + groups) % (2 * groups)]
            total = jnp.concatenate([total.astype(BF16).astype(F32)] * GROUP, axis=0)
            total = jnp.where(own, total, 0.0).astype(BF16)
            first = (g % groups) * GROUP
            factor = (mine, other)[g // groups][first : first + GROUP].reshape(span, half)
            return jnp.dot(total, factor, preferred_element_type=F32)

        def add(g, outer):
            row, first = at_rows[g // groups], (g % groups) * GROUP
            for i in range(GROUP):
                to = at[row, first + i]
                out[to] = out[to] + outer[i * probes : (i + 1) * probes]

        skewed(2 * groups, dots, add)
        for part, (start, size) in zip(parts, sends):
            part[...] = out[start : start + size].astype(BF16)

    return local(
        body,
        [shape(acc.shape, F32)] + [shape((size, probes, half), BF16) for _, size in sends],
        table,
        acc,
        mine_sum,
        other_sum,
        *factors,
        name=name,
        specs=[whole(pltpu.SMEM)] + [whole()] * 5,
        aliases={1: 0},
        flops=4 * count * rank * half * probes * GROUP,
    )


def place(relative, order):
    at = jnp.zeros_like(relative)
    for k, bit in enumerate(order):
        at = at + jnp.where((relative & bit) != 0, 1 << k, 0)
    return at


def plan(owners, weight, orders, cell_blocks, station_blocks, after):
    peers, count = owners[0].shape
    rows = 2 * (weight.shape[0] // peers)
    rest = peers // 8

    def body(*refs):
        far, weight_far, table_out, weight_near = refs[:5], refs[5], refs[6], refs[7]
        near, table, sems = refs[8:13], refs[13], refs[14]
        me = lax.axis_index("tile")
        pairs = list(zip(far, near))
        for k in range(rest):
            start = pl.multiple_of((k * 4 + (me & 6) // 2) * rows, rows)
            pairs.append((weight_far.at[pl.ds(start, rows)], weight_near.at[pl.ds(k * rows, rows)]))
        fetch(pairs, sems)
        span = peers // 2
        for k, holder in enumerate((me, me ^ 1)):
            col_owner, col_local, row_owner, row_local, rank = [ref[pl.ds(holder, 1), :] for ref in near]
            away = col_owner ^ me
            spot = jnp.where((away & 1) != 0, span + place(away, orders[1]), place(away, orders[0]))
            table[k : k + 1, :] = spot * cell_blocks + col_local
            away = row_owner ^ me
            spot = (((away & 6) // 2) * rest + row_owner // 8) * 2 + (row_owner & 1)
            table[k + 2 : k + 3, :] = spot * station_blocks + row_local
            table[k + 4 : k + 5, :] = rank
        fetch([(table, table_out)], sems)

    return local(
        body,
        [shape((8, count), I32), shape((rest * rows, LANES), F32)],
        *owners,
        weight,
        name="plan",
        specs=[whole(pltpu.HBM)] * 6,
        out_specs=[whole(pltpu.SMEM), whole()],
        scratches=[pltpu.VMEM((peers, count), I32)] * 5
        + [pltpu.VMEM((8, count), I32), pltpu.SemaphoreType.DMA((5 + rest,))],
        after=after,
    )


def shards(
    probes,
    level_set,
    unit_label,
    contrast,
    station_weight,
    u_factor,
    v_factor,
    col_owner,
    col_local,
    row_owner,
    row_local,
    tile_rank,
):
    peers = lax.axis_size("tile")
    tile_count, _, station_width = u_factor.shape
    cell_width = v_factor.shape[2]
    probe_count, cell_total = probes.shape
    cell_blocks = cell_total // cell_width
    station_blocks = station_weight.shape[0] // (peers * station_width)
    bits = [1 << k for k in range(1, peers.bit_length() - 1)]
    far = bits[:0:-1]
    orders = (far + bits[:1], bits[:1] + far)

    lanes = (cell_total // LANES, LANES)
    half_dims = (cell_blocks, probe_count, cell_width // 2)
    part_p, send, scaling = local(
        scale_body,
        [shape(half_dims, BF16), shape(half_dims, BF16), shape(lanes, F32)],
        contrast,
        level_set.reshape(lanes),
        unit_label.reshape(lanes),
        probes,
        name="scale",
        specs=[whole(pltpu.HBM)] * 4,
        scratches=[
            pltpu.SMEM(contrast.shape, F32),
            pltpu.VMEM(lanes, F32),
            pltpu.VMEM(lanes, I32),
            pltpu.VMEM(probes.shape, F32),
            pltpu.SemaphoreType.DMA((4,)),
        ],
    )
    part_q = swap(send, 1)
    table, weight = plan(
        [a.reshape(peers, tile_count) for a in (col_owner, col_local, row_owner, row_local, tile_rank)],
        station_weight.reshape(-1, LANES),
        orders,
        cell_blocks,
        station_blocks,
        (scaling,),
    )
    steps = list(zip(*orders))
    after = (weight,)
    for step, (bit_p, bit_q) in enumerate(steps):
        got_p = swap(part_p, bit_p)
        got_q = swap(part_q, bit_q) if step else swap(send, bit_q ^ 1)
        if step == 1:
            v_here, v_send = load(v_factor, (part_p, part_q), "load_v")
            u_here, u_send = load(u_factor, (part_p, part_q, v_here), "load_u")
            after = (u_here,)
        if step < len(steps) - 1:
            part_p = join(part_p, got_p, after=after)
            part_q = join(part_q, got_q)
            after = ()
        if step == 1:
            v_send, u_send = gate((v_send, u_send), (part_p, part_q))
    v_both = (v_here, swap(v_send, 1))
    u_both = (u_here, swap(u_send, 1))

    stations = peers * station_blocks
    acc = zeros((stations, probe_count, station_width // 2), (part_p, part_q))
    coeff = shrink([part_p, got_p, part_q, got_q], (0, 1), table, v_both, "coeff")
    quarter = stations // 4
    total, *sends = expand(
        coeff,
        swap(coeff, 1),
        (2, 3),
        table,
        u_both,
        acc,
        [(k // 2 * quarter, quarter) for k in SQUARE],
        "partial",
    )
    total, send = plus(total, *[swap(send, k) for k, send in zip(SQUARE, sends)])
    for bit in bits[2:-1]:
        total, send = plus(total, swap(send, bit))
    weighted = weigh(total, swap(send, bits[-1]), weight)
    gots = {k: swap(weighted, k) for k in SQUARE}

    cells = peers * cell_blocks
    acc = zeros((cells, probe_count, cell_width // 2), (total,))
    back = shrink([weighted, gots[2], gots[4], gots[6]], (2, 3), table, u_both, "back")
    total, send_p, send_q = expand(
        back,
        swap(back, 1),
        (0, 1),
        table,
        v_both,
        acc,
        [(cells // 4, cells // 4), (3 * cells // 4, cells // 4)],
        "spread",
    )
    keep_p, keep_q, base = total, total, cells // 2
    for step, (bit_p, bit_q) in enumerate(steps[::-1]):
        ends = step == len(steps) - 1
        got_p = swap(send_p, bit_p)
        got_q = swap(send_q, bit_q ^ ends)
        if not ends:
            keep_p, send_p = fold(keep_p, got_p)
            keep_q, send_q = fold(keep_q, got_q, base=base)
            base = 0
    return local(
        final_body,
        [shape((probe_count, cell_total), F32)],
        keep_p,
        got_p,
        swap(keep_q, 1),
        got_q,
        scaling,
        name="final",
        out_specs=[whole(None)],
    )[0]


def solution(mesh):
    placed = (
        P(None, ("groups", "tile")),
        P(("groups", "tile")),
        P(("groups", "tile")),
        P("groups"),
        P("groups"),
        P(("groups", "tile"), None, None),
        P(("groups", "tile"), None, None),
        P("groups", None),
        P("groups"),
        P("groups", None),
        P("groups"),
        P("groups"),
    )
    return jax.shard_map(
        shards, mesh=mesh, in_specs=placed, out_specs=P(None, ("groups", "tile")), check_vma=False
    )
```

```python
import math

import jax
import jax.numpy as jnp
from jax import lax
from jax.experimental import pallas as pl
from jax.experimental.pallas import tpu as pltpu
from jax.sharding import PartitionSpec as P

BF16 = jnp.bfloat16
F32 = jnp.float32
I32 = jnp.int32
GROUP = 8
SKEW = 3
SQUARE = (6, 2, 4)
LANES = 128
MIB = 1024 * 1024


def whole(space=pltpu.VMEM):
    return pl.BlockSpec(memory_space=space)


def shape(dims, dtype):
    return jax.ShapeDtypeStruct(tuple(dims), dtype)


def size_of(array):
    return math.prod(array.shape) * jnp.dtype(array.dtype).itemsize


def swap(array, bits):
    count = lax.axis_size("tile")
    return lax.ppermute(array, "tile", [(i, i ^ bits) for i in range(count)])


def local(
    body, outs, *ins, name, scratch=0, scratches=(), specs=None, out_specs=None, flops=0, after=(), aliases=None
):
    nbytes = sum(size_of(a) for a in (*ins, *outs))
    specs = list(specs or [whole()] * len(ins)) + [whole()] * len(after)
    out_specs = list(out_specs or [whole()] * len(outs))
    own = len(ins)
    ins = [pltpu.with_memory_space_constraint(a, s.memory_space) for a, s in zip((*ins, *after), specs)]

    def run(*refs):
        body(*refs[:own], *refs[len(ins) :])

    return pl.pallas_call(
        run,
        out_shape=[a if s.memory_space is None else s.memory_space(a.shape, a.dtype) for a, s in zip(outs, out_specs)],
        in_specs=specs,
        out_specs=[whole() if s.memory_space is None else s for s in out_specs],
        input_output_aliases=aliases or {},
        scratch_shapes=list(scratches),
        compiler_params=pltpu.CompilerParams(vmem_limit_bytes=scratch + 8 * MIB),
        cost_estimate=pl.CostEstimate(flops=0, bytes_accessed=0, transcendentals=0),
        name=name,
    )(*ins)


def fetch(pairs, sems):
    copies = [pltpu.make_async_copy(a, b, sems.at[i]) for i, (a, b) in enumerate(pairs)]
    for copy in copies:
        copy.start()
    for copy in copies:
        copy.wait()


def load(arrays, after):
    count, rank, width = arrays[0].shape
    half = width // 2
    parts = 4
    n = count // parts

    def body(*refs):
        sources, mine, other, sems = refs[:2], refs[2:4], refs[4], refs[5]
        core = lax.axis_index("tile") & 1
        pairs = []
        for k, source in enumerate(sources):
            for which, out, base in ((1 - core, other, k * count), (core, mine[k], 0)):
                lanes = pl.ds(pl.multiple_of(which * half, half), half)
                for i in range(parts):
                    pairs.append((source.at[pl.ds(i * n, n), :, lanes], out.at[pl.ds(base + i * n, n)]))
        fetch(pairs, sems)

    return local(
        body,
        [shape((k * count, rank, half), arrays[0].dtype) for k in (1, 1, 2)],
        *arrays,
        name="load",
        specs=[whole(pltpu.HBM)] * 2,
        scratches=[pltpu.SemaphoreType.DMA((4 * parts,))],
        after=after,
    )


def scale_body(contrast, level, label, probes, mine, other, scaling, contrast_near, level_near, label_near, probes_near, sems):
    fetch(
        [(contrast, contrast_near), (level, level_near), (label, label_near), (probes, probes_near)],
        sems,
    )
    odd = (lax.axis_index("tile") & 1) != 0
    value = level_near[...]
    unit = label_near[...]
    factor = jnp.zeros_like(value)
    for k in range(contrast.shape[0]):
        factor = jnp.where(unit == k, contrast_near[k], factor)
    scaling[...] = factor / (1.0 + value * value)
    blocks, _, half = mine.shape
    rows = half // LANES
    for b in range(blocks):
        for c in range(rows):
            low, high = [
                probes_near[:, j * LANES : (j + 1) * LANES] * scaling[j : j + 1, :]
                for j in (2 * b * rows + c, (2 * b + 1) * rows + c)
            ]
            lanes = slice(c * LANES, (c + 1) * LANES)
            mine[b, :, lanes] = jnp.where(odd, high, low).astype(BF16)
            other[b, :, lanes] = jnp.where(odd, low, high).astype(BF16)


def final_body(keep, recv, other_keep, other_recv, scaling, out):
    odd = (lax.axis_index("tile") & 1) != 0
    blocks, _, half = keep.shape
    rows = half // LANES
    for b in range(blocks):
        for c in range(rows):
            lanes = slice(c * LANES, (c + 1) * LANES)
            own = keep[b, :, lanes] + recv[b, :, lanes].astype(F32)
            got = other_keep[b, :, lanes] + other_recv[b, :, lanes].astype(F32)
            for j, total in (
                (2 * b * rows + c, jnp.where(odd, got, own)),
                ((2 * b + 1) * rows + c, jnp.where(odd, own, got)),
            ):
                out[:, j * LANES : (j + 1) * LANES] = total * scaling[j : j + 1, :]


def join_body(*refs):
    out, at = refs[-1], 0
    for ref in refs[:-1]:
        out[at : at + ref.shape[0]] = ref[...]
        at += ref.shape[0]


def join(*pieces, after=()):
    out = shape((sum(a.shape[0] for a in pieces),) + pieces[0].shape[1:], pieces[0].dtype)
    return local(join_body, [out], *pieces, name="join", after=after)[0]


def plus(total, *gots):
    dims = gots[0].shape

    def body(total, *refs):
        done = total[: dims[0]]
        for ref in refs[:-2]:
            done = done + ref[...].astype(F32)
        refs[-2][...] = done
        refs[-1][...] = done.astype(BF16)

    return local(body, [shape(dims, F32), shape(dims, BF16)], total, *gots, name="plus")


def weigh(total, got, weight):
    def body(total, got, weight, out):
        core = lax.axis_index("tile") & 1
        blocks, _, half = out.shape
        rows = half // LANES
        for b in range(blocks):
            for c in range(rows):
                lanes = slice(c * LANES, (c + 1) * LANES)
                done = total[b, :, lanes] + got[b, :, lanes].astype(F32)
                row = weight[pl.ds((2 * b + core) * rows + c, 1), :]
                out[b, :, lanes] = (done * row).astype(BF16)

    return local(body, [shape(total.shape, BF16)], total, got, weight, name="weigh")[0]


def fold(keep, recv, dtypes=(F32, BF16), base=0):
    n = recv.shape[0] // len(dtypes)
    outs = [shape((n,) + keep.shape[1:], t) for t in dtypes]

    def body(keep, recv, *outs):
        for i, out in enumerate(outs):
            mine = keep[base + i * n : base + (i + 1) * n]
            out[...] = (mine + recv[i * n : (i + 1) * n].astype(F32)).astype(out.dtype)

    return local(body, outs, keep, recv, name="fold")


def gate(arrays, after):
    def body(*refs):
        pass

    outs = [shape(a.shape, a.dtype) for a in arrays]
    return local(body, outs, *arrays, name="gate", after=after, aliases={i: i for i in range(len(arrays))})


def zeros(dims, after):
    def body(out):
        out[...] = jnp.zeros_like(out)

    return local(body, [shape(dims, F32)], name="zeros", after=after)[0]


def own_mask(rank, probes):
    dims = (GROUP * probes, GROUP * rank)
    rows = lax.broadcasted_iota(I32, dims, 0) // probes
    columns = lax.broadcasted_iota(I32, dims, 1)
    return jnp.where(rows == columns // rank, columns % rank, rank)


def skewed(groups, *stages):
    held = {}
    last = SKEW * (len(stages) - 1)
    for step in range(groups + last):
        for k in range(len(stages) - 1, -1, -1):
            g = step - k * SKEW
            if 0 <= g < groups:
                held[g] = stages[k](g, held.get(g))
                if k == len(stages) - 1:
                    del held[g]


def shrink(pieces, at_rows, table, factors, name):
    count, rank, half = factors[0].shape
    probes = pieces[0].shape[1]
    groups = count // GROUP
    span = GROUP * rank
    rows = sum(piece.shape[0] for piece in pieces)

    def body(at, *refs):
        mine, other, out, near = refs[len(pieces) :]
        join_body(*refs[: len(pieces)], near)
        own = own_mask(rank, probes)
        lane_tile = lax.broadcasted_iota(I32, (1, span), 1) // rank

        def dots(g, _):
            row, first = at_rows[g // groups], (g % groups) * GROUP
            taken = jnp.concatenate([near[at[row, first + i]].astype(F32) for i in range(GROUP)], axis=0)
            if g >= groups:
                first += factors[2] * count
            factor = (mine, other)[g // groups][first : first + GROUP].reshape(span, half)
            return lax.dot_general(
                taken.astype(BF16), factor, (((1,), (1,)), ((), ())), preferred_element_type=F32
            )

        def store(g, inner):
            row, first = 4 + g // groups, (g % groups) * GROUP
            limit = jnp.zeros((1, span), I32)
            for i in range(GROUP):
                limit = jnp.where(lane_tile == i, at[row, first + i], limit)
            inner = jnp.where(own < limit, inner, 0.0)
            out[g] = sum(inner[i * probes : (i + 1) * probes] for i in range(GROUP))

        skewed(2 * groups, dots, store)

    return local(
        body,
        [shape((2 * groups, probes, span), F32)],
        table,
        *pieces,
        *factors[:2],
        name=name,
        specs=[whole(pltpu.SMEM)] + [whole()] * (len(pieces) + 2),
        flops=4 * count * rank * half * probes * GROUP,
        scratch=2 * rows * probes * half,
        scratches=[pltpu.VMEM((rows, probes, half), BF16)],
    )[0]


def expand(mine_sum, other_sum, at_rows, table, factors, acc, sends, name):
    count, rank, half = factors[0].shape
    probes = acc.shape[1]
    groups = count // GROUP
    span = GROUP * rank

    def body(at, _, sums, got, mine, other, out, *parts):
        own = own_mask(rank, probes) < rank

        def dots(g, _):
            total = sums[g] + got[(g + groups) % (2 * groups)]
            total = jnp.concatenate([total.astype(BF16).astype(F32)] * GROUP, axis=0)
            total = jnp.where(own, total, 0.0).astype(BF16)
            first = (g % groups) * GROUP
            if g >= groups:
                first += factors[2] * count
            factor = (mine, other)[g // groups][first : first + GROUP].reshape(span, half)
            return jnp.dot(total, factor, preferred_element_type=F32)

        def add(g, outer):
            row, first = at_rows[g // groups], (g % groups) * GROUP
            for i in range(GROUP):
                to = at[row, first + i]
                out[to] = out[to] + outer[i * probes : (i + 1) * probes]

        skewed(2 * groups, dots, add)
        for part, (start, size) in zip(parts, sends):
            part[...] = out[start : start + size].astype(BF16)

    return local(
        body,
        [shape(acc.shape, F32)] + [shape((size, probes, half), BF16) for _, size in sends],
        table,
        acc,
        mine_sum,
        other_sum,
        *factors[:2],
        name=name,
        specs=[whole(pltpu.SMEM)] + [whole()] * 5,
        aliases={1: 0},
        flops=4 * count * rank * half * probes * GROUP,
    )


def place(relative, order):
    at = jnp.zeros_like(relative)
    for k, bit in enumerate(order):
        at = at + jnp.where((relative & bit) != 0, 1 << k, 0)
    return at


def plan(owners, weight, orders, cell_blocks, station_blocks, after):
    peers, count = owners[0].shape
    rows = 2 * (weight.shape[0] // peers)
    rest = peers // 8

    def body(*refs):
        far, weight_far, table_out, weight_near = refs[:5], refs[5], refs[6], refs[7]
        near, table, sems = refs[8:13], refs[13], refs[14]
        me = lax.axis_index("tile")
        pairs = list(zip(far, near))
        for k in range(rest):
            start = pl.multiple_of((k * 4 + (me & 6) // 2) * rows, rows)
            pairs.append((weight_far.at[pl.ds(start, rows)], weight_near.at[pl.ds(k * rows, rows)]))
        fetch(pairs, sems)
        span = peers // 2
        for k, holder in enumerate((me, me ^ 1)):
            col_owner, col_local, row_owner, row_local, rank = [ref[pl.ds(holder, 1), :] for ref in near]
            away = col_owner ^ me
            spot = jnp.where((away & 1) != 0, span + place(away, orders[1]), place(away, orders[0]))
            table[k : k + 1, :] = spot * cell_blocks + col_local
            away = row_owner ^ me
            quarter = jnp.zeros_like(away)
            for j, bit in enumerate(SQUARE):
                quarter = jnp.where((away & 6) == bit, 1 + j, quarter)
            spot = (quarter * rest + row_owner // 8) * 2 + (row_owner & 1)
            table[k + 2 : k + 3, :] = spot * station_blocks + row_local
            table[k + 4 : k + 5, :] = rank
        fetch([(table, table_out)], sems)

    return local(
        body,
        [shape((8, count), I32), shape((rest * rows, LANES), F32)],
        *owners,
        weight,
        name="plan",
        specs=[whole(pltpu.HBM)] * 6,
        out_specs=[whole(pltpu.SMEM), whole()],
        scratches=[pltpu.VMEM((peers, count), I32)] * 5
        + [pltpu.VMEM((8, count), I32), pltpu.SemaphoreType.DMA((5 + rest,))],
        after=after,
    )


def shards(
    probes,
    level_set,
    unit_label,
    contrast,
    station_weight,
    u_factor,
    v_factor,
    col_owner,
    col_local,
    row_owner,
    row_local,
    tile_rank,
):
    peers = lax.axis_size("tile")
    tile_count, _, station_width = u_factor.shape
    cell_width = v_factor.shape[2]
    probe_count, cell_total = probes.shape
    cell_blocks = cell_total // cell_width
    station_blocks = station_weight.shape[0] // (peers * station_width)
    bits = [1 << k for k in range(1, peers.bit_length() - 1)]
    far = bits[:0:-1]
    orders = (far + bits[:1], bits[:1] + far)

    lanes = (cell_total // LANES, LANES)
    half_dims = (cell_blocks, probe_count, cell_width // 2)
    part_p, send, scaling = local(
        scale_body,
        [shape(half_dims, BF16), shape(half_dims, BF16), shape(lanes, F32)],
        contrast,
        level_set.reshape(lanes),
        unit_label.reshape(lanes),
        probes,
        name="scale",
        specs=[whole(pltpu.HBM)] * 4,
        scratches=[
            pltpu.SMEM(contrast.shape, F32),
            pltpu.VMEM(lanes, F32),
            pltpu.VMEM(lanes, I32),
            pltpu.VMEM(probes.shape, F32),
            pltpu.SemaphoreType.DMA((4,)),
        ],
    )
    part_q = swap(send, 1)
    table, weight = plan(
        [a.reshape(peers, tile_count) for a in (col_owner, col_local, row_owner, row_local, tile_rank)],
        station_weight.reshape(-1, LANES),
        orders,
        cell_blocks,
        station_blocks,
        (scaling,),
    )
    steps = list(zip(*orders))
    after = (weight,)
    for step, (bit_p, bit_q) in enumerate(steps):
        got_p = swap(part_p, bit_p)
        got_q = swap(part_q, bit_q) if step else swap(send, bit_q ^ 1)
        if step == 1:
            v_here, u_here, halves = load((v_factor, u_factor), (part_p, part_q))
            after = (u_here,)
        if step < len(steps) - 1:
            part_p = join(part_p, got_p, after=after)
            part_q = join(part_q, got_q)
            after = ()
        if step == 1:
            halves = gate((halves,), (part_p, part_q))[0]
    halves = swap(halves, 1)

    stations = peers * station_blocks
    acc = zeros((stations, probe_count, station_width // 2), (part_p, part_q))
    coeff = shrink([part_p, got_p, part_q, got_q], (0, 1), table, (v_here, halves, 0), "coeff")
    quarter = stations // 4
    total, *sends = expand(
        coeff,
        swap(coeff, 1),
        (2, 3),
        table,
        (u_here, halves, 1),
        acc,
        [((1 + j) * quarter, quarter) for j in range(len(SQUARE))],
        "partial",
    )
    sends = dict(zip(SQUARE, sends))
    total, send = plus(total, *[swap(sends[k], k) for k in (4, 6, 2)])
    for bit in bits[2:-1]:
        total, send = plus(total, swap(send, bit))
    weighted = weigh(total, swap(send, bits[-1]), weight)
    pieces = [weighted] + [swap(weighted, k) for k in SQUARE]

    cells = peers * cell_blocks
    acc = zeros((cells, probe_count, cell_width // 2), (total,))
    back = shrink(pieces, (2, 3), table, (u_here, halves, 1), "back")
    total, send_p, send_q = expand(
        back,
        swap(back, 1),
        (0, 1),
        table,
        (v_here, halves, 0),
        acc,
        [(cells // 4, cells // 4), (3 * cells // 4, cells // 4)],
        "spread",
    )
    keep_p, keep_q, base = total, total, cells // 2
    for step, (bit_p, bit_q) in enumerate(steps[::-1]):
        ends = step == len(steps) - 1
        got_p = swap(send_p, bit_p)
        got_q = swap(send_q, bit_q ^ ends)
        if not ends:
            keep_p, send_p = fold(keep_p, got_p)
            keep_q, send_q = fold(keep_q, got_q, base=base)
            base = 0
    return local(
        final_body,
        [shape((probe_count, cell_total), F32)],
        keep_p,
        got_p,
        swap(keep_q, 1),
        got_q,
        scaling,
        name="final",
        out_specs=[whole(None)],
    )[0]


def solution(mesh):
    placed = (
        P(None, ("groups", "tile")),
        P(("groups", "tile")),
        P(("groups", "tile")),
        P("groups"),
        P("groups"),
        P(("groups", "tile"), None, None),
        P(("groups", "tile"), None, None),
        P("groups", None),
        P("groups"),
        P("groups", None),
        P("groups"),
        P("groups"),
    )
    return jax.shard_map(
        shards, mesh=mesh, in_specs=placed, out_specs=P(None, ("groups", "tile")), check_vma=False
    )
```

```python
import math

import jax
import jax.numpy as jnp
from jax import lax
from jax.experimental import pallas as pl
from jax.experimental.pallas import tpu as pltpu
from jax.sharding import PartitionSpec as P

BF16 = jnp.bfloat16
F32 = jnp.float32
I32 = jnp.int32
GROUP = 8
SKEW = 3
SQUARE = (6, 2, 4)
LANES = 128
MIB = 1024 * 1024


def whole(space=pltpu.VMEM):
    return pl.BlockSpec(memory_space=space)


def shape(dims, dtype):
    return jax.ShapeDtypeStruct(tuple(dims), dtype)


def size_of(array):
    return math.prod(array.shape) * jnp.dtype(array.dtype).itemsize


def swap(array, bits):
    count = lax.axis_size("tile")
    return lax.ppermute(array, "tile", [(i, i ^ bits) for i in range(count)])


def local(
    body, outs, *ins, name, scratch=0, scratches=(), specs=None, out_specs=None, flops=0, after=(), aliases=None
):
    nbytes = sum(size_of(a) for a in (*ins, *outs))
    specs = list(specs or [whole()] * len(ins)) + [whole()] * len(after)
    out_specs = list(out_specs or [whole()] * len(outs))
    own = len(ins)
    ins = [pltpu.with_memory_space_constraint(a, s.memory_space) for a, s in zip((*ins, *after), specs)]

    def run(*refs):
        body(*refs[:own], *refs[len(ins) :])

    return pl.pallas_call(
        run,
        out_shape=[a if s.memory_space is None else s.memory_space(a.shape, a.dtype) for a, s in zip(outs, out_specs)],
        in_specs=specs,
        out_specs=[whole() if s.memory_space is None else s for s in out_specs],
        input_output_aliases=aliases or {},
        scratch_shapes=list(scratches),
        compiler_params=pltpu.CompilerParams(vmem_limit_bytes=scratch + 8 * MIB),
        cost_estimate=pl.CostEstimate(flops=flops, bytes_accessed=nbytes, transcendentals=0),
        name=name,
    )(*ins)


def fetch(pairs, sems):
    copies = [pltpu.make_async_copy(a, b, sems.at[i]) for i, (a, b) in enumerate(pairs)]
    for copy in copies:
        copy.start()
    for copy in copies:
        copy.wait()


def load(arrays, after):
    parts = 4

    def body(*refs):
        count = len(refs) // 2
        pairs = []
        for source, out in zip(refs[:count], refs[count:-1]):
            n = source.shape[0] // parts
            pairs += [(source.at[pl.ds(i * n, n)], out.at[pl.ds(i * n, n)]) for i in range(parts)]
        fetch(pairs, refs[-1])

    return local(
        body,
        [shape(a.shape, a.dtype) for a in arrays],
        *arrays,
        name="load",
        specs=[whole(pltpu.HBM)] * len(arrays),
        scratches=[pltpu.SemaphoreType.DMA((parts * len(arrays),))],
        after=after,
    )


def scale_body(
    contrast, level, label, probes, part_p, part_q, scaling, contrast_near, level_near, label_near, probes_near, sems
):
    fetch(
        [(contrast, contrast_near), (level, level_near), (label, label_near), (probes, probes_near)],
        sems,
    )
    value = level_near[...]
    unit = label_near[...]
    factor = jnp.zeros_like(value)
    for k in range(contrast.shape[0]):
        factor = jnp.where(unit == k, contrast_near[k], factor)
    scaling[...] = factor / (1.0 + value * value)
    blocks, _, width = part_p.shape
    rows = width // LANES
    for half, part in enumerate((part_p, part_q)):
        for b in range(blocks):
            for c in range(rows):
                j = (half * blocks + b) * rows + c
                piece = probes_near[:, j * LANES : (j + 1) * LANES] * scaling[j : j + 1, :]
                part[b, :, c * LANES : (c + 1) * LANES] = piece.astype(BF16)


def final_body(keep_q, recv_q, keep_p, recv_p, scaling, out):
    blocks, _, width = keep_p.shape
    rows = width // LANES
    for half, (keep, recv) in enumerate(((keep_p, recv_p), (keep_q, recv_q))):
        for b in range(blocks):
            for c in range(rows):
                j = (half * blocks + b) * rows + c
                lanes = slice(c * LANES, (c + 1) * LANES)
                total = keep[b, :, lanes] + recv[b, :, lanes].astype(F32)
                out[:, j * LANES : (j + 1) * LANES] = total * scaling[j : j + 1, :]


def join_body(*refs):
    out, at = refs[-1], 0
    for ref in refs[:-1]:
        out[at : at + ref.shape[0]] = ref[...]
        at += ref.shape[0]


def join(*pieces, after=()):
    out = shape((sum(a.shape[0] for a in pieces),) + pieces[0].shape[1:], pieces[0].dtype)
    return local(join_body, [out], *pieces, name="join", after=after)[0]


def plus(total, *gots):
    def body(total, *refs):
        done = total[...]
        for ref in refs[:-2]:
            done = done + ref[...].astype(F32)
        refs[-2][...] = done
        refs[-1][...] = done.astype(BF16)

    return local(body, [shape(total.shape, F32), shape(total.shape, BF16)], total, *gots, name="plus")


def weigh(total, got, weight):
    def body(total, got, weight, out):
        blocks, _, width = out.shape
        rows = width // LANES
        for b in range(blocks):
            for c in range(rows):
                lanes = slice(c * LANES, (c + 1) * LANES)
                done = total[b, :, lanes] + got[b, :, lanes].astype(F32)
                j = b * rows + c
                out[b, :, lanes] = (done * weight[j : j + 1, :]).astype(BF16)

    return local(body, [shape(total.shape, BF16)], total, got, weight, name="weigh")[0]


def fold(keep, recv, dtypes=(F32, BF16), base=0):
    n = recv.shape[0] // len(dtypes)

    def body(keep, recv, *outs):
        for i, out in enumerate(outs):
            mine = keep[base + i * n : base + (i + 1) * n]
            out[...] = (mine + recv[i * n : (i + 1) * n].astype(F32)).astype(out.dtype)

    return local(body, [shape((n,) + keep.shape[1:], t) for t in dtypes], keep, recv, name="fold")


def zeros(dims, after):
    def body(out):
        out[...] = jnp.zeros_like(out)

    return local(body, [shape(dims, F32)], name="zeros", after=after)[0]


def tiles_body(piece_count, src_row, dst_row, at, _, *refs):
    pieces = refs[:piece_count]
    first, second, acc, *sends, table = refs[piece_count:]
    count, rank, width = first.shape
    groups = count // GROUP
    join_body(*pieces, table)
    probes = table.shape[1]
    span = GROUP * rank
    row_tile = lax.broadcasted_iota(I32, (GROUP * probes, span), 0) // probes
    col_tile = lax.broadcasted_iota(I32, (GROUP * probes, span), 1) // rank
    component = lax.broadcasted_iota(I32, (GROUP * probes, span), 1) % rank
    own = jnp.where(row_tile == col_tile, component, rank)
    lane_tile = lax.broadcasted_iota(I32, (1, span), 1) // rank

    def inner_of(g):
        taken = jnp.concatenate(
            [table[at[src_row, g * GROUP + i]].astype(F32) for i in range(GROUP)], axis=0
        ).astype(BF16)
        left = first[g * GROUP : (g + 1) * GROUP].reshape(span, width)
        inner = lax.dot_general(taken, left, (((1,), (1,)), ((), ())), preferred_element_type=F32)
        limit = jnp.zeros((1, span), I32)
        for i in range(GROUP):
            limit = jnp.where(lane_tile == i, at[2, g * GROUP + i], limit)
        return jnp.where(own < limit, inner, 0.0).astype(BF16)

    def outer_of(g, kept):
        right = second[g * GROUP : (g + 1) * GROUP].reshape(span, width)
        return jnp.dot(kept, right, preferred_element_type=F32)

    def add(g, outer):
        for i in range(GROUP):
            to = at[dst_row, g * GROUP + i]
            acc[to] = acc[to] + outer[i * probes : (i + 1) * probes]

    kept, outer = {}, {}
    for step in range(groups + 2 * SKEW):
        if step >= 2 * SKEW:
            add(step - 2 * SKEW, outer.pop(step - 2 * SKEW))
        if 0 <= step - SKEW < groups:
            outer[step - SKEW] = outer_of(step - SKEW, kept.pop(step - SKEW))
        if step < groups:
            kept[step] = inner_of(step)
    base = acc.shape[0] // 2
    for send in sends:
        send[...] = acc[base : base + send.shape[0]].astype(send.dtype)
        base += send.shape[0]


def tiles(pieces, src_row, dst_row, table, first, second, acc, parts, send_dtype, name):
    count, rank, width = first.shape
    blocks, probes, _ = acc.shape
    rows = sum(piece.shape[0] for piece in pieces)

    def body(*refs):
        tiles_body(len(pieces), src_row, dst_row, *refs)

    return local(
        body,
        [shape(acc.shape, F32)] + [shape((blocks // 2 // parts, probes, width), send_dtype)] * parts,
        table,
        acc,
        *pieces,
        first,
        second,
        name=name,
        specs=[whole(pltpu.SMEM)] + [whole()] * (len(pieces) + 3),
        aliases={1: 0},
        flops=4 * count * rank * width * probes * GROUP,
        scratch=2 * rows * probes * width,
        scratches=[pltpu.VMEM((rows, probes, width), BF16)],
    )


def place(relative, order):
    at = jnp.zeros_like(relative)
    for k, bit in enumerate(order):
        at = at + jnp.where((relative & bit) != 0, 1 << k, 0)
    return at


def plan(owners, weight, orders, cell_blocks, station_blocks, after):
    peers, count = owners[0].shape
    rows = weight.shape[0] // peers
    rest = peers // 8
    half = cell_blocks // 2

    def body(*refs):
        far, weight_far, table_out, weight_near = refs[:5], refs[5], refs[6], refs[7]
        near, table, sems = refs[8:13], refs[13], refs[14]
        me = lax.axis_index("tile")
        pairs = list(zip(far, near))
        for k in range(rest):
            start = pl.multiple_of((k * 8 + (me & 7)) * rows, rows)
            pairs.append((weight_far.at[pl.ds(start, rows)], weight_near.at[pl.ds(k * rows, rows)]))
        fetch(pairs, sems)
        col_owner, col_local, row_owner, row_local, rank = [ref[pl.ds(me, 1), :] for ref in near]
        span = peers // 2
        away = col_owner ^ me
        is_q = col_local >= half
        spot = jnp.where(is_q, place(away, orders[1]) + (span - 1), place(away, orders[0]))
        table[0:1, :] = (away & 1) * (span * cell_blocks) + spot * half + col_local
        away = row_owner ^ me
        spot = (away & 1) * 4 + ((away & 4) // 2) + ((away & 2) // 2)
        table[1:2, :] = (spot * rest + row_owner // 8) * station_blocks + row_local
        table[2:3, :] = rank
        fetch([(table, table_out)], sems)

    return local(
        body,
        [shape((8, count), I32), shape((rest * rows, LANES), F32)],
        *owners,
        weight,
        name="plan",
        specs=[whole(pltpu.HBM)] * 6,
        out_specs=[whole(pltpu.SMEM), whole()],
        scratches=[pltpu.VMEM((peers, count), I32)] * 5
        + [pltpu.VMEM((8, count), I32), pltpu.SemaphoreType.DMA((5 + rest,))],
        after=after,
    )


def shards(
    probes,
    level_set,
    unit_label,
    contrast,
    station_weight,
    u_factor,
    v_factor,
    col_owner,
    col_local,
    row_owner,
    row_local,
    tile_rank,
):
    peers = lax.axis_size("tile")
    tile_count, _, station_width = u_factor.shape
    cell_width = v_factor.shape[2]
    probe_count, cell_total = probes.shape
    cell_blocks = cell_total // cell_width
    station_blocks = station_weight.shape[0] // (peers * station_width)
    bits = [1 << k for k in range(1, peers.bit_length() - 1)]
    far = bits[:0:-1]
    orders = (bits[:1] + far, far + bits[:1])

    lanes = (cell_total // LANES, LANES)
    half_dims = (cell_blocks // 2, probe_count, cell_width)
    part_p, part_q, scaling = local(
        scale_body,
        [shape(half_dims, BF16), shape(half_dims, BF16), shape(lanes, F32)],
        contrast,
        level_set.reshape(lanes),
        unit_label.reshape(lanes),
        probes,
        name="scale",
        specs=[whole(pltpu.HBM)] * 4,
        scratches=[
            pltpu.SMEM(contrast.shape, F32),
            pltpu.VMEM(lanes, F32),
            pltpu.VMEM(lanes, I32),
            pltpu.VMEM(probes.shape, F32),
            pltpu.SemaphoreType.DMA((4,)),
        ],
    )
    table, weight = plan(
        [a.reshape(peers, tile_count) for a in (col_owner, col_local, row_owner, row_local, tile_rank)],
        station_weight.reshape(-1, LANES),
        orders,
        cell_blocks,
        station_blocks,
        (scaling,),
    )
    steps = list(zip(*orders))
    after = (weight,)
    for step, (bit_p, bit_q) in enumerate(steps):
        got_p = swap(part_p, bit_p)
        got_q = swap(part_q, bit_q)
        if step == 1:
            v_here, u_here = load((v_factor, u_factor), (part_p, part_q))
            after = (u_here,)
        if step < len(steps) - 1:
            part_p = join(part_p, got_p, after=after)
            part_q = join(part_q, got_q)
            after = ()
    pieces = [part_p, got_p, part_q, got_q]
    pieces = pieces + [swap(piece, 1) for piece in pieces]

    acc = zeros((peers * station_blocks, probe_count, station_width), (part_p, part_q))
    total, *sends = tiles(pieces, 0, 1, table, v_here, u_here, acc, 4, F32, "forward")
    quarters = [0] * 4
    for k in SQUARE + (0,):
        kept = F32 if k == 0 else BF16
        quarters[k // 2] = fold(total, swap(sends[k // 2], 1), (kept,), base=k // 2 * sends[0].shape[0])[0]
    total, send = plus(quarters[0], *[swap(quarters[k // 2], k) for k in SQUARE])
    for bit in bits[2:-1]:
        total, send = plus(total, swap(send, bit))
    weighted = weigh(total, swap(send, bits[-1]), weight)
    gots = {k: swap(weighted, k) for k in SQUARE}
    around = join(gots[2], gots[4], gots[6])
    pieces = [weighted, around, swap(weighted, 1), swap(around, 1)]

    acc = zeros((peers * cell_blocks, probe_count, cell_width), (total,))
    total, send_p, send_q = tiles(pieces, 1, 0, table, u_here, v_here, acc, 2, BF16, "adjoint")
    keep_q, send_q = fold(total, swap(send_q, 1), base=total.shape[0] // 4)
    keep_p, send_p = fold(total, swap(send_p, 1))
    for step, (bit_p, bit_q) in enumerate(steps[::-1]):
        if step > 0:
            keep_q, send_q = fold(keep_q, got_q)
            keep_p, send_p = fold(keep_p, got_p)
        got_q = swap(send_q, bit_q)
        got_p = swap(send_p, bit_p)
    return local(
        final_body,
        [shape((probe_count, cell_total), F32)],
        keep_q,
        got_q,
        keep_p,
        got_p,
        scaling,
        name="final",
        out_specs=[whole(None)],
    )[0]


def solution(mesh):
    placed = (
        P(None, ("groups", "tile")),
        P(("groups", "tile")),
        P(("groups", "tile")),
        P("groups"),
        P("groups"),
        P(("groups", "tile"), None, None),
        P(("groups", "tile"), None, None),
        P("groups", None),
        P("groups"),
        P("groups", None),
        P("groups"),
        P("groups"),
    )
    return jax.shard_map(
        shards, mesh=mesh, in_specs=placed, out_specs=P(None, ("groups", "tile")), check_vma=False
    )
```

```python
import math

import jax
import jax.numpy as jnp
from jax import lax
from jax.experimental import pallas as pl
from jax.experimental.pallas import tpu as pltpu
from jax.sharding import PartitionSpec as P

BF16 = jnp.bfloat16
F32 = jnp.float32
I32 = jnp.int32
GROUP = 8
SKEW = 3
SQUARE = (6, 2, 4)
LANES = 128
MIB = 1024 * 1024


def whole(space=pltpu.VMEM):
    return pl.BlockSpec(memory_space=space)


def shape(dims, dtype):
    return jax.ShapeDtypeStruct(tuple(dims), dtype)


def size_of(array):
    return math.prod(array.shape) * jnp.dtype(array.dtype).itemsize


def swap(array, bits):
    count = lax.axis_size("tile")
    return lax.ppermute(array, "tile", [(i, i ^ bits) for i in range(count)])


def local(
    body, outs, *ins, name, scratch=0, scratches=(), specs=None, out_specs=None, flops=0, after=(), aliases=None
):
    nbytes = sum(size_of(a) for a in (*ins, *outs))
    specs = list(specs or [whole()] * len(ins)) + [whole()] * len(after)
    out_specs = list(out_specs or [whole()] * len(outs))
    own = len(ins)
    ins = [pltpu.with_memory_space_constraint(a, s.memory_space) for a, s in zip((*ins, *after), specs)]

    def run(*refs):
        body(*refs[:own], *refs[len(ins) :])

    return pl.pallas_call(
        run,
        out_shape=[a if s.memory_space is None else s.memory_space(a.shape, a.dtype) for a, s in zip(outs, out_specs)],
        in_specs=specs,
        out_specs=[whole() if s.memory_space is None else s for s in out_specs],
        input_output_aliases=aliases or {},
        scratch_shapes=list(scratches),
        compiler_params=pltpu.CompilerParams(vmem_limit_bytes=scratch + 8 * MIB),
        cost_estimate=pl.CostEstimate(flops=flops, bytes_accessed=nbytes, transcendentals=0),
        name=name,
    )(*ins)


def fetch(pairs, sems):
    copies = [pltpu.make_async_copy(a, b, sems.at[i]) for i, (a, b) in enumerate(pairs)]
    for copy in copies:
        copy.start()
    for copy in copies:
        copy.wait()


def load(arrays, after):
    parts = 4

    def body(*refs):
        count = len(refs) // 2
        pairs = []
        for source, out in zip(refs[:count], refs[count:-1]):
            n = source.shape[0] // parts
            pairs += [(source.at[pl.ds(i * n, n)], out.at[pl.ds(i * n, n)]) for i in range(parts)]
        fetch(pairs, refs[-1])

    return local(
        body,
        [shape(a.shape, a.dtype) for a in arrays],
        *arrays,
        name="load",
        specs=[whole(pltpu.HBM)] * len(arrays),
        scratches=[pltpu.SemaphoreType.DMA((parts * len(arrays),))],
        after=after,
    )


def scale_body(
    contrast, level, label, probes, part_p, part_q, scaling, contrast_near, level_near, label_near, probes_near, sems
):
    fetch(
        [(contrast, contrast_near), (level, level_near), (label, label_near), (probes, probes_near)],
        sems,
    )
    value = level_near[...]
    unit = label_near[...]
    factor = jnp.zeros_like(value)
    for k in range(contrast.shape[0]):
        factor = jnp.where(unit == k, contrast_near[k], factor)
    scaling[...] = factor / (1.0 + value * value)
    blocks, _, width = part_p.shape
    rows = width // LANES
    for half, part in enumerate((part_p, part_q)):
        for b in range(blocks):
            for c in range(rows):
                j = (half * blocks + b) * rows + c
                piece = probes_near[:, j * LANES : (j + 1) * LANES] * scaling[j : j + 1, :]
                part[b, :, c * LANES : (c + 1) * LANES] = piece.astype(BF16)


def final_body(keep_q, recv_q, keep_p, recv_p, scaling, out):
    blocks, _, width = keep_p.shape
    rows = width // LANES
    for half, (keep, recv) in enumerate(((keep_p, recv_p), (keep_q, recv_q))):
        for b in range(blocks):
            for c in range(rows):
                j = (half * blocks + b) * rows + c
                lanes = slice(c * LANES, (c + 1) * LANES)
                total = keep[b, :, lanes] + recv[b, :, lanes].astype(F32)
                out[:, j * LANES : (j + 1) * LANES] = total * scaling[j : j + 1, :]


def join_body(*refs):
    out, at = refs[-1], 0
    for ref in refs[:-1]:
        out[at : at + ref.shape[0]] = ref[...]
        at += ref.shape[0]


def join(*pieces, after=()):
    out = shape((sum(a.shape[0] for a in pieces),) + pieces[0].shape[1:], pieces[0].dtype)
    return local(join_body, [out], *pieces, name="join", after=after)[0]


def plus(total, *gots):
    def body(total, *refs):
        done = total[...]
        for ref in refs[:-2]:
            done = done + ref[...].astype(F32)
        refs[-2][...] = done
        refs[-1][...] = done.astype(BF16)

    return local(body, [shape(total.shape, F32), shape(total.shape, BF16)], total, *gots, name="plus")


def weigh(total, got, weight):
    def body(total, got, weight, out):
        blocks, _, width = out.shape
        rows = width // LANES
        for b in range(blocks):
            for c in range(rows):
                lanes = slice(c * LANES, (c + 1) * LANES)
                done = total[b, :, lanes] + got[b, :, lanes].astype(F32)
                j = b * rows + c
                out[b, :, lanes] = (done * weight[j : j + 1, :]).astype(BF16)

    return local(body, [shape(total.shape, BF16)], total, got, weight, name="weigh")[0]


def fold(keep, recv, dtypes=(F32, BF16), base=0):
    n = recv.shape[0] // len(dtypes)

    def body(keep, recv, *outs):
        for i, out in enumerate(outs):
            mine = keep[base + i * n : base + (i + 1) * n]
            out[...] = (mine + recv[i * n : (i + 1) * n].astype(F32)).astype(out.dtype)

    return local(body, [shape((n,) + keep.shape[1:], t) for t in dtypes], keep, recv, name="fold")


def zeros(dims, after):
    def body(out):
        out[...] = jnp.zeros_like(out)

    return local(body, [shape(dims, F32)], name="zeros", after=after)[0]


def tiles_body(piece_count, src_row, dst_row, at, _, *refs):
    pieces = refs[:piece_count]
    first, second, acc, *sends, table = refs[piece_count:]
    count, rank, width = first.shape
    groups = count // GROUP
    join_body(*pieces, table)
    probes = table.shape[1]
    span = GROUP * rank
    row_tile = lax.broadcasted_iota(I32, (GROUP * probes, span), 0) // probes
    col_tile = lax.broadcasted_iota(I32, (GROUP * probes, span), 1) // rank
    component = lax.broadcasted_iota(I32, (GROUP * probes, span), 1) % rank
    own = jnp.where(row_tile == col_tile, component, rank)
    lane_tile = lax.broadcasted_iota(I32, (1, span), 1) // rank

    def inner_of(g):
        taken = jnp.concatenate(
            [table[at[src_row, g * GROUP + i]].astype(F32) for i in range(GROUP)], axis=0
        ).astype(BF16)
        left = first[g * GROUP : (g + 1) * GROUP].reshape(span, width)
        inner = lax.dot_general(taken, left, (((1,), (1,)), ((), ())), preferred_element_type=F32)
        limit = jnp.zeros((1, span), I32)
        for i in range(GROUP):
            limit = jnp.where(lane_tile == i, at[2, g * GROUP + i], limit)
        return jnp.where(own < limit, inner, 0.0).astype(BF16)

    def outer_of(g, kept):
        right = second[g * GROUP : (g + 1) * GROUP].reshape(span, width)
        return jnp.dot(kept, right, preferred_element_type=F32)

    def add(g, outer):
        for i in range(GROUP):
            to = at[dst_row, g * GROUP + i]
            acc[to] = acc[to] + outer[i * probes : (i + 1) * probes]

    kept, outer = {}, {}
    for step in range(groups + 2 * SKEW):
        if step >= 2 * SKEW:
            add(step - 2 * SKEW, outer.pop(step - 2 * SKEW))
        if 0 <= step - SKEW < groups:
            outer[step - SKEW] = outer_of(step - SKEW, kept.pop(step - SKEW))
        if step < groups:
            kept[step] = inner_of(step)
    base = acc.shape[0] // 2
    for send in sends:
        send[...] = acc[base : base + send.shape[0]].astype(send.dtype)
        base += send.shape[0]


def tiles(pieces, src_row, dst_row, table, first, second, acc, parts, send_dtype, name):
    count, rank, width = first.shape
    blocks, probes, _ = acc.shape
    rows = sum(piece.shape[0] for piece in pieces)

    def body(*refs):
        tiles_body(len(pieces), src_row, dst_row, *refs)

    return local(
        body,
        [shape(acc.shape, F32)] + [shape((blocks // 2 // parts, probes, width), send_dtype)] * parts,
        table,
        acc,
        *pieces,
        first,
        second,
        name=name,
        specs=[whole(pltpu.SMEM)] + [whole()] * (len(pieces) + 3),
        aliases={1: 0},
        flops=4 * count * rank * width * probes * GROUP,
        scratch=2 * rows * probes * width,
        scratches=[pltpu.VMEM((rows, probes, width), BF16)],
    )


def place(relative, order):
    at = jnp.zeros_like(relative)
    for k, bit in enumerate(order):
        at = at + jnp.where((relative & bit) != 0, 1 << k, 0)
    return at


def plan(owners, weight, orders, cell_blocks, station_blocks, after):
    peers, count = owners[0].shape
    rows = weight.shape[0] // peers
    rest = peers // 8
    half = cell_blocks // 2

    def body(*refs):
        far, weight_far, table_out, weight_near = refs[:5], refs[5], refs[6], refs[7]
        near, table, sems = refs[8:13], refs[13], refs[14]
        me = lax.axis_index("tile")
        pairs = list(zip(far, near))
        for k in range(rest):
            start = pl.multiple_of((k * 8 + (me & 7)) * rows, rows)
            pairs.append((weight_far.at[pl.ds(start, rows)], weight_near.at[pl.ds(k * rows, rows)]))
        fetch(pairs, sems)
        col_owner, col_local, row_owner, row_local, rank = [ref[pl.ds(me, 1), :] for ref in near]
        span = peers // 2
        away = col_owner ^ me
        is_q = col_local >= half
        spot = jnp.where(is_q, place(away, orders[1]) + (span - 1), place(away, orders[0]))
        table[0:1, :] = (away & 1) * (span * cell_blocks) + spot * half + col_local
        away = row_owner ^ me
        spot = (away & 1) * 4 + ((away & 4) // 2) + ((away & 2) // 2)
        table[1:2, :] = (spot * rest + row_owner // 8) * station_blocks + row_local
        table[2:3, :] = rank
        fetch([(table, table_out)], sems)

    return local(
        body,
        [shape((8, count), I32), shape((rest * rows, LANES), F32)],
        *owners,
        weight,
        name="plan",
        specs=[whole(pltpu.HBM)] * 6,
        out_specs=[whole(pltpu.SMEM), whole()],
        scratches=[pltpu.VMEM((peers, count), I32)] * 5
        + [pltpu.VMEM((8, count), I32), pltpu.SemaphoreType.DMA((5 + rest,))],
        after=after,
    )


def shards(
    probes,
    level_set,
    unit_label,
    contrast,
    station_weight,
    u_factor,
    v_factor,
    col_owner,
    col_local,
    row_owner,
    row_local,
    tile_rank,
):
    peers = lax.axis_size("tile")
    tile_count, _, station_width = u_factor.shape
    cell_width = v_factor.shape[2]
    probe_count, cell_total = probes.shape
    cell_blocks = cell_total // cell_width
    station_blocks = station_weight.shape[0] // (peers * station_width)
    bits = [1 << k for k in range(1, peers.bit_length() - 1)]
    far = bits[:0:-1]
    orders = (bits[:1] + far, far + bits[:1])

    lanes = (cell_total // LANES, LANES)
    half_dims = (cell_blocks // 2, probe_count, cell_width)
    part_p, part_q, scaling = local(
        scale_body,
        [shape(half_dims, BF16), shape(half_dims, BF16), shape(lanes, F32)],
        contrast,
        level_set.reshape(lanes),
        unit_label.reshape(lanes),
        probes,
        name="scale",
        specs=[whole(pltpu.HBM)] * 4,
        scratches=[
            pltpu.SMEM(contrast.shape, F32),
            pltpu.VMEM(lanes, F32),
            pltpu.VMEM(lanes, I32),
            pltpu.VMEM(probes.shape, F32),
            pltpu.SemaphoreType.DMA((4,)),
        ],
    )
    table, weight = plan(
        [a.reshape(peers, tile_count) for a in (col_owner, col_local, row_owner, row_local, tile_rank)],
        station_weight.reshape(-1, LANES),
        orders,
        cell_blocks,
        station_blocks,
        (scaling,),
    )
    steps = list(zip(*orders))
    early = swap(part_p, steps[1][0])
    for step, (bit_p, bit_q) in enumerate(steps):
        got_q = swap(part_q, bit_q)
        if step == 1:
            parts_p = (part_p, got_p, early, swap(got_p, bit_p))
            v_here, u_here = load((v_factor, u_factor), (part_q,))
            part_p = join(*parts_p, after=(u_here,))
        else:
            got_p = swap(part_p, bit_p)
        if step == 0:
            part_q = join(part_q, got_q, after=(weight,))
        elif step < len(steps) - 1:
            part_q = join(part_q, got_q)
            if step > 1:
                part_p = join(part_p, got_p)
    pieces = [part_p, got_p, part_q, got_q]
    pieces = pieces + [swap(piece, 1) for piece in pieces]

    acc = zeros((peers * station_blocks, probe_count, station_width), (part_p, part_q))
    total, *sends = tiles(pieces, 0, 1, table, v_here, u_here, acc, 4, F32, "forward")
    quarters = [0] * 4
    for k in SQUARE + (0,):
        kept = F32 if k == 0 else BF16
        quarters[k // 2] = fold(total, swap(sends[k // 2], 1), (kept,), base=k // 2 * sends[0].shape[0])[0]
    total, send = plus(quarters[0], *[swap(quarters[k // 2], k) for k in SQUARE])
    for bit in bits[2:-1]:
        total, send = plus(total, swap(send, bit))
    weighted = weigh(total, swap(send, bits[-1]), weight)
    gots = {k: swap(weighted, k) for k in SQUARE}
    around = join(gots[2], gots[4], gots[6])
    pieces = [weighted, around, swap(weighted, 1), swap(around, 1)]

    acc = zeros((peers * cell_blocks, probe_count, cell_width), (total,))
    total, send_p, send_q = tiles(pieces, 1, 0, table, u_here, v_here, acc, 2, BF16, "adjoint")
    keep_q, send_q = fold(total, swap(send_q, 1), base=total.shape[0] // 4)
    keep_p, send_p = fold(total, swap(send_p, 1))
    for step, (bit_p, bit_q) in enumerate(steps[::-1]):
        if step > 0:
            keep_q, send_q = fold(keep_q, got_q)
            keep_p, send_p = fold(keep_p, got_p)
        got_q = swap(send_q, bit_q)
        got_p = swap(send_p, bit_p)
    return local(
        final_body,
        [shape((probe_count, cell_total), F32)],
        keep_q,
        got_q,
        keep_p,
        got_p,
        scaling,
        name="final",
        out_specs=[whole(None)],
    )[0]


def solution(mesh):
    placed = (
        P(None, ("groups", "tile")),
        P(("groups", "tile")),
        P(("groups", "tile")),
        P("groups"),
        P("groups"),
        P(("groups", "tile"), None, None),
        P(("groups", "tile"), None, None),
        P("groups", None),
        P("groups"),
        P("groups", None),
        P("groups"),
        P("groups"),
    )
    return jax.shard_map(
        shards, mesh=mesh, in_specs=placed, out_specs=P(None, ("groups", "tile")), check_vma=False
    )
```

```python
import math

import jax
import jax.numpy as jnp
from jax import lax
from jax.experimental import pallas as pl
from jax.experimental.pallas import tpu as pltpu
from jax.sharding import PartitionSpec as P

BF16 = jnp.bfloat16
F32 = jnp.float32
I32 = jnp.int32
GROUP = 8
SKEW = 3
SQUARE = (6, 2, 4)
LANES = 128
MIB = 1024 * 1024


def whole(space=pltpu.VMEM):
    return pl.BlockSpec(memory_space=space)


def shape(dims, dtype):
    return jax.ShapeDtypeStruct(tuple(dims), dtype)


def size_of(array):
    return math.prod(array.shape) * jnp.dtype(array.dtype).itemsize


def swap(array, bits):
    count = lax.axis_size("tile")
    return lax.ppermute(array, "tile", [(i, i ^ bits) for i in range(count)])


def local(
    body, outs, *ins, name, scratch=0, scratches=(), specs=None, out_specs=None, flops=0, after=(), aliases=None
):
    nbytes = sum(size_of(a) for a in (*ins, *outs))
    specs = list(specs or [whole()] * len(ins)) + [whole()] * len(after)
    out_specs = list(out_specs or [whole()] * len(outs))
    own = len(ins)
    ins = [pltpu.with_memory_space_constraint(a, s.memory_space) for a, s in zip((*ins, *after), specs)]

    def run(*refs):
        body(*refs[:own], *refs[len(ins) :])

    return pl.pallas_call(
        run,
        out_shape=[a if s.memory_space is None else s.memory_space(a.shape, a.dtype) for a, s in zip(outs, out_specs)],
        in_specs=specs,
        out_specs=[whole() if s.memory_space is None else s for s in out_specs],
        input_output_aliases=aliases or {},
        scratch_shapes=list(scratches),
        compiler_params=pltpu.CompilerParams(vmem_limit_bytes=scratch + 8 * MIB),
        cost_estimate=pl.CostEstimate(flops=flops, bytes_accessed=nbytes, transcendentals=0),
        name=name,
    )(*ins)


def fetch(pairs, sems):
    copies = [pltpu.make_async_copy(a, b, sems.at[i]) for i, (a, b) in enumerate(pairs)]
    for copy in copies:
        copy.start()
    for copy in copies:
        copy.wait()


def load_body(source, out, sems):
    n = source.shape[0] // sems.shape[0]
    rows = [pl.ds(i * n, n) for i in range(sems.shape[0])]
    fetch([(source.at[r], out.at[r]) for r in rows], sems)


def load(array, after, name):
    return local(
        load_body,
        [shape(array.shape, array.dtype)],
        array,
        name=name,
        specs=[whole(pltpu.HBM)],
        scratches=[pltpu.SemaphoreType.DMA((8,))],
        after=after,
    )[0]


def scale_body(
    contrast, level, label, probes, part_p, part_q, scaling, contrast_near, level_near, label_near, probes_near, sems
):
    fetch(
        [(contrast, contrast_near), (level, level_near), (label, label_near), (probes, probes_near)],
        sems,
    )
    value = level_near[...]
    unit = label_near[...]
    factor = jnp.zeros_like(value)
    for k in range(contrast.shape[0]):
        factor = jnp.where(unit == k, contrast_near[k], factor)
    scaling[...] = factor / (1.0 + value * value)
    blocks, _, width = part_p.shape
    rows = width // LANES
    for half, part in enumerate((part_p, part_q)):
        for b in range(blocks):
            for c in range(rows):
                j = (half * blocks + b) * rows + c
                piece = probes_near[:, j * LANES : (j + 1) * LANES] * scaling[j : j + 1, :]
                part[b, :, c * LANES : (c + 1) * LANES] = piece.astype(BF16)


def final_body(keep_p, recv_p, keep_q, recv_q, scaling, out):
    blocks, _, width = keep_p.shape
    rows = width // LANES
    for half, (keep, recv) in enumerate(((keep_p, recv_p), (keep_q, recv_q))):
        for b in range(blocks):
            for c in range(rows):
                j = (half * blocks + b) * rows + c
                lanes = slice(c * LANES, (c + 1) * LANES)
                total = keep[b, :, lanes] + recv[b, :, lanes].astype(F32)
                out[:, j * LANES : (j + 1) * LANES] = total * scaling[j : j + 1, :]


def join_body(*refs):
    out, at = refs[-1], 0
    for ref in refs[:-1]:
        out[at : at + ref.shape[0]] = ref[...]
        at += ref.shape[0]


def join(*pieces, after=()):
    out = shape((sum(a.shape[0] for a in pieces),) + pieces[0].shape[1:], pieces[0].dtype)
    return local(join_body, [out], *pieces, name="join", after=after)[0]


def plus(total, *gots):
    def body(total, *refs):
        done = total[...]
        for ref in refs[:-2]:
            done = done + ref[...].astype(F32)
        refs[-2][...] = done
        refs[-1][...] = done.astype(BF16)

    return local(body, [shape(total.shape, F32), shape(total.shape, BF16)], total, *gots, name="plus")


def weigh(total, got, weight):
    def body(total, got, weight, out):
        blocks, _, width = out.shape
        rows = width // LANES
        for b in range(blocks):
            for c in range(rows):
                lanes = slice(c * LANES, (c + 1) * LANES)
                done = total[b, :, lanes] + got[b, :, lanes].astype(F32)
                j = b * rows + c
                out[b, :, lanes] = (done * weight[j : j + 1, :]).astype(BF16)

    return local(body, [shape(total.shape, BF16)], total, got, weight, name="weigh")[0]


def fold(keep, recv, dtypes=(F32, BF16), base=0):
    n = recv.shape[0] // len(dtypes)

    def body(keep, recv, *outs):
        for i, out in enumerate(outs):
            mine = keep[base + i * n : base + (i + 1) * n]
            out[...] = (mine + recv[i * n : (i + 1) * n].astype(F32)).astype(out.dtype)

    return local(body, [shape((n,) + keep.shape[1:], t) for t in dtypes], keep, recv, name="fold")


def zeros(dims, after):
    def body(out):
        out[...] = jnp.zeros_like(out)

    return local(body, [shape(dims, F32)], name="zeros", after=after)[0]


def tiles_body(piece_count, src_row, dst_row, at, _, *refs):
    pieces = refs[:piece_count]
    first, second, acc, *sends, table = refs[piece_count:]
    count, rank, width = first.shape
    groups = count // GROUP
    join_body(*pieces, table)
    probes = table.shape[1]
    span = GROUP * rank
    row_tile = lax.broadcasted_iota(I32, (GROUP * probes, span), 0) // probes
    col_tile = lax.broadcasted_iota(I32, (GROUP * probes, span), 1) // rank
    component = lax.broadcasted_iota(I32, (GROUP * probes, span), 1) % rank
    own = jnp.where(row_tile == col_tile, component, rank)
    lane_tile = lax.broadcasted_iota(I32, (1, span), 1) // rank

    def inner_of(g):
        taken = jnp.concatenate(
            [table[at[src_row, g * GROUP + i]].astype(F32) for i in range(GROUP)], axis=0
        ).astype(BF16)
        left = first[g * GROUP : (g + 1) * GROUP].reshape(span, width)
        inner = lax.dot_general(taken, left, (((1,), (1,)), ((), ())), preferred_element_type=F32)
        limit = jnp.zeros((1, span), I32)
        for i in range(GROUP):
            limit = jnp.where(lane_tile == i, at[2, g * GROUP + i], limit)
        return jnp.where(own < limit, inner, 0.0).astype(BF16)

    def outer_of(g, kept):
        right = second[g * GROUP : (g + 1) * GROUP].reshape(span, width)
        return jnp.dot(kept, right, preferred_element_type=F32)

    def add(g, outer):
        for i in range(GROUP):
            to = at[dst_row, g * GROUP + i]
            acc[to] = acc[to] + outer[i * probes : (i + 1) * probes]

    kept, outer = {}, {}
    for step in range(groups + 2 * SKEW):
        if step >= 2 * SKEW:
            add(step - 2 * SKEW, outer.pop(step - 2 * SKEW))
        if 0 <= step - SKEW < groups:
            outer[step - SKEW] = outer_of(step - SKEW, kept.pop(step - SKEW))
        if step < groups:
            kept[step] = inner_of(step)
    base = acc.shape[0] // 2
    for send in sends:
        send[...] = acc[base : base + send.shape[0]].astype(send.dtype)
        base += send.shape[0]


def tiles(pieces, src_row, dst_row, table, first, second, acc, parts, send_dtype, name):
    count, rank, width = first.shape
    blocks, probes, _ = acc.shape
    rows = sum(piece.shape[0] for piece in pieces)

    def body(*refs):
        tiles_body(len(pieces), src_row, dst_row, *refs)

    return local(
        body,
        [shape(acc.shape, F32)] + [shape((blocks // 2 // parts, probes, width), send_dtype)] * parts,
        table,
        acc,
        *pieces,
        first,
        second,
        name=name,
        specs=[whole(pltpu.SMEM)] + [whole()] * (len(pieces) + 3),
        aliases={1: 0},
        flops=4 * count * rank * width * probes * GROUP,
        scratch=2 * rows * probes * width,
        scratches=[pltpu.VMEM((rows, probes, width), BF16)],
    )


def place(relative, order):
    at = jnp.zeros_like(relative)
    for k, bit in enumerate(order):
        at = at + jnp.where((relative & bit) != 0, 1 << k, 0)
    return at


def plan(owners, weight, orders, cell_blocks, station_blocks, after):
    peers, count = owners[0].shape
    rows = weight.shape[0] // peers
    rest = peers // 8
    half = cell_blocks // 2

    def body(*refs):
        far, weight_far, table_out, weight_near = refs[:5], refs[5], refs[6], refs[7]
        near, table, sems = refs[8:13], refs[13], refs[14]
        me = lax.axis_index("tile")
        pairs = list(zip(far, near))
        for k in range(rest):
            start = pl.multiple_of((k * 8 + (me & 7)) * rows, rows)
            pairs.append((weight_far.at[pl.ds(start, rows)], weight_near.at[pl.ds(k * rows, rows)]))
        fetch(pairs, sems)
        col_owner, col_local, row_owner, row_local, rank = [ref[pl.ds(me, 1), :] for ref in near]
        span = peers // 2
        away = col_owner ^ me
        is_q = col_local >= half
        spot = jnp.where(is_q, place(away, orders[1]) + (span - 1), place(away, orders[0]))
        table[0:1, :] = (away & 1) * (span * cell_blocks) + spot * half + col_local
        away = row_owner ^ me
        spot = (away & 1) * 4 + ((away & 4) // 2) + ((away & 2) // 2)
        table[1:2, :] = (spot * rest + row_owner // 8) * station_blocks + row_local
        table[2:3, :] = rank
        fetch([(table, table_out)], sems)

    return local(
        body,
        [shape((8, count), I32), shape((rest * rows, LANES), F32)],
        *owners,
        weight,
        name="plan",
        specs=[whole(pltpu.HBM)] * 6,
        out_specs=[whole(pltpu.SMEM), whole()],
        scratches=[pltpu.VMEM((peers, count), I32)] * 5
        + [pltpu.VMEM((8, count), I32), pltpu.SemaphoreType.DMA((5 + rest,))],
        after=after,
    )


def shards(
    probes,
    level_set,
    unit_label,
    contrast,
    station_weight,
    u_factor,
    v_factor,
    col_owner,
    col_local,
    row_owner,
    row_local,
    tile_rank,
):
    peers = lax.axis_size("tile")
    tile_count, _, station_width = u_factor.shape
    cell_width = v_factor.shape[2]
    probe_count, cell_total = probes.shape
    cell_blocks = cell_total // cell_width
    station_blocks = station_weight.shape[0] // (peers * station_width)
    bits = [1 << k for k in range(1, peers.bit_length() - 1)]
    far = bits[:0:-1]
    orders = (far[:1] + bits[:1] + far[1:], far + bits[:1])

    lanes = (cell_total // LANES, LANES)
    half_dims = (cell_blocks // 2, probe_count, cell_width)
    part_p, part_q, scaling = local(
        scale_body,
        [shape(half_dims, BF16), shape(half_dims, BF16), shape(lanes, F32)],
        contrast,
        level_set.reshape(lanes),
        unit_label.reshape(lanes),
        probes,
        name="scale",
        specs=[whole(pltpu.HBM)] * 4,
        scratches=[
            pltpu.SMEM(contrast.shape, F32),
            pltpu.VMEM(lanes, F32),
            pltpu.VMEM(lanes, I32),
            pltpu.VMEM(probes.shape, F32),
            pltpu.SemaphoreType.DMA((4,)),
        ],
    )
    table, weight = plan(
        [a.reshape(peers, tile_count) for a in (col_owner, col_local, row_owner, row_local, tile_rank)],
        station_weight.reshape(-1, LANES),
        orders,
        cell_blocks,
        station_blocks,
        (scaling,),
    )
    steps = list(zip(*orders))
    after = (weight,)
    for step, (bit_p, bit_q) in enumerate(steps):
        got_p = swap(part_p, bit_p)
        got_q = swap(part_q, bit_q)
        if step == 1:
            v_here = load(v_factor, (part_p, part_q), "load_v")
            u_here = load(u_factor, (part_p, part_q, v_here), "load_u")
            after = (u_here,)
        if step < len(steps) - 1:
            part_p = join(part_p, got_p, after=after)
            part_q = join(part_q, got_q)
            after = ()
    pieces = [part_p, got_p, part_q, got_q]
    pieces = pieces + [swap(piece, 1) for piece in pieces]

    acc = zeros((peers * station_blocks, probe_count, station_width), (part_p, part_q))
    total, *sends = tiles(pieces, 0, 1, table, v_here, u_here, acc, 4, F32, "forward")
    quarters = [0] * 4
    for k in SQUARE + (0,):
        kept = F32 if k == 0 else BF16
        quarters[k // 2] = fold(total, swap(sends[k // 2], 1), (kept,), base=k // 2 * sends[0].shape[0])[0]
    total, send = plus(quarters[0], *[swap(quarters[k // 2], k) for k in SQUARE])
    for bit in bits[2:-1]:
        total, send = plus(total, swap(send, bit))
    weighted = weigh(total, swap(send, bits[-1]), weight)
    gots = {k: swap(weighted, k) for k in SQUARE}
    around = join(gots[2], gots[4], gots[6])
    pieces = [weighted, around, swap(weighted, 1), swap(around, 1)]

    acc = zeros((peers * cell_blocks, probe_count, cell_width), (total,))
    total, send_p, send_q = tiles(pieces, 1, 0, table, u_here, v_here, acc, 2, BF16, "adjoint")
    keep_p, send_p = fold(total, swap(send_p, 1))
    keep_q, send_q = fold(total, swap(send_q, 1), base=total.shape[0] // 4)
    for step, (bit_p, bit_q) in enumerate(steps[::-1]):
        if step > 0:
            keep_p, send_p = fold(keep_p, got_p)
            keep_q, send_q = fold(keep_q, got_q)
        got_p = swap(send_p, bit_p)
        got_q = swap(send_q, bit_q)
    return local(
        final_body,
        [shape((probe_count, cell_total), F32)],
        keep_p,
        got_p,
        keep_q,
        got_q,
        scaling,
        name="final",
        out_specs=[whole(None)],
    )[0]


def solution(mesh):
    placed = (
        P(None, ("groups", "tile")),
        P(("groups", "tile")),
        P(("groups", "tile")),
        P("groups"),
        P("groups"),
        P(("groups", "tile"), None, None),
        P(("groups", "tile"), None, None),
        P("groups", None),
        P("groups"),
        P("groups", None),
        P("groups"),
        P("groups"),
    )
    return jax.shard_map(
        shards, mesh=mesh, in_specs=placed, out_specs=P(None, ("groups", "tile")), check_vma=False
    )
```

```python
import math

import jax
import jax.numpy as jnp
from jax import lax
from jax.experimental import pallas as pl
from jax.experimental.pallas import tpu as pltpu
from jax.sharding import PartitionSpec as P

BF16 = jnp.bfloat16
F32 = jnp.float32
I32 = jnp.int32
GROUP = 8
SKEW = 3
SQUARE = (6, 2, 4)
LANES = 128
MIB = 1024 * 1024


def whole(space=pltpu.VMEM):
    return pl.BlockSpec(memory_space=space)


def shape(dims, dtype):
    return jax.ShapeDtypeStruct(tuple(dims), dtype)


def size_of(array):
    return math.prod(array.shape) * jnp.dtype(array.dtype).itemsize


def swap(array, bits):
    count = lax.axis_size("tile")
    return lax.ppermute(array, "tile", [(i, i ^ bits) for i in range(count)])


def local(
    body, outs, *ins, name, scratch=0, scratches=(), specs=None, out_specs=None, flops=0, after=(), aliases=None
):
    nbytes = sum(size_of(a) for a in (*ins, *outs))
    specs = list(specs or [whole()] * len(ins)) + [whole()] * len(after)
    out_specs = list(out_specs or [whole()] * len(outs))
    own = len(ins)
    ins = [pltpu.with_memory_space_constraint(a, s.memory_space) for a, s in zip((*ins, *after), specs)]

    def run(*refs):
        body(*refs[:own], *refs[len(ins) :])

    return pl.pallas_call(
        run,
        out_shape=[a if s.memory_space is None else s.memory_space(a.shape, a.dtype) for a, s in zip(outs, out_specs)],
        in_specs=specs,
        out_specs=[whole() if s.memory_space is None else s for s in out_specs],
        input_output_aliases=aliases or {},
        scratch_shapes=list(scratches),
        compiler_params=pltpu.CompilerParams(vmem_limit_bytes=scratch + 8 * MIB),
        cost_estimate=pl.CostEstimate(flops=flops, bytes_accessed=nbytes, transcendentals=0),
        name=name,
    )(*ins)


def fetch(pairs, sems):
    copies = [pltpu.make_async_copy(a, b, sems.at[i]) for i, (a, b) in enumerate(pairs)]
    for copy in copies:
        copy.start()
    for copy in copies:
        copy.wait()


def load_body(source, out, sems):
    n = source.shape[0] // sems.shape[0]
    rows = [pl.ds(i * n, n) for i in range(sems.shape[0])]
    fetch([(source.at[r], out.at[r]) for r in rows], sems)


def load(array, after, name):
    return local(
        load_body,
        [shape(array.shape, array.dtype)],
        array,
        name=name,
        specs=[whole(pltpu.HBM)],
        scratches=[pltpu.SemaphoreType.DMA((8,))],
        after=after,
    )[0]


def scale_body(
    contrast, level, label, probes, part_p, part_q, scaling, contrast_near, level_near, label_near, probes_near, sems
):
    fetch(
        [(contrast, contrast_near), (level, level_near), (label, label_near), (probes, probes_near)],
        sems,
    )
    value = level_near[...]
    unit = label_near[...]
    factor = jnp.zeros_like(value)
    for k in range(contrast.shape[0]):
        factor = jnp.where(unit == k, contrast_near[k], factor)
    scaling[...] = factor / (1.0 + value * value)
    blocks, _, width = part_p.shape
    rows = width // LANES
    for half, part in enumerate((part_p, part_q)):
        for b in range(blocks):
            for c in range(rows):
                j = (half * blocks + b) * rows + c
                piece = probes_near[:, j * LANES : (j + 1) * LANES] * scaling[j : j + 1, :]
                part[b, :, c * LANES : (c + 1) * LANES] = piece.astype(BF16)


def final_body(keep_p, recv_p, keep_q, recv_q, scaling, out):
    blocks, _, width = keep_p.shape
    rows = width // LANES
    for half, (keep, recv) in enumerate(((keep_p, recv_p), (keep_q, recv_q))):
        for b in range(blocks):
            for c in range(rows):
                j = (half * blocks + b) * rows + c
                lanes = slice(c * LANES, (c + 1) * LANES)
                total = keep[b, :, lanes] + recv[b, :, lanes].astype(F32)
                out[:, j * LANES : (j + 1) * LANES] = total * scaling[j : j + 1, :]


def join_body(*refs):
    out, at = refs[-1], 0
    for ref in refs[:-1]:
        out[at : at + ref.shape[0]] = ref[...]
        at += ref.shape[0]


def join(*pieces, after=()):
    out = shape((sum(a.shape[0] for a in pieces),) + pieces[0].shape[1:], pieces[0].dtype)
    return local(join_body, [out], *pieces, name="join", after=after)[0]


def plus(total, *gots):
    def body(total, *refs):
        done = total[...]
        for ref in refs[:-2]:
            done = done + ref[...].astype(F32)
        refs[-2][...] = done
        refs[-1][...] = done.astype(BF16)

    return local(body, [shape(total.shape, F32), shape(total.shape, BF16)], total, *gots, name="plus")


def weigh(total, got, weight):
    def body(total, got, weight, out):
        blocks, _, width = out.shape
        rows = width // LANES
        for b in range(blocks):
            for c in range(rows):
                lanes = slice(c * LANES, (c + 1) * LANES)
                done = total[b, :, lanes] + got[b, :, lanes].astype(F32)
                j = b * rows + c
                out[b, :, lanes] = (done * weight[j : j + 1, :]).astype(BF16)

    return local(body, [shape(total.shape, BF16)], total, got, weight, name="weigh")[0]


def fold(keep, recv, dtypes=(F32, BF16), base=0):
    n = recv.shape[0] // len(dtypes)

    def body(keep, recv, *outs):
        for i, out in enumerate(outs):
            mine = keep[base + i * n : base + (i + 1) * n]
            out[...] = (mine + recv[i * n : (i + 1) * n].astype(F32)).astype(out.dtype)

    return local(body, [shape((n,) + keep.shape[1:], t) for t in dtypes], keep, recv, name="fold")


def zeros(dims, after):
    def body(out):
        out[...] = jnp.zeros_like(out)

    return local(body, [shape(dims, F32)], name="zeros", after=after)[0]


def tiles_body(piece_count, src_row, dst_row, at, _, *refs):
    pieces = refs[:piece_count]
    first, second, acc, *sends, table = refs[piece_count:]
    count, rank, width = first.shape
    groups = count // GROUP
    join_body(*pieces, table)
    probes = table.shape[1]
    span = GROUP * rank
    row_tile = lax.broadcasted_iota(I32, (GROUP * probes, span), 0) // probes
    col_tile = lax.broadcasted_iota(I32, (GROUP * probes, span), 1) // rank
    component = lax.broadcasted_iota(I32, (GROUP * probes, span), 1) % rank
    own = jnp.where(row_tile == col_tile, component, rank)
    lane_tile = lax.broadcasted_iota(I32, (1, span), 1) // rank

    def inner_of(g):
        taken = jnp.concatenate(
            [table[at[src_row, g * GROUP + i]].astype(F32) for i in range(GROUP)], axis=0
        ).astype(BF16)
        left = first[g * GROUP : (g + 1) * GROUP].reshape(span, width)
        inner = lax.dot_general(taken, left, (((1,), (1,)), ((), ())), preferred_element_type=F32)
        limit = jnp.zeros((1, span), I32)
        for i in range(GROUP):
            limit = jnp.where(lane_tile == i, at[2, g * GROUP + i], limit)
        return jnp.where(own < limit, inner, 0.0).astype(BF16)

    def outer_of(g, kept):
        right = second[g * GROUP : (g + 1) * GROUP].reshape(span, width)
        return jnp.dot(kept, right, preferred_element_type=F32)

    def add(g, outer):
        for i in range(GROUP):
            to = at[dst_row, g * GROUP + i]
            acc[to] = acc[to] + outer[i * probes : (i + 1) * probes]

    kept, outer = {}, {}
    for step in range(groups + 2 * SKEW):
        if step >= 2 * SKEW:
            add(step - 2 * SKEW, outer.pop(step - 2 * SKEW))
        if 0 <= step - SKEW < groups:
            outer[step - SKEW] = outer_of(step - SKEW, kept.pop(step - SKEW))
        if step < groups:
            kept[step] = inner_of(step)
    base = acc.shape[0] // 2
    for send in sends:
        send[...] = acc[base : base + send.shape[0]].astype(send.dtype)
        base += send.shape[0]


def tiles(pieces, src_row, dst_row, table, first, second, acc, parts, send_dtype, name):
    count, rank, width = first.shape
    blocks, probes, _ = acc.shape
    rows = sum(piece.shape[0] for piece in pieces)

    def body(*refs):
        tiles_body(len(pieces), src_row, dst_row, *refs)

    return local(
        body,
        [shape(acc.shape, F32)] + [shape((blocks // 2 // parts, probes, width), send_dtype)] * parts,
        table,
        acc,
        *pieces,
        first,
        second,
        name=name,
        specs=[whole(pltpu.SMEM)] + [whole()] * (len(pieces) + 3),
        aliases={1: 0},
        flops=4 * count * rank * width * probes * GROUP,
        scratch=2 * rows * probes * width,
        scratches=[pltpu.VMEM((rows, probes, width), BF16)],
    )


def place(relative, order):
    at = jnp.zeros_like(relative)
    for k, bit in enumerate(order):
        at = at + jnp.where((relative & bit) != 0, 1 << k, 0)
    return at


def plan(owners, weight, orders, cell_blocks, station_blocks, after):
    peers, count = owners[0].shape
    rows = weight.shape[0] // peers
    rest = peers // 8
    half = cell_blocks // 2

    def body(*refs):
        far, weight_far, table_out, weight_near = refs[:5], refs[5], refs[6], refs[7]
        near, table, sems = refs[8:13], refs[13], refs[14]
        me = lax.axis_index("tile")
        pairs = list(zip(far, near))
        for k in range(rest):
            start = pl.multiple_of((k * 8 + (me & 7)) * rows, rows)
            pairs.append((weight_far.at[pl.ds(start, rows)], weight_near.at[pl.ds(k * rows, rows)]))
        fetch(pairs, sems)
        col_owner, col_local, row_owner, row_local, rank = [ref[pl.ds(me, 1), :] for ref in near]
        span = peers // 2
        away = col_owner ^ me
        is_q = col_local >= half
        for row, (order_p, order_q) in zip((0, 3), orders):
            spot = jnp.where(is_q, place(away, order_q) + (span - 1), place(away, order_p))
            table[row : row + 1, :] = (away & 1) * (span * cell_blocks) + spot * half + col_local
        away = row_owner ^ me
        spot = (away & 1) * 4 + ((away & 4) // 2) + ((away & 2) // 2)
        table[1:2, :] = (spot * rest + row_owner // 8) * station_blocks + row_local
        table[2:3, :] = rank
        fetch([(table, table_out)], sems)

    return local(
        body,
        [shape((8, count), I32), shape((rest * rows, LANES), F32)],
        *owners,
        weight,
        name="plan",
        specs=[whole(pltpu.HBM)] * 6,
        out_specs=[whole(pltpu.SMEM), whole()],
        scratches=[pltpu.VMEM((peers, count), I32)] * 5
        + [pltpu.VMEM((8, count), I32), pltpu.SemaphoreType.DMA((5 + rest,))],
        after=after,
    )


def shards(
    probes,
    level_set,
    unit_label,
    contrast,
    station_weight,
    u_factor,
    v_factor,
    col_owner,
    col_local,
    row_owner,
    row_local,
    tile_rank,
):
    peers = lax.axis_size("tile")
    tile_count, _, station_width = u_factor.shape
    cell_width = v_factor.shape[2]
    probe_count, cell_total = probes.shape
    cell_blocks = cell_total // cell_width
    station_blocks = station_weight.shape[0] // (peers * station_width)
    bits = [1 << k for k in range(1, peers.bit_length() - 1)]
    far = bits[:0:-1]
    gather = (bits[:1] + far, far + bits[:1])
    scatter = (far[:1] + bits[:1] + far[1:], far + bits[:1])

    lanes = (cell_total // LANES, LANES)
    half_dims = (cell_blocks // 2, probe_count, cell_width)
    part_p, part_q, scaling = local(
        scale_body,
        [shape(half_dims, BF16), shape(half_dims, BF16), shape(lanes, F32)],
        contrast,
        level_set.reshape(lanes),
        unit_label.reshape(lanes),
        probes,
        name="scale",
        specs=[whole(pltpu.HBM)] * 4,
        scratches=[
            pltpu.SMEM(contrast.shape, F32),
            pltpu.VMEM(lanes, F32),
            pltpu.VMEM(lanes, I32),
            pltpu.VMEM(probes.shape, F32),
            pltpu.SemaphoreType.DMA((4,)),
        ],
    )
    table, weight = plan(
        [a.reshape(peers, tile_count) for a in (col_owner, col_local, row_owner, row_local, tile_rank)],
        station_weight.reshape(-1, LANES),
        (gather, scatter),
        cell_blocks,
        station_blocks,
        (scaling,),
    )
    steps = list(zip(*gather))
    after = (weight,)
    for step, (bit_p, bit_q) in enumerate(steps):
        got_p = swap(part_p, bit_p)
        got_q = swap(part_q, bit_q)
        if step == 1:
            v_here = load(v_factor, (part_p, part_q), "load_v")
            u_here = load(u_factor, (part_p, part_q, v_here), "load_u")
            after = (u_here,)
        if step < len(steps) - 1:
            part_p = join(part_p, got_p, after=after)
            part_q = join(part_q, got_q)
            after = ()
    pieces = [part_p, got_p, part_q, got_q]
    pieces = pieces + [swap(piece, 1) for piece in pieces]

    acc = zeros((peers * station_blocks, probe_count, station_width), (part_p, part_q))
    total, *sends = tiles(pieces, 0, 1, table, v_here, u_here, acc, 4, F32, "forward")
    quarters = [0] * 4
    for k in SQUARE + (0,):
        kept = F32 if k == 0 else BF16
        quarters[k // 2] = fold(total, swap(sends[k // 2], 1), (kept,), base=k // 2 * sends[0].shape[0])[0]
    total, send = plus(quarters[0], *[swap(quarters[k // 2], k) for k in SQUARE])
    for bit in bits[2:-1]:
        total, send = plus(total, swap(send, bit))
    weighted = weigh(total, swap(send, bits[-1]), weight)
    gots = {k: swap(weighted, k) for k in SQUARE}
    around = join(gots[2], gots[4], gots[6])
    pieces = [weighted, around, swap(weighted, 1), swap(around, 1)]

    acc = zeros((peers * cell_blocks, probe_count, cell_width), (total,))
    total, send_p, send_q = tiles(pieces, 1, 3, table, u_here, v_here, acc, 2, BF16, "adjoint")
    keep_p, send_p = fold(total, swap(send_p, 1))
    keep_q, send_q = fold(total, swap(send_q, 1), base=total.shape[0] // 4)
    for step, (bit_p, bit_q) in enumerate(list(zip(*scatter))[::-1]):
        if step > 0:
            keep_p, send_p = fold(keep_p, got_p)
            keep_q, send_q = fold(keep_q, got_q)
        got_p = swap(send_p, bit_p)
        got_q = swap(send_q, bit_q)
    return local(
        final_body,
        [shape((probe_count, cell_total), F32)],
        keep_p,
        got_p,
        keep_q,
        got_q,
        scaling,
        name="final",
        out_specs=[whole(None)],
    )[0]


def solution(mesh):
    placed = (
        P(None, ("groups", "tile")),
        P(("groups", "tile")),
        P(("groups", "tile")),
        P("groups"),
        P("groups"),
        P(("groups", "tile"), None, None),
        P(("groups", "tile"), None, None),
        P("groups", None),
        P("groups"),
        P("groups", None),
        P("groups"),
        P("groups"),
    )
    return jax.shard_map(
        shards, mesh=mesh, in_specs=placed, out_specs=P(None, ("groups", "tile")), check_vma=False
    )
```

```python
import math

import jax
import jax.numpy as jnp
from jax import lax
from jax.experimental import pallas as pl
from jax.experimental.pallas import tpu as pltpu
from jax.sharding import PartitionSpec as P

BF16 = jnp.bfloat16
F32 = jnp.float32
I32 = jnp.int32
GROUP = 8
SKEW = 3
SQUARE = (6, 2, 4)
LANES = 128
MIB = 1024 * 1024


def whole(space=pltpu.VMEM):
    return pl.BlockSpec(memory_space=space)


def shape(dims, dtype):
    return jax.ShapeDtypeStruct(tuple(dims), dtype)


def size_of(array):
    return math.prod(array.shape) * jnp.dtype(array.dtype).itemsize


def swap(array, bits):
    count = lax.axis_size("tile")
    return lax.ppermute(array, "tile", [(i, i ^ bits) for i in range(count)])


def local(
    body, outs, *ins, name, scratch=0, scratches=(), specs=None, out_specs=None, flops=0, after=(), aliases=None
):
    nbytes = sum(size_of(a) for a in (*ins, *outs))
    specs = list(specs or [whole()] * len(ins)) + [whole()] * len(after)
    out_specs = list(out_specs or [whole()] * len(outs))
    own = len(ins)
    ins = [pltpu.with_memory_space_constraint(a, s.memory_space) for a, s in zip((*ins, *after), specs)]

    def run(*refs):
        body(*refs[:own], *refs[len(ins) :])

    return pl.pallas_call(
        run,
        out_shape=[a if s.memory_space is None else s.memory_space(a.shape, a.dtype) for a, s in zip(outs, out_specs)],
        in_specs=specs,
        out_specs=[whole() if s.memory_space is None else s for s in out_specs],
        input_output_aliases=aliases or {},
        scratch_shapes=list(scratches),
        compiler_params=pltpu.CompilerParams(vmem_limit_bytes=scratch + 8 * MIB),
        cost_estimate=pl.CostEstimate(flops=flops, bytes_accessed=nbytes, transcendentals=0),
        name=name,
    )(*ins)


def fetch(pairs, sems):
    copies = [pltpu.make_async_copy(a, b, sems.at[i]) for i, (a, b) in enumerate(pairs)]
    for copy in copies:
        copy.start()
    for copy in copies:
        copy.wait()


def load_body(source, out, sems):
    n = source.shape[0] // sems.shape[0]
    rows = [pl.ds(i * n, n) for i in range(sems.shape[0])]
    fetch([(source.at[r], out.at[r]) for r in rows], sems)


def load(array, after, name):
    return local(
        load_body,
        [shape(array.shape, array.dtype)],
        array,
        name=name,
        specs=[whole(pltpu.HBM)],
        scratches=[pltpu.SemaphoreType.DMA((8,))],
        after=after,
    )[0]


def scale_body(
    contrast, level, label, probes, part_p, part_q, scaling, contrast_near, level_near, label_near, probes_near, sems
):
    fetch(
        [(contrast, contrast_near), (level, level_near), (label, label_near), (probes, probes_near)],
        sems,
    )
    value = level_near[...]
    unit = label_near[...]
    factor = jnp.zeros_like(value)
    for k in range(contrast.shape[0]):
        factor = jnp.where(unit == k, contrast_near[k], factor)
    scaling[...] = factor / (1.0 + value * value)
    blocks, _, width = part_p.shape
    rows = width // LANES
    for half, part in enumerate((part_p, part_q)):
        for b in range(blocks):
            for c in range(rows):
                j = (half * blocks + b) * rows + c
                piece = probes_near[:, j * LANES : (j + 1) * LANES] * scaling[j : j + 1, :]
                part[b, :, c * LANES : (c + 1) * LANES] = piece.astype(BF16)


def final_body(keep_p, recv_p, keep_q, recv_q, scaling, out):
    blocks, _, width = keep_p.shape
    rows = width // LANES
    for half, (keep, recv) in enumerate(((keep_p, recv_p), (keep_q, recv_q))):
        for b in range(blocks):
            for c in range(rows):
                j = (half * blocks + b) * rows + c
                lanes = slice(c * LANES, (c + 1) * LANES)
                total = keep[b, :, lanes] + recv[b, :, lanes].astype(F32)
                out[:, j * LANES : (j + 1) * LANES] = total * scaling[j : j + 1, :]


def join_body(*refs):
    out, at = refs[-1], 0
    for ref in refs[:-1]:
        out[at : at + ref.shape[0]] = ref[...]
        at += ref.shape[0]


def join(*pieces, after=()):
    out = shape((sum(a.shape[0] for a in pieces),) + pieces[0].shape[1:], pieces[0].dtype)
    return local(join_body, [out], *pieces, name="join", after=after)[0]


def plus(total, *gots):
    def body(total, *refs):
        done = total[...]
        for ref in refs[:-2]:
            done = done + ref[...].astype(F32)
        refs[-2][...] = done
        refs[-1][...] = done.astype(BF16)

    return local(body, [shape(total.shape, F32), shape(total.shape, BF16)], total, *gots, name="plus")


def weigh(total, got, weight):
    def body(total, got, weight, out):
        blocks, _, width = out.shape
        rows = width // LANES
        for b in range(blocks):
            for c in range(rows):
                lanes = slice(c * LANES, (c + 1) * LANES)
                done = total[b, :, lanes] + got[b, :, lanes].astype(F32)
                j = b * rows + c
                out[b, :, lanes] = (done * weight[j : j + 1, :]).astype(BF16)

    return local(body, [shape(total.shape, BF16)], total, got, weight, name="weigh")[0]


def fold(keep, recv, dtypes=(F32, BF16), base=0):
    n = recv.shape[0] // len(dtypes)

    def body(keep, recv, *outs):
        for i, out in enumerate(outs):
            mine = keep[base + i * n : base + (i + 1) * n]
            out[...] = (mine + recv[i * n : (i + 1) * n].astype(F32)).astype(out.dtype)

    return local(body, [shape((n,) + keep.shape[1:], t) for t in dtypes], keep, recv, name="fold")


def zeros(dims, after):
    def body(out):
        out[...] = jnp.zeros_like(out)

    return local(body, [shape(dims, F32)], name="zeros", after=after)[0]


def tiles_body(piece_count, src_row, dst_row, at, _, *refs):
    pieces = refs[:piece_count]
    first, second, acc, *sends, table = refs[piece_count:]
    count, rank, width = first.shape
    groups = count // GROUP
    join_body(*pieces, table)
    probes = table.shape[1]
    span = GROUP * rank
    row_tile = lax.broadcasted_iota(I32, (GROUP * probes, span), 0) // probes
    col_tile = lax.broadcasted_iota(I32, (GROUP * probes, span), 1) // rank
    component = lax.broadcasted_iota(I32, (GROUP * probes, span), 1) % rank
    own = jnp.where(row_tile == col_tile, component, rank)
    lane_tile = lax.broadcasted_iota(I32, (1, span), 1) // rank

    def inner_of(g):
        taken = jnp.concatenate(
            [table[at[src_row, g * GROUP + i]].astype(F32) for i in range(GROUP)], axis=0
        ).astype(BF16)
        left = first[g * GROUP : (g + 1) * GROUP].reshape(span, width)
        inner = lax.dot_general(taken, left, (((1,), (1,)), ((), ())), preferred_element_type=F32)
        limit = jnp.zeros((1, span), I32)
        for i in range(GROUP):
            limit = jnp.where(lane_tile == i, at[2, g * GROUP + i], limit)
        return jnp.where(own < limit, inner, 0.0).astype(BF16)

    def outer_of(g, kept):
        right = second[g * GROUP : (g + 1) * GROUP].reshape(span, width)
        return jnp.dot(kept, right, preferred_element_type=F32)

    def add(g, outer):
        for i in range(GROUP):
            to = at[dst_row, g * GROUP + i]
            acc[to] = acc[to] + outer[i * probes : (i + 1) * probes]

    kept, outer = {}, {}
    for step in range(groups + 2 * SKEW):
        if step >= 2 * SKEW:
            add(step - 2 * SKEW, outer.pop(step - 2 * SKEW))
        if 0 <= step - SKEW < groups:
            outer[step - SKEW] = outer_of(step - SKEW, kept.pop(step - SKEW))
        if step < groups:
            kept[step] = inner_of(step)
    base = acc.shape[0] // 2
    for send in sends:
        send[...] = acc[base : base + send.shape[0]].astype(send.dtype)
        base += send.shape[0]


def tiles(pieces, src_row, dst_row, table, first, second, acc, parts, send_dtype, name):
    count, rank, width = first.shape
    blocks, probes, _ = acc.shape
    rows = sum(piece.shape[0] for piece in pieces)

    def body(*refs):
        tiles_body(len(pieces), src_row, dst_row, *refs)

    return local(
        body,
        [shape(acc.shape, F32)] + [shape((blocks // 2 // parts, probes, width), send_dtype)] * parts,
        table,
        acc,
        *pieces,
        first,
        second,
        name=name,
        specs=[whole(pltpu.SMEM)] + [whole()] * (len(pieces) + 3),
        aliases={1: 0},
        flops=4 * count * rank * width * probes * GROUP,
        scratch=2 * rows * probes * width,
        scratches=[pltpu.VMEM((rows, probes, width), BF16)],
    )


def place(relative, order):
    at = jnp.zeros_like(relative)
    for k, bit in enumerate(order):
        at = at + jnp.where((relative & bit) != 0, 1 << k, 0)
    return at


def plan(owners, weight, orders, cell_blocks, station_blocks, after):
    peers, count = owners[0].shape
    rows = weight.shape[0] // peers
    rest = peers // 8
    half = cell_blocks // 2

    def body(*refs):
        far, weight_far, table_out, weight_near = refs[:5], refs[5], refs[6], refs[7]
        near, table, sems = refs[8:13], refs[13], refs[14]
        me = lax.axis_index("tile")
        pairs = list(zip(far, near))
        for k in range(rest):
            start = pl.multiple_of((k * 8 + (me & 7)) * rows, rows)
            pairs.append((weight_far.at[pl.ds(start, rows)], weight_near.at[pl.ds(k * rows, rows)]))
        fetch(pairs, sems)
        col_owner, col_local, row_owner, row_local, rank = [ref[pl.ds(me, 1), :] for ref in near]
        span = peers // 2
        away = col_owner ^ me
        is_q = col_local >= half
        for row, (order_p, order_q) in zip((0, 3), orders):
            spot = jnp.where(is_q, place(away, order_q) + (span - 1), place(away, order_p))
            table[row : row + 1, :] = (away & 1) * (span * cell_blocks) + spot * half + col_local
        away = row_owner ^ me
        spot = (away & 1) * 4 + ((away & 4) // 2) + ((away & 2) // 2)
        table[1:2, :] = (spot * rest + row_owner // 8) * station_blocks + row_local
        table[2:3, :] = rank
        fetch([(table, table_out)], sems)

    return local(
        body,
        [shape((8, count), I32), shape((rest * rows, LANES), F32)],
        *owners,
        weight,
        name="plan",
        specs=[whole(pltpu.HBM)] * 6,
        out_specs=[whole(pltpu.SMEM), whole()],
        scratches=[pltpu.VMEM((peers, count), I32)] * 5
        + [pltpu.VMEM((8, count), I32), pltpu.SemaphoreType.DMA((5 + rest,))],
        after=after,
    )


def shards(
    probes,
    level_set,
    unit_label,
    contrast,
    station_weight,
    u_factor,
    v_factor,
    col_owner,
    col_local,
    row_owner,
    row_local,
    tile_rank,
):
    peers = lax.axis_size("tile")
    tile_count, _, station_width = u_factor.shape
    cell_width = v_factor.shape[2]
    probe_count, cell_total = probes.shape
    cell_blocks = cell_total // cell_width
    station_blocks = station_weight.shape[0] // (peers * station_width)
    bits = [1 << k for k in range(1, peers.bit_length() - 1)]
    far = bits[:0:-1]
    gather = (bits[:1] + far, far + bits[:1])
    scatter = (far[:1] + bits[:1] + far[1:], far + bits[:1])

    lanes = (cell_total // LANES, LANES)
    half_dims = (cell_blocks // 2, probe_count, cell_width)
    part_p, part_q, scaling = local(
        scale_body,
        [shape(half_dims, BF16), shape(half_dims, BF16), shape(lanes, F32)],
        contrast,
        level_set.reshape(lanes),
        unit_label.reshape(lanes),
        probes,
        name="scale",
        specs=[whole(pltpu.HBM)] * 4,
        scratches=[
            pltpu.SMEM(contrast.shape, F32),
            pltpu.VMEM(lanes, F32),
            pltpu.VMEM(lanes, I32),
            pltpu.VMEM(probes.shape, F32),
            pltpu.SemaphoreType.DMA((4,)),
        ],
    )
    table, weight = plan(
        [a.reshape(peers, tile_count) for a in (col_owner, col_local, row_owner, row_local, tile_rank)],
        station_weight.reshape(-1, LANES),
        (gather, scatter),
        cell_blocks,
        station_blocks,
        (scaling,),
    )
    steps = list(zip(*gather))
    after = (weight,)
    for step, (bit_p, bit_q) in enumerate(steps):
        got_p = swap(part_p, bit_p)
        got_q = swap(part_q, bit_q)
        if step == 1:
            v_here = load(v_factor, (part_p, part_q), "load_v")
            u_here = load(u_factor, (part_p, part_q, v_here), "load_u")
            after = (u_here,)
        if step < len(steps) - 1:
            part_p = join(part_p, got_p, after=after)
            part_q = join(part_q, got_q)
            after = ()
    pieces = [part_p, got_p, part_q, got_q]
    pieces = pieces + [swap(piece, 1) for piece in pieces]

    acc = zeros((peers * station_blocks, probe_count, station_width), (part_p, part_q))
    total, *sends = tiles(pieces, 0, 1, table, v_here, u_here, acc, 4, F32, "forward")
    quarters = [0] * 4
    for k in SQUARE + (0,):
        kept = F32 if k == 0 else BF16
        quarters[k // 2] = fold(total, swap(sends[k // 2], 1), (kept,), base=k // 2 * sends[0].shape[0])[0]
    total, send = plus(quarters[0], *[swap(quarters[k // 2], k) for k in SQUARE])
    for bit in bits[2:-1]:
        total, send = plus(total, swap(send, bit))
    weighted = weigh(total, swap(send, bits[-1]), weight)
    gots = {k: swap(weighted, k) for k in SQUARE}
    around = join(weighted, gots[2], gots[4], gots[6])
    pieces = [around, swap(around, 1)]

    acc = zeros((peers * cell_blocks, probe_count, cell_width), (total,))
    total, send_p, send_q = tiles(pieces, 1, 3, table, u_here, v_here, acc, 2, BF16, "adjoint")
    keep_p, send_p = fold(total, swap(send_p, 1))
    keep_q, send_q = fold(total, swap(send_q, 1), base=total.shape[0] // 4)
    for step, (bit_p, bit_q) in enumerate(list(zip(*scatter))[::-1]):
        if step > 0:
            keep_p, send_p = fold(keep_p, got_p)
            keep_q, send_q = fold(keep_q, got_q)
        got_p = swap(send_p, bit_p)
        got_q = swap(send_q, bit_q)
    return local(
        final_body,
        [shape((probe_count, cell_total), F32)],
        keep_p,
        got_p,
        keep_q,
        got_q,
        scaling,
        name="final",
        out_specs=[whole(None)],
    )[0]


def solution(mesh):
    placed = (
        P(None, ("groups", "tile")),
        P(("groups", "tile")),
        P(("groups", "tile")),
        P("groups"),
        P("groups"),
        P(("groups", "tile"), None, None),
        P(("groups", "tile"), None, None),
        P("groups", None),
        P("groups"),
        P("groups", None),
        P("groups"),
        P("groups"),
    )
    return jax.shard_map(
        shards, mesh=mesh, in_specs=placed, out_specs=P(None, ("groups", "tile")), check_vma=False
    )
```

```python
import math

import jax
import jax.numpy as jnp
from jax import lax
from jax.experimental import pallas as pl
from jax.experimental.pallas import tpu as pltpu
from jax.sharding import PartitionSpec as P

BF16 = jnp.bfloat16
F32 = jnp.float32
I32 = jnp.int32
GROUP = 8
SKEW = 3
SQUARE = (6, 2, 4)
LANES = 128
MIB = 1024 * 1024


def whole(space=pltpu.VMEM):
    return pl.BlockSpec(memory_space=space)


def shape(dims, dtype):
    return jax.ShapeDtypeStruct(tuple(dims), dtype)


def size_of(array):
    return math.prod(array.shape) * jnp.dtype(array.dtype).itemsize


def swap(array, bits):
    count = lax.axis_size("tile")
    return lax.ppermute(array, "tile", [(i, i ^ bits) for i in range(count)])


def local(
    body, outs, *ins, name, scratch=0, scratches=(), specs=None, out_specs=None, flops=0, after=(), aliases=None
):
    nbytes = sum(size_of(a) for a in (*ins, *outs))
    specs = list(specs or [whole()] * len(ins)) + [whole()] * len(after)
    out_specs = list(out_specs or [whole()] * len(outs))
    own = len(ins)
    ins = [pltpu.with_memory_space_constraint(a, s.memory_space) for a, s in zip((*ins, *after), specs)]

    def run(*refs):
        body(*refs[:own], *refs[len(ins) :])

    return pl.pallas_call(
        run,
        out_shape=[a if s.memory_space is None else s.memory_space(a.shape, a.dtype) for a, s in zip(outs, out_specs)],
        in_specs=specs,
        out_specs=[whole() if s.memory_space is None else s for s in out_specs],
        input_output_aliases=aliases or {},
        scratch_shapes=list(scratches),
        compiler_params=pltpu.CompilerParams(vmem_limit_bytes=scratch + 8 * MIB),
        cost_estimate=pl.CostEstimate(flops=flops, bytes_accessed=nbytes, transcendentals=0),
        name=name,
    )(*ins)


def fetch(pairs, sems):
    copies = [pltpu.make_async_copy(a, b, sems.at[i]) for i, (a, b) in enumerate(pairs)]
    for copy in copies:
        copy.start()
    for copy in copies:
        copy.wait()


def load(arrays, after):
    parts = 4

    def body(*refs):
        count = len(refs) // 2
        pairs = []
        for source, out in zip(refs[:count], refs[count:-1]):
            n = source.shape[0] // parts
            pairs += [(source.at[pl.ds(i * n, n)], out.at[pl.ds(i * n, n)]) for i in range(parts)]
        fetch(pairs, refs[-1])

    return local(
        body,
        [shape(a.shape, a.dtype) for a in arrays],
        *arrays,
        name="load",
        specs=[whole(pltpu.HBM)] * len(arrays),
        scratches=[pltpu.SemaphoreType.DMA((parts * len(arrays),))],
        after=after,
    )


def scale_body(
    contrast, level, label, probes, part_p, part_q, scaling, contrast_near, level_near, label_near, probes_near, sems
):
    fetch(
        [(contrast, contrast_near), (level, level_near), (label, label_near), (probes, probes_near)],
        sems,
    )
    value = level_near[...]
    unit = label_near[...]
    factor = jnp.zeros_like(value)
    for k in range(contrast.shape[0]):
        factor = jnp.where(unit == k, contrast_near[k], factor)
    scaling[...] = factor / (1.0 + value * value)
    blocks, _, width = part_p.shape
    rows = width // LANES
    for half, part in enumerate((part_p, part_q)):
        for b in range(blocks):
            for c in range(rows):
                j = (half * blocks + b) * rows + c
                piece = probes_near[:, j * LANES : (j + 1) * LANES] * scaling[j : j + 1, :]
                part[b, :, c * LANES : (c + 1) * LANES] = piece.astype(BF16)


def final_body(keep_p, recv_p, keep_q, recv_q, scaling, out):
    blocks, _, width = keep_p.shape
    rows = width // LANES
    for half, (keep, recv) in enumerate(((keep_p, recv_p), (keep_q, recv_q))):
        for b in range(blocks):
            for c in range(rows):
                j = (half * blocks + b) * rows + c
                lanes = slice(c * LANES, (c + 1) * LANES)
                total = keep[b, :, lanes] + recv[b, :, lanes].astype(F32)
                out[:, j * LANES : (j + 1) * LANES] = total * scaling[j : j + 1, :]


def join_body(*refs):
    out, at = refs[-1], 0
    for ref in refs[:-1]:
        out[at : at + ref.shape[0]] = ref[...]
        at += ref.shape[0]


def join(*pieces, after=()):
    out = shape((sum(a.shape[0] for a in pieces),) + pieces[0].shape[1:], pieces[0].dtype)
    return local(join_body, [out], *pieces, name="join", after=after)[0]


def plus(total, *gots):
    def body(total, *refs):
        done = total[...]
        for ref in refs[:-2]:
            done = done + ref[...].astype(F32)
        refs[-2][...] = done
        refs[-1][...] = done.astype(BF16)

    return local(body, [shape(total.shape, F32), shape(total.shape, BF16)], total, *gots, name="plus")


def weigh(total, got, weight):
    def body(total, got, weight, out):
        blocks, _, width = out.shape
        rows = width // LANES
        for b in range(blocks):
            for c in range(rows):
                lanes = slice(c * LANES, (c + 1) * LANES)
                done = total[b, :, lanes] + got[b, :, lanes].astype(F32)
                j = b * rows + c
                out[b, :, lanes] = (done * weight[j : j + 1, :]).astype(BF16)

    return local(body, [shape(total.shape, BF16)], total, got, weight, name="weigh")[0]


def fold(keep, recv, dtypes=(F32, BF16), base=0):
    n = recv.shape[0] // len(dtypes)

    def body(keep, recv, *outs):
        for i, out in enumerate(outs):
            mine = keep[base + i * n : base + (i + 1) * n]
            out[...] = (mine + recv[i * n : (i + 1) * n].astype(F32)).astype(out.dtype)

    return local(body, [shape((n,) + keep.shape[1:], t) for t in dtypes], keep, recv, name="fold")


def zeros(dims, after):
    def body(out):
        out[...] = jnp.zeros_like(out)

    return local(body, [shape(dims, F32)], name="zeros", after=after)[0]


def tiles_body(piece_count, src_row, dst_row, at, _, *refs):
    pieces = refs[:piece_count]
    first, second, acc, *sends, table = refs[piece_count:]
    count, rank, width = first.shape
    groups = count // GROUP
    join_body(*pieces, table)
    probes = table.shape[1]
    span = GROUP * rank
    row_tile = lax.broadcasted_iota(I32, (GROUP * probes, span), 0) // probes
    col_tile = lax.broadcasted_iota(I32, (GROUP * probes, span), 1) // rank
    component = lax.broadcasted_iota(I32, (GROUP * probes, span), 1) % rank
    own = jnp.where(row_tile == col_tile, component, rank)
    lane_tile = lax.broadcasted_iota(I32, (1, span), 1) // rank

    def inner_of(g):
        taken = jnp.concatenate(
            [table[at[src_row, g * GROUP + i]].astype(F32) for i in range(GROUP)], axis=0
        ).astype(BF16)
        left = first[g * GROUP : (g + 1) * GROUP].reshape(span, width)
        inner = lax.dot_general(taken, left, (((1,), (1,)), ((), ())), preferred_element_type=F32)
        limit = jnp.zeros((1, span), I32)
        for i in range(GROUP):
            limit = jnp.where(lane_tile == i, at[2, g * GROUP + i], limit)
        return jnp.where(own < limit, inner, 0.0).astype(BF16)

    def outer_of(g, kept):
        right = second[g * GROUP : (g + 1) * GROUP].reshape(span, width)
        return jnp.dot(kept, right, preferred_element_type=F32)

    def add(g, outer):
        for i in range(GROUP):
            to = at[dst_row, g * GROUP + i]
            acc[to] = acc[to] + outer[i * probes : (i + 1) * probes]

    kept, outer = {}, {}
    for step in range(groups + 2 * SKEW):
        if step >= 2 * SKEW:
            add(step - 2 * SKEW, outer.pop(step - 2 * SKEW))
        if 0 <= step - SKEW < groups:
            outer[step - SKEW] = outer_of(step - SKEW, kept.pop(step - SKEW))
        if step < groups:
            kept[step] = inner_of(step)
    base = acc.shape[0] // 2
    for send in sends:
        send[...] = acc[base : base + send.shape[0]].astype(send.dtype)
        base += send.shape[0]


def tiles(pieces, src_row, dst_row, table, first, second, acc, parts, send_dtype, name):
    count, rank, width = first.shape
    blocks, probes, _ = acc.shape
    rows = sum(piece.shape[0] for piece in pieces)

    def body(*refs):
        tiles_body(len(pieces), src_row, dst_row, *refs)

    return local(
        body,
        [shape(acc.shape, F32)] + [shape((blocks // 2 // parts, probes, width), send_dtype)] * parts,
        table,
        acc,
        *pieces,
        first,
        second,
        name=name,
        specs=[whole(pltpu.SMEM)] + [whole()] * (len(pieces) + 3),
        aliases={1: 0},
        flops=4 * count * rank * width * probes * GROUP,
        scratch=2 * rows * probes * width,
        scratches=[pltpu.VMEM((rows, probes, width), BF16)],
    )


def place(relative, order):
    at = jnp.zeros_like(relative)
    for k, bit in enumerate(order):
        at = at + jnp.where((relative & bit) != 0, 1 << k, 0)
    return at


def plan(owners, weight, orders, cell_blocks, station_blocks, after):
    peers, count = owners[0].shape
    rows = weight.shape[0] // peers
    rest = peers // 8
    half = cell_blocks // 2

    def body(*refs):
        far, weight_far, table_out, weight_near = refs[:5], refs[5], refs[6], refs[7]
        near, table, sems = refs[8:13], refs[13], refs[14]
        me = lax.axis_index("tile")
        pairs = list(zip(far, near))
        for k in range(rest):
            start = pl.multiple_of((k * 8 + (me & 7)) * rows, rows)
            pairs.append((weight_far.at[pl.ds(start, rows)], weight_near.at[pl.ds(k * rows, rows)]))
        fetch(pairs, sems)
        col_owner, col_local, row_owner, row_local, rank = [ref[pl.ds(me, 1), :] for ref in near]
        span = peers // 2
        away = col_owner ^ me
        is_q = col_local >= half
        for row, (order_p, order_q) in zip((0, 3), orders):
            spot = jnp.where(is_q, place(away, order_q) + (span - 1), place(away, order_p))
            table[row : row + 1, :] = (away & 1) * (span * cell_blocks) + spot * half + col_local
        away = row_owner ^ me
        spot = (away & 1) * 4 + ((away & 4) // 2) + ((away & 2) // 2)
        table[1:2, :] = (spot * rest + row_owner // 8) * station_blocks + row_local
        table[2:3, :] = rank
        fetch([(table, table_out)], sems)

    return local(
        body,
        [shape((8, count), I32), shape((rest * rows, LANES), F32)],
        *owners,
        weight,
        name="plan",
        specs=[whole(pltpu.HBM)] * 6,
        out_specs=[whole(pltpu.SMEM), whole()],
        scratches=[pltpu.VMEM((peers, count), I32)] * 5
        + [pltpu.VMEM((8, count), I32), pltpu.SemaphoreType.DMA((5 + rest,))],
        after=after,
    )


def shards(
    probes,
    level_set,
    unit_label,
    contrast,
    station_weight,
    u_factor,
    v_factor,
    col_owner,
    col_local,
    row_owner,
    row_local,
    tile_rank,
):
    peers = lax.axis_size("tile")
    tile_count, _, station_width = u_factor.shape
    cell_width = v_factor.shape[2]
    probe_count, cell_total = probes.shape
    cell_blocks = cell_total // cell_width
    station_blocks = station_weight.shape[0] // (peers * station_width)
    bits = [1 << k for k in range(1, peers.bit_length() - 1)]
    far = bits[:0:-1]
    gather = (bits[:1] + far, far + bits[:1])
    scatter = (far[:1] + bits[:1] + far[1:], far + bits[:1])

    lanes = (cell_total // LANES, LANES)
    half_dims = (cell_blocks // 2, probe_count, cell_width)
    part_p, part_q, scaling = local(
        scale_body,
        [shape(half_dims, BF16), shape(half_dims, BF16), shape(lanes, F32)],
        contrast,
        level_set.reshape(lanes),
        unit_label.reshape(lanes),
        probes,
        name="scale",
        specs=[whole(pltpu.HBM)] * 4,
        scratches=[
            pltpu.SMEM(contrast.shape, F32),
            pltpu.VMEM(lanes, F32),
            pltpu.VMEM(lanes, I32),
            pltpu.VMEM(probes.shape, F32),
            pltpu.SemaphoreType.DMA((4,)),
        ],
    )
    table, weight = plan(
        [a.reshape(peers, tile_count) for a in (col_owner, col_local, row_owner, row_local, tile_rank)],
        station_weight.reshape(-1, LANES),
        (gather, scatter),
        cell_blocks,
        station_blocks,
        (scaling,),
    )
    steps = list(zip(*gather))
    after = (weight,)
    for step, (bit_p, bit_q) in enumerate(steps):
        got_p = swap(part_p, bit_p)
        got_q = swap(part_q, bit_q)
        if step == 1:
            v_here, u_here = load((v_factor, u_factor), (part_p, part_q))
            after = (u_here,)
        if step < len(steps) - 1:
            part_p = join(part_p, got_p, after=after)
            part_q = join(part_q, got_q)
            after = ()
    pieces = [part_p, got_p, part_q, got_q]
    pieces = pieces + [swap(piece, 1) for piece in pieces]

    acc = zeros((peers * station_blocks, probe_count, station_width), (part_p, part_q))
    total, *sends = tiles(pieces, 0, 1, table, v_here, u_here, acc, 4, F32, "forward")
    quarters = [0] * 4
    for k in SQUARE + (0,):
        kept = F32 if k == 0 else BF16
        quarters[k // 2] = fold(total, swap(sends[k // 2], 1), (kept,), base=k // 2 * sends[0].shape[0])[0]
    total, send = plus(quarters[0], *[swap(quarters[k // 2], k) for k in SQUARE])
    for bit in bits[2:-1]:
        total, send = plus(total, swap(send, bit))
    weighted = weigh(total, swap(send, bits[-1]), weight)
    gots = {k: swap(weighted, k) for k in SQUARE}
    around = join(weighted, gots[2], gots[4], gots[6])
    pieces = [around, swap(around, 1)]

    acc = zeros((peers * cell_blocks, probe_count, cell_width), (total,))
    total, send_p, send_q = tiles(pieces, 1, 3, table, u_here, v_here, acc, 2, BF16, "adjoint")
    keep_p, send_p = fold(total, swap(send_p, 1))
    keep_q, send_q = fold(total, swap(send_q, 1), base=total.shape[0] // 4)
    for step, (bit_p, bit_q) in enumerate(list(zip(*scatter))[::-1]):
        if step > 0:
            keep_p, send_p = fold(keep_p, got_p)
            keep_q, send_q = fold(keep_q, got_q)
        got_p = swap(send_p, bit_p)
        got_q = swap(send_q, bit_q)
    return local(
        final_body,
        [shape((probe_count, cell_total), F32)],
        keep_p,
        got_p,
        keep_q,
        got_q,
        scaling,
        name="final",
        out_specs=[whole(None)],
    )[0]


def solution(mesh):
    placed = (
        P(None, ("groups", "tile")),
        P(("groups", "tile")),
        P(("groups", "tile")),
        P("groups"),
        P("groups"),
        P(("groups", "tile"), None, None),
        P(("groups", "tile"), None, None),
        P("groups", None),
        P("groups"),
        P("groups", None),
        P("groups"),
        P("groups"),
    )
    return jax.shard_map(
        shards, mesh=mesh, in_specs=placed, out_specs=P(None, ("groups", "tile")), check_vma=False
    )
```

```python
import math

import jax
import jax.numpy as jnp
from jax import lax
from jax.experimental import pallas as pl
from jax.experimental.pallas import tpu as pltpu
from jax.sharding import PartitionSpec as P

BF16 = jnp.bfloat16
F32 = jnp.float32
I32 = jnp.int32
GROUP = 8
SKEW = 3
SQUARE = (6, 2, 4)
LANES = 128
MIB = 1024 * 1024


def whole(space=pltpu.VMEM):
    return pl.BlockSpec(memory_space=space)


def shape(dims, dtype):
    return jax.ShapeDtypeStruct(tuple(dims), dtype)


def size_of(array):
    return math.prod(array.shape) * jnp.dtype(array.dtype).itemsize


def swap(array, bits):
    count = lax.axis_size("tile")
    return lax.ppermute(array, "tile", [(i, i ^ bits) for i in range(count)])


def local(
    body, outs, *ins, name, scratch=0, scratches=(), specs=None, out_specs=None, flops=0, after=(), aliases=None
):
    nbytes = sum(size_of(a) for a in (*ins, *outs))
    specs = list(specs or [whole()] * len(ins)) + [whole()] * len(after)
    out_specs = list(out_specs or [whole()] * len(outs))
    own = len(ins)
    ins = [pltpu.with_memory_space_constraint(a, s.memory_space) for a, s in zip((*ins, *after), specs)]

    def run(*refs):
        body(*refs[:own], *refs[len(ins) :])

    return pl.pallas_call(
        run,
        out_shape=[a if s.memory_space is None else s.memory_space(a.shape, a.dtype) for a, s in zip(outs, out_specs)],
        in_specs=specs,
        out_specs=[whole() if s.memory_space is None else s for s in out_specs],
        input_output_aliases=aliases or {},
        scratch_shapes=list(scratches),
        compiler_params=pltpu.CompilerParams(vmem_limit_bytes=scratch + 8 * MIB),
        cost_estimate=pl.CostEstimate(flops=flops, bytes_accessed=nbytes, transcendentals=0),
        name=name,
    )(*ins)


def fetch(pairs, sems):
    copies = [pltpu.make_async_copy(a, b, sems.at[i]) for i, (a, b) in enumerate(pairs)]
    for copy in copies:
        copy.start()
    for copy in copies:
        copy.wait()


def load_body(source, out, sems):
    n = source.shape[0] // sems.shape[0]
    rows = [pl.ds(i * n, n) for i in range(sems.shape[0])]
    fetch([(source.at[r], out.at[r]) for r in rows], sems)


def load(array, after, name):
    return local(
        load_body,
        [shape(array.shape, array.dtype)],
        array,
        name=name,
        specs=[whole(pltpu.HBM)],
        scratches=[pltpu.SemaphoreType.DMA((8,))],
        after=after,
    )[0]


def scale_body(
    contrast, level, label, probes, part_p, part_q, scaling, contrast_near, level_near, label_near, probes_near, sems
):
    fetch(
        [(contrast, contrast_near), (level, level_near), (label, label_near), (probes, probes_near)],
        sems,
    )
    value = level_near[...]
    unit = label_near[...]
    factor = jnp.zeros_like(value)
    for k in range(contrast.shape[0]):
        factor = jnp.where(unit == k, contrast_near[k], factor)
    scaling[...] = factor / (1.0 + value * value)
    blocks, _, width = part_p.shape
    rows = width // LANES
    for half, part in enumerate((part_p, part_q)):
        for b in range(blocks):
            for c in range(rows):
                j = (half * blocks + b) * rows + c
                piece = probes_near[:, j * LANES : (j + 1) * LANES] * scaling[j : j + 1, :]
                part[b, :, c * LANES : (c + 1) * LANES] = piece.astype(BF16)


def final_body(keep_p, recv_p, keep_q, recv_q, scaling, out):
    blocks, _, width = keep_p.shape
    rows = width // LANES
    for half, (keep, recv) in enumerate(((keep_p, recv_p), (keep_q, recv_q))):
        for b in range(blocks):
            for c in range(rows):
                j = (half * blocks + b) * rows + c
                lanes = slice(c * LANES, (c + 1) * LANES)
                total = keep[b, :, lanes] + recv[b, :, lanes].astype(F32)
                out[:, j * LANES : (j + 1) * LANES] = total * scaling[j : j + 1, :]


def join_body(*refs):
    out, at = refs[-1], 0
    for ref in refs[:-1]:
        out[at : at + ref.shape[0]] = ref[...]
        at += ref.shape[0]


def join(*pieces, after=()):
    out = shape((sum(a.shape[0] for a in pieces),) + pieces[0].shape[1:], pieces[0].dtype)
    return local(join_body, [out], *pieces, name="join", after=after)[0]


def plus(total, *gots):
    def body(total, *refs):
        done = total[...]
        for ref in refs[:-2]:
            done = done + ref[...].astype(F32)
        refs[-2][...] = done
        refs[-1][...] = done.astype(BF16)

    return local(body, [shape(total.shape, F32), shape(total.shape, BF16)], total, *gots, name="plus")


def weigh(total, got, weight):
    def body(total, got, weight, out):
        blocks, _, width = out.shape
        rows = width // LANES
        for b in range(blocks):
            for c in range(rows):
                lanes = slice(c * LANES, (c + 1) * LANES)
                done = total[b, :, lanes] + got[b, :, lanes].astype(F32)
                j = b * rows + c
                out[b, :, lanes] = (done * weight[j : j + 1, :]).astype(BF16)

    return local(body, [shape(total.shape, BF16)], total, got, weight, name="weigh")[0]


def fold(keep, recv, dtypes=(F32, BF16), base=0):
    n = recv.shape[0] // len(dtypes)

    def body(keep, recv, *outs):
        for i, out in enumerate(outs):
            mine = keep[base + i * n : base + (i + 1) * n]
            out[...] = (mine + recv[i * n : (i + 1) * n].astype(F32)).astype(out.dtype)

    return local(body, [shape((n,) + keep.shape[1:], t) for t in dtypes], keep, recv, name="fold")


def zeros(dims, after):
    def body(out):
        out[...] = jnp.zeros_like(out)

    return local(body, [shape(dims, F32)], name="zeros", after=after)[0]


def tiles_body(piece_count, src_row, dst_row, at, _, *refs):
    pieces = refs[:piece_count]
    first, second, acc, *sends, table = refs[piece_count:]
    count, rank, width = first.shape
    groups = count // GROUP
    join_body(*pieces, table)
    probes = table.shape[1]
    span = GROUP * rank
    row_tile = lax.broadcasted_iota(I32, (GROUP * probes, span), 0) // probes
    col_tile = lax.broadcasted_iota(I32, (GROUP * probes, span), 1) // rank
    component = lax.broadcasted_iota(I32, (GROUP * probes, span), 1) % rank
    own = jnp.where(row_tile == col_tile, component, rank)
    lane_tile = lax.broadcasted_iota(I32, (1, span), 1) // rank

    def inner_of(g):
        taken = jnp.concatenate(
            [table[at[src_row, g * GROUP + i]].astype(F32) for i in range(GROUP)], axis=0
        ).astype(BF16)
        left = first[g * GROUP : (g + 1) * GROUP].reshape(span, width)
        inner = lax.dot_general(taken, left, (((1,), (1,)), ((), ())), preferred_element_type=F32)
        limit = jnp.zeros((1, span), I32)
        for i in range(GROUP):
            limit = jnp.where(lane_tile == i, at[2, g * GROUP + i], limit)
        return jnp.where(own < limit, inner, 0.0).astype(BF16)

    def outer_of(g, kept):
        right = second[g * GROUP : (g + 1) * GROUP].reshape(span, width)
        return jnp.dot(kept, right, preferred_element_type=F32)

    def add(g, outer):
        for i in range(GROUP):
            to = at[dst_row, g * GROUP + i]
            acc[to] = acc[to] + outer[i * probes : (i + 1) * probes]

    kept, outer = {}, {}
    for step in range(groups + 2 * SKEW):
        if step >= 2 * SKEW:
            add(step - 2 * SKEW, outer.pop(step - 2 * SKEW))
        if 0 <= step - SKEW < groups:
            outer[step - SKEW] = outer_of(step - SKEW, kept.pop(step - SKEW))
        if step < groups:
            kept[step] = inner_of(step)
    base = acc.shape[0] // 2
    for send in sends:
        send[...] = acc[base : base + send.shape[0]].astype(send.dtype)
        base += send.shape[0]


def tiles(pieces, src_row, dst_row, table, first, second, acc, parts, send_dtype, name):
    count, rank, width = first.shape
    blocks, probes, _ = acc.shape
    rows = sum(piece.shape[0] for piece in pieces)

    def body(*refs):
        tiles_body(len(pieces), src_row, dst_row, *refs)

    return local(
        body,
        [shape(acc.shape, F32)] + [shape((blocks // 2 // parts, probes, width), send_dtype)] * parts,
        table,
        acc,
        *pieces,
        first,
        second,
        name=name,
        specs=[whole(pltpu.SMEM)] + [whole()] * (len(pieces) + 3),
        aliases={1: 0},
        flops=4 * count * rank * width * probes * GROUP,
        scratch=2 * rows * probes * width,
        scratches=[pltpu.VMEM((rows, probes, width), BF16)],
    )


def place(relative, order):
    at = jnp.zeros_like(relative)
    for k, bit in enumerate(order):
        at = at + jnp.where((relative & bit) != 0, 1 << k, 0)
    return at


def plan(owners, weight, orders, cell_blocks, station_blocks, after):
    peers, count = owners[0].shape
    rows = weight.shape[0] // peers
    rest = peers // 8
    half = cell_blocks // 2

    def body(*refs):
        far, weight_far, table_out, weight_near = refs[:5], refs[5], refs[6], refs[7]
        near, table, sems = refs[8:13], refs[13], refs[14]
        me = lax.axis_index("tile")
        pairs = list(zip(far, near))
        for k in range(rest):
            start = pl.multiple_of((k * 8 + (me & 7)) * rows, rows)
            pairs.append((weight_far.at[pl.ds(start, rows)], weight_near.at[pl.ds(k * rows, rows)]))
        fetch(pairs, sems)
        col_owner, col_local, row_owner, row_local, rank = [ref[pl.ds(me, 1), :] for ref in near]
        span = peers // 2
        away = col_owner ^ me
        is_q = col_local >= half
        for row, (order_p, order_q) in zip((0, 3), orders):
            spot = jnp.where(is_q, place(away, order_q) + (span - 1), place(away, order_p))
            table[row : row + 1, :] = (away & 1) * (span * cell_blocks) + spot * half + col_local
        away = row_owner ^ me
        spot = (away & 1) * 4 + ((away & 4) // 2) + ((away & 2) // 2)
        table[1:2, :] = (spot * rest + row_owner // 8) * station_blocks + row_local
        table[2:3, :] = rank
        fetch([(table, table_out)], sems)

    return local(
        body,
        [shape((8, count), I32), shape((rest * rows, LANES), F32)],
        *owners,
        weight,
        name="plan",
        specs=[whole(pltpu.HBM)] * 6,
        out_specs=[whole(pltpu.SMEM), whole()],
        scratches=[pltpu.VMEM((peers, count), I32)] * 5
        + [pltpu.VMEM((8, count), I32), pltpu.SemaphoreType.DMA((5 + rest,))],
        after=after,
    )


def shards(
    probes,
    level_set,
    unit_label,
    contrast,
    station_weight,
    u_factor,
    v_factor,
    col_owner,
    col_local,
    row_owner,
    row_local,
    tile_rank,
):
    peers = lax.axis_size("tile")
    tile_count, _, station_width = u_factor.shape
    cell_width = v_factor.shape[2]
    probe_count, cell_total = probes.shape
    cell_blocks = cell_total // cell_width
    station_blocks = station_weight.shape[0] // (peers * station_width)
    bits = [1 << k for k in range(1, peers.bit_length() - 1)]
    far = bits[:0:-1]
    gather = (bits[:1] + far, far + bits[:1])
    scatter = (far[:1] + bits[:1] + far[1:], far + bits[:1])

    lanes = (cell_total // LANES, LANES)
    half_dims = (cell_blocks // 2, probe_count, cell_width)
    part_p, part_q, scaling = local(
        scale_body,
        [shape(half_dims, BF16), shape(half_dims, BF16), shape(lanes, F32)],
        contrast,
        level_set.reshape(lanes),
        unit_label.reshape(lanes),
        probes,
        name="scale",
        specs=[whole(pltpu.HBM)] * 4,
        scratches=[
            pltpu.SMEM(contrast.shape, F32),
            pltpu.VMEM(lanes, F32),
            pltpu.VMEM(lanes, I32),
            pltpu.VMEM(probes.shape, F32),
            pltpu.SemaphoreType.DMA((4,)),
        ],
    )
    table, weight = plan(
        [a.reshape(peers, tile_count) for a in (col_owner, col_local, row_owner, row_local, tile_rank)],
        station_weight.reshape(-1, LANES),
        (gather, scatter),
        cell_blocks,
        station_blocks,
        (scaling,),
    )
    steps = list(zip(*gather))
    after = (weight,)
    for step, (bit_p, bit_q) in enumerate(steps):
        got_p = swap(part_p, bit_p)
        got_q = swap(part_q, bit_q)
        if step == 1:
            v_here = load(v_factor, (part_p, part_q), "load_v")
            u_here = load(u_factor, (part_p, part_q, v_here), "load_u")
            after = (u_here,)
        if step < len(steps) - 1:
            part_p = join(part_p, got_p, after=after)
            part_q = join(part_q, got_q)
            after = ()
    pieces = [part_p, got_p, part_q, got_q]
    pieces = pieces + [swap(piece, 1) for piece in pieces]

    acc = zeros((peers * station_blocks, probe_count, station_width), (part_p, part_q))
    total, *sends = tiles(pieces, 0, 1, table, v_here, u_here, acc, 4, BF16, "forward")
    quarters = [0] * 4
    for k in SQUARE + (0,):
        kept = F32 if k == 0 else BF16
        quarters[k // 2] = fold(total, swap(sends[k // 2], 1), (kept,), base=k // 2 * sends[0].shape[0])[0]
    total, send = plus(quarters[0], *[swap(quarters[k // 2], k) for k in SQUARE])
    for bit in bits[2:-1]:
        total, send = plus(total, swap(send, bit))
    weighted = weigh(total, swap(send, bits[-1]), weight)
    gots = {k: swap(weighted, k) for k in SQUARE}
    around = join(weighted, gots[2], gots[4], gots[6])
    pieces = [around, swap(around, 1)]

    acc = zeros((peers * cell_blocks, probe_count, cell_width), (total,))
    total, send_p, send_q = tiles(pieces, 1, 3, table, u_here, v_here, acc, 2, BF16, "adjoint")
    keep_p, send_p = fold(total, swap(send_p, 1))
    keep_q, send_q = fold(total, swap(send_q, 1), base=total.shape[0] // 4)
    for step, (bit_p, bit_q) in enumerate(list(zip(*scatter))[::-1]):
        if step > 0:
            keep_p, send_p = fold(keep_p, got_p)
            keep_q, send_q = fold(keep_q, got_q)
        got_p = swap(send_p, bit_p)
        got_q = swap(send_q, bit_q)
    return local(
        final_body,
        [shape((probe_count, cell_total), F32)],
        keep_p,
        got_p,
        keep_q,
        got_q,
        scaling,
        name="final",
        out_specs=[whole(None)],
    )[0]


def solution(mesh):
    placed = (
        P(None, ("groups", "tile")),
        P(("groups", "tile")),
        P(("groups", "tile")),
        P("groups"),
        P("groups"),
        P(("groups", "tile"), None, None),
        P(("groups", "tile"), None, None),
        P("groups", None),
        P("groups"),
        P("groups", None),
        P("groups"),
        P("groups"),
    )
    return jax.shard_map(
        shards, mesh=mesh, in_specs=placed, out_specs=P(None, ("groups", "tile")), check_vma=False
    )
```

```python
import math

import jax
import jax.numpy as jnp
from jax import lax
from jax.experimental import pallas as pl
from jax.experimental.pallas import tpu as pltpu
from jax.sharding import PartitionSpec as P

BF16 = jnp.bfloat16
F32 = jnp.float32
I32 = jnp.int32
GROUP = 8
SKEW = 3
SQUARE = (6, 4, 2)
LANES = 128
MIB = 1024 * 1024


def whole(space=pltpu.VMEM):
    return pl.BlockSpec(memory_space=space)


def shape(dims, dtype):
    return jax.ShapeDtypeStruct(tuple(dims), dtype)


def size_of(array):
    return math.prod(array.shape) * jnp.dtype(array.dtype).itemsize


def swap(array, bits):
    count = lax.axis_size("tile")
    return lax.ppermute(array, "tile", [(i, i ^ bits) for i in range(count)])


def local(
    body, outs, *ins, name, scratch=0, scratches=(), specs=None, out_specs=None, flops=0, after=(), aliases=None
):
    nbytes = sum(size_of(a) for a in (*ins, *outs))
    specs = list(specs or [whole()] * len(ins)) + [whole()] * len(after)
    out_specs = list(out_specs or [whole()] * len(outs))
    own = len(ins)
    ins = [pltpu.with_memory_space_constraint(a, s.memory_space) for a, s in zip((*ins, *after), specs)]

    def run(*refs):
        body(*refs[:own], *refs[len(ins) :])

    return pl.pallas_call(
        run,
        out_shape=[a if s.memory_space is None else s.memory_space(a.shape, a.dtype) for a, s in zip(outs, out_specs)],
        in_specs=specs,
        out_specs=[whole() if s.memory_space is None else s for s in out_specs],
        input_output_aliases=aliases or {},
        scratch_shapes=list(scratches),
        compiler_params=pltpu.CompilerParams(vmem_limit_bytes=scratch + 8 * MIB),
        cost_estimate=pl.CostEstimate(flops=flops, bytes_accessed=nbytes, transcendentals=0),
        name=name,
    )(*ins)


def fetch(pairs, sems):
    copies = [pltpu.make_async_copy(a, b, sems.at[i]) for i, (a, b) in enumerate(pairs)]
    for copy in copies:
        copy.start()
    for copy in copies:
        copy.wait()


def load_body(source, out, sems):
    n = source.shape[0] // sems.shape[0]
    rows = [pl.ds(i * n, n) for i in range(sems.shape[0])]
    fetch([(source.at[r], out.at[r]) for r in rows], sems)


def load(array, after, name):
    return local(
        load_body,
        [shape(array.shape, array.dtype)],
        array,
        name=name,
        specs=[whole(pltpu.HBM)],
        scratches=[pltpu.SemaphoreType.DMA((8,))],
        after=after,
    )[0]


def scale_body(
    contrast, level, label, probes, part_p, part_q, scaling, contrast_near, level_near, label_near, probes_near, sems
):
    fetch(
        [(contrast, contrast_near), (level, level_near), (label, label_near), (probes, probes_near)],
        sems,
    )
    value = level_near[...]
    unit = label_near[...]
    factor = jnp.zeros_like(value)
    for k in range(contrast.shape[0]):
        factor = jnp.where(unit == k, contrast_near[k], factor)
    scaling[...] = factor / (1.0 + value * value)
    blocks, _, width = part_p.shape
    rows = width // LANES
    for half, part in enumerate((part_p, part_q)):
        for b in range(blocks):
            for c in range(rows):
                j = (half * blocks + b) * rows + c
                piece = probes_near[:, j * LANES : (j + 1) * LANES] * scaling[j : j + 1, :]
                part[b, :, c * LANES : (c + 1) * LANES] = piece.astype(BF16)


def final_body(keep_p, recv_p, keep_q, recv_q, scaling, out):
    blocks, _, width = keep_p.shape
    rows = width // LANES
    for half, (keep, recv) in enumerate(((keep_p, recv_p), (keep_q, recv_q))):
        for b in range(blocks):
            for c in range(rows):
                j = (half * blocks + b) * rows + c
                lanes = slice(c * LANES, (c + 1) * LANES)
                total = keep[b, :, lanes] + recv[b, :, lanes].astype(F32)
                out[:, j * LANES : (j + 1) * LANES] = total * scaling[j : j + 1, :]


def join_body(*refs):
    out, at = refs[-1], 0
    for ref in refs[:-1]:
        out[at : at + ref.shape[0]] = ref[...]
        at += ref.shape[0]


def join(*pieces, after=()):
    out = shape((sum(a.shape[0] for a in pieces),) + pieces[0].shape[1:], pieces[0].dtype)
    return local(join_body, [out], *pieces, name="join", after=after)[0]


def plus(total, *gots):
    def body(total, *refs):
        done = total[...]
        for ref in refs[:-2]:
            done = done + ref[...].astype(F32)
        refs[-2][...] = done
        refs[-1][...] = done.astype(BF16)

    return local(body, [shape(total.shape, F32), shape(total.shape, BF16)], total, *gots, name="plus")


def weigh(total, got, weight):
    def body(total, got, weight, out):
        blocks, _, width = out.shape
        rows = width // LANES
        for b in range(blocks):
            for c in range(rows):
                lanes = slice(c * LANES, (c + 1) * LANES)
                done = total[b, :, lanes] + got[b, :, lanes].astype(F32)
                j = b * rows + c
                out[b, :, lanes] = (done * weight[j : j + 1, :]).astype(BF16)

    return local(body, [shape(total.shape, BF16)], total, got, weight, name="weigh")[0]


def fold(keep, recv, dtypes=(F32, BF16), base=0):
    n = recv.shape[0] // len(dtypes)

    def body(keep, recv, *outs):
        for i, out in enumerate(outs):
            mine = keep[base + i * n : base + (i + 1) * n]
            out[...] = (mine + recv[i * n : (i + 1) * n].astype(F32)).astype(out.dtype)

    return local(body, [shape((n,) + keep.shape[1:], t) for t in dtypes], keep, recv, name="fold")


def zeros(dims, after):
    def body(out):
        out[...] = jnp.zeros_like(out)

    return local(body, [shape(dims, F32)], name="zeros", after=after)[0]


def tiles_body(piece_count, src_row, dst_row, at, _, *refs):
    pieces = refs[:piece_count]
    first, second, acc, *sends, table = refs[piece_count:]
    count, rank, width = first.shape
    groups = count // GROUP
    join_body(*pieces, table)
    probes = table.shape[1]
    span = GROUP * rank
    row_tile = lax.broadcasted_iota(I32, (GROUP * probes, span), 0) // probes
    col_tile = lax.broadcasted_iota(I32, (GROUP * probes, span), 1) // rank
    component = lax.broadcasted_iota(I32, (GROUP * probes, span), 1) % rank
    own = jnp.where(row_tile == col_tile, component, rank)
    lane_tile = lax.broadcasted_iota(I32, (1, span), 1) // rank

    def inner_of(g):
        taken = jnp.concatenate(
            [table[at[src_row, g * GROUP + i]].astype(F32) for i in range(GROUP)], axis=0
        ).astype(BF16)
        left = first[g * GROUP : (g + 1) * GROUP].reshape(span, width)
        inner = lax.dot_general(taken, left, (((1,), (1,)), ((), ())), preferred_element_type=F32)
        limit = jnp.zeros((1, span), I32)
        for i in range(GROUP):
            limit = jnp.where(lane_tile == i, at[2, g * GROUP + i], limit)
        return jnp.where(own < limit, inner, 0.0).astype(BF16)

    def outer_of(g, kept):
        right = second[g * GROUP : (g + 1) * GROUP].reshape(span, width)
        return jnp.dot(kept, right, preferred_element_type=F32)

    def add(g, outer):
        for i in range(GROUP):
            to = at[dst_row, g * GROUP + i]
            acc[to] = acc[to] + outer[i * probes : (i + 1) * probes]

    kept, outer = {}, {}
    for step in range(groups + 2 * SKEW):
        if step >= 2 * SKEW:
            add(step - 2 * SKEW, outer.pop(step - 2 * SKEW))
        if 0 <= step - SKEW < groups:
            outer[step - SKEW] = outer_of(step - SKEW, kept.pop(step - SKEW))
        if step < groups:
            kept[step] = inner_of(step)
    base = acc.shape[0] // 2
    for send in sends:
        send[...] = acc[base : base + send.shape[0]].astype(send.dtype)
        base += send.shape[0]


def tiles(pieces, src_row, dst_row, table, first, second, acc, parts, send_dtype, name):
    count, rank, width = first.shape
    blocks, probes, _ = acc.shape
    rows = sum(piece.shape[0] for piece in pieces)

    def body(*refs):
        tiles_body(len(pieces), src_row, dst_row, *refs)

    return local(
        body,
        [shape(acc.shape, F32)] + [shape((blocks // 2 // parts, probes, width), send_dtype)] * parts,
        table,
        acc,
        *pieces,
        first,
        second,
        name=name,
        specs=[whole(pltpu.SMEM)] + [whole()] * (len(pieces) + 3),
        aliases={1: 0},
        flops=4 * count * rank * width * probes * GROUP,
        scratch=2 * rows * probes * width,
        scratches=[pltpu.VMEM((rows, probes, width), BF16)],
    )


def place(relative, order):
    at = jnp.zeros_like(relative)
    for k, bit in enumerate(order):
        at = at + jnp.where((relative & bit) != 0, 1 << k, 0)
    return at


def plan(owners, weight, orders, cell_blocks, station_blocks, after):
    peers, count = owners[0].shape
    rows = weight.shape[0] // peers
    rest = peers // 8
    half = cell_blocks // 2

    def body(*refs):
        far, weight_far, table_out, weight_near = refs[:5], refs[5], refs[6], refs[7]
        near, table, sems = refs[8:13], refs[13], refs[14]
        me = lax.axis_index("tile")
        pairs = list(zip(far, near))
        for k in range(rest):
            start = pl.multiple_of((k * 8 + (me & 7)) * rows, rows)
            pairs.append((weight_far.at[pl.ds(start, rows)], weight_near.at[pl.ds(k * rows, rows)]))
        fetch(pairs, sems)
        col_owner, col_local, row_owner, row_local, rank = [ref[pl.ds(me, 1), :] for ref in near]
        span = peers // 2
        away = col_owner ^ me
        is_q = col_local >= half
        for row, (order_p, order_q) in zip((0, 3), orders):
            spot = jnp.where(is_q, place(away, order_q) + (span - 1), place(away, order_p))
            table[row : row + 1, :] = (away & 1) * (span * cell_blocks) + spot * half + col_local
        away = row_owner ^ me
        spot = (away & 1) * 4 + ((away & 4) // 2) + ((away & 2) // 2)
        table[1:2, :] = (spot * rest + row_owner // 8) * station_blocks + row_local
        table[2:3, :] = rank
        fetch([(table, table_out)], sems)

    return local(
        body,
        [shape((8, count), I32), shape((rest * rows, LANES), F32)],
        *owners,
        weight,
        name="plan",
        specs=[whole(pltpu.HBM)] * 6,
        out_specs=[whole(pltpu.SMEM), whole()],
        scratches=[pltpu.VMEM((peers, count), I32)] * 5
        + [pltpu.VMEM((8, count), I32), pltpu.SemaphoreType.DMA((5 + rest,))],
        after=after,
    )


def shards(
    probes,
    level_set,
    unit_label,
    contrast,
    station_weight,
    u_factor,
    v_factor,
    col_owner,
    col_local,
    row_owner,
    row_local,
    tile_rank,
):
    peers = lax.axis_size("tile")
    tile_count, _, station_width = u_factor.shape
    cell_width = v_factor.shape[2]
    probe_count, cell_total = probes.shape
    cell_blocks = cell_total // cell_width
    station_blocks = station_weight.shape[0] // (peers * station_width)
    bits = [1 << k for k in range(1, peers.bit_length() - 1)]
    far = bits[:0:-1]
    gather = (bits[:1] + far, far + bits[:1])
    scatter = (far[:1] + bits[:1] + far[1:], far + bits[:1])

    lanes = (cell_total // LANES, LANES)
    half_dims = (cell_blocks // 2, probe_count, cell_width)
    part_p, part_q, scaling = local(
        scale_body,
        [shape(half_dims, BF16), shape(half_dims, BF16), shape(lanes, F32)],
        contrast,
        level_set.reshape(lanes),
        unit_label.reshape(lanes),
        probes,
        name="scale",
        specs=[whole(pltpu.HBM)] * 4,
        scratches=[
            pltpu.SMEM(contrast.shape, F32),
            pltpu.VMEM(lanes, F32),
            pltpu.VMEM(lanes, I32),
            pltpu.VMEM(probes.shape, F32),
            pltpu.SemaphoreType.DMA((4,)),
        ],
    )
    table, weight = plan(
        [a.reshape(peers, tile_count) for a in (col_owner, col_local, row_owner, row_local, tile_rank)],
        station_weight.reshape(-1, LANES),
        (gather, scatter),
        cell_blocks,
        station_blocks,
        (scaling,),
    )
    steps = list(zip(*gather))
    after = (weight,)
    for step, (bit_p, bit_q) in enumerate(steps):
        got_p = swap(part_p, bit_p)
        got_q = swap(part_q, bit_q)
        if step == 1:
            v_here = load(v_factor, (part_p, part_q), "load_v")
            u_here = load(u_factor, (part_p, part_q, v_here), "load_u")
            after = (u_here,)
        if step < len(steps) - 1:
            part_p = join(part_p, got_p, after=after)
            part_q = join(part_q, got_q)
            after = ()
    pieces = [part_p, got_p, part_q, got_q]
    pieces = pieces + [swap(piece, 1) for piece in pieces]

    acc = zeros((peers * station_blocks, probe_count, station_width), (part_p, part_q))
    total, *sends = tiles(pieces, 0, 1, table, v_here, u_here, acc, 4, F32, "forward")
    quarters = [0] * 4
    for k in SQUARE + (0,):
        kept = F32 if k == 0 else BF16
        quarters[k // 2] = fold(total, swap(sends[k // 2], 1), (kept,), base=k // 2 * sends[0].shape[0])[0]
    total, send = plus(quarters[0], *[swap(quarters[k // 2], k) for k in SQUARE])
    for bit in bits[2:-1]:
        total, send = plus(total, swap(send, bit))
    weighted = weigh(total, swap(send, bits[-1]), weight)
    gots = {k: swap(weighted, k) for k in SQUARE}
    around = join(weighted, gots[2], gots[4], gots[6])
    pieces = [around, swap(around, 1)]

    acc = zeros((peers * cell_blocks, probe_count, cell_width), (total,))
    total, send_p, send_q = tiles(pieces, 1, 3, table, u_here, v_here, acc, 2, BF16, "adjoint")
    keep_p, send_p = fold(total, swap(send_p, 1))
    keep_q, send_q = fold(total, swap(send_q, 1), base=total.shape[0] // 4)
    for step, (bit_p, bit_q) in enumerate(list(zip(*scatter))[::-1]):
        if step > 0:
            keep_p, send_p = fold(keep_p, got_p)
            keep_q, send_q = fold(keep_q, got_q)
        got_p = swap(send_p, bit_p)
        got_q = swap(send_q, bit_q)
    return local(
        final_body,
        [shape((probe_count, cell_total), F32)],
        keep_p,
        got_p,
        keep_q,
        got_q,
        scaling,
        name="final",
        out_specs=[whole(None)],
    )[0]


def solution(mesh):
    placed = (
        P(None, ("groups", "tile")),
        P(("groups", "tile")),
        P(("groups", "tile")),
        P("groups"),
        P("groups"),
        P(("groups", "tile"), None, None),
        P(("groups", "tile"), None, None),
        P("groups", None),
        P("groups"),
        P("groups", None),
        P("groups"),
        P("groups"),
    )
    return jax.shard_map(
        shards, mesh=mesh, in_specs=placed, out_specs=P(None, ("groups", "tile")), check_vma=False
    )
```
